32 devices in a mesh: dp: 2 (over x), row: 4 (over y, core), col: 4 (over z).
Axes of the slice: x: 2, y: 2, z: 4, core: 2. Of those that a mesh axis runs over, the one named last changes fastest.
Arguments:
- inputs: bfloat16 [2, 768, 4096], P(None, 'row', ('dp', 'col')), may hold values from -6 to 6
- cotangent: bfloat16 [2, 768, 4096], P(None, 'row', ('dp', 'col')), may hold values from -6 to 6
- lengths: int32 [2, 2], P('dp'), may hold values from 512 to 1536, as said below
- source: int32 [2, 4096], P(None, ('dp', 'col')), may hold values from 0 to 8191, as said below
- query_weight: bfloat16 [768, 768], P('row', 'col'), may hold values from -0.21875 to 0.21875
- key_weight: bfloat16 [768, 768], P('row', 'col'), may hold values from -0.21875 to 0.21875
- value_weight: bfloat16 [768, 768], P('row', 'col'), may hold values from -0.21875 to 0.21875
- output_weight: bfloat16 [768, 768], P('col', 'row'), may hold values from -6 to 6
- inner_weight: bfloat16 [768, 3072], P('row', 'col'), may hold values from -0.21875 to 0.21875
- outer_weight: bfloat16 [768, 3072], P('row', 'col'), may hold values from -0.109375 to 0.109375
- first_gain: float32 [768], P('row'), may hold values from 0.5 to 1.5
- first_shift: float32 [768], P('row'), may hold values from -3 to 3
- second_gain: float32 [768], P('row'), may hold values from 0.5 to 1.5
- second_shift: float32 [768], P('row'), may hold values from -3 to 3
Outputs:
- layer_out: bfloat16 [2, 768, 4096], P(None, 'row', ('dp', 'col'))
- input_grad: bfloat16 [2, 768, 4096], P(None, 'row', ('dp', 'col'))
- query_grad: float32 [768, 768], P('row', 'col')
- key_grad: float32 [768, 768], P('row', 'col')
- value_grad: float32 [768, 768], P('row', 'col')
- output_grad: float32 [768, 768], P('col', 'row')
- inner_grad: float32 [768, 3072], P('row', 'col')
- outer_grad: float32 [768, 3072], P('row', 'col')
- first_gain_grad: float32 [768], P('row')
- first_shift_grad: float32 [768], P('row')
- second_gain_grad: float32 [768], P('row')
- second_shift_grad: float32 [768], P('row')
The draws below stay inside these ranges and needn't reach their ends.
Inputs may be any that keep to these rules, and one draw needn't show every extreme that they name: lengths is that of each pack's first sequence; the second takes the other 2048 - lengths tokens. source is a permutation of the 8192 flat loader positions, flat index m0 * 2 * 2048 + p0. A token keeps (p // 512) % 4; and for any d, s and col index, exactly 512 of the dealt positions with p // 2048 == d and that col index come from p0 // 2048 == s.
All inputs are finite; a program needn't handle non-finite values.
Results may differ from the reference program's by a relative error of at most 0.018.
Values may be sent and summed in bfloat16 or wider, within the bound.
No kernel may reach another device: no remote copies, remote signals or barrier semaphores. Data moves between devices by JAX's collectives and lax.ppermute only.
A program may use at most 192 MiB of HBM per device.

```python
import jax
import jax.numpy as jnp
from jax import lax

D = 768
H = 12
DH = 64
FF = 3072
BIN = 512
MB = 2
MINLEN = 512
PACK = 2048
N_DP = 2
N_COL = 4


def draw_lengths(key, part):
    first_len = jax.random.randint(key, (N_DP, MB), MINLEN, PACK - MINLEN + 1)
    first_len = first_len.at[0, 0].set(MINLEN)
    first_len = first_len.at[0, MB - 1].set(PACK - MINLEN)
    return first_len.astype(jnp.int32)


def draw_source(key, part):
    local_count = MB * BIN
    sent_rows = local_count // N_DP
    first_key, second_key = jax.random.split(jax.random.fold_in(key, 7))
    outgoing = jax.vmap(lambda member: jax.random.permutation(member, local_count))(jax.random.split(first_key, N_DP * N_COL))
    incoming = jax.vmap(lambda member: jax.random.permutation(member, local_count))(jax.random.split(second_key, N_DP * N_COL))
    outgoing = outgoing.reshape(N_DP, N_COL, N_DP, sent_rows)
    local_index = jnp.transpose(outgoing, (2, 1, 0, 3))
    sender = jnp.arange(N_DP, dtype=jnp.int32)[None, None, :, None]
    column = jnp.arange(N_COL, dtype=jnp.int32)[None, :, None, None]
    anchor = local_index // BIN * (N_DP * PACK) + (sender * N_COL + column) * BIN + local_index % BIN
    anchor = anchor.reshape(N_DP, N_COL, local_count)
    inverse = jnp.argsort(incoming, axis=-1).reshape(N_DP, N_COL, local_count)
    placed = jnp.take_along_axis(anchor, inverse, axis=-1)
    placed = placed.reshape(N_DP, N_COL, MB, BIN).transpose(2, 0, 1, 3).reshape(MB, N_DP * PACK)
    return placed.astype(jnp.int32)


def block_levels(rng, dims, cuts, smallest, high):
    level = 1.0
    for position, parts in cuts:
        draws = jax.random.uniform(jax.random.fold_in(jax.random.fold_in(rng, 6), position), (parts,), jnp.float32, smallest / len(cuts), high / len(cuts))
        level = level * jnp.repeat(jnp.exp(draws), dims[position] // parts).reshape((-1,) + (1,) * (len(dims) - 1 - position))
    return level


def bell_draw(key, dims, deviation, limit, cuts=(), kind=jnp.bfloat16):
    array = deviation * jax.random.normal(key, dims, jnp.float32)
    if cuts:
        array = array * block_levels(key, dims, cuts, -0.22, 0.18)
    return jnp.clip(array, -limit, limit).astype(kind)


def setup_inputs(seed: int = 0) -> dict:
    splits = jax.random.split(jax.random.key(seed), 15)
    return {
        "inputs": bell_draw(splits[0], (MB, D, N_DP * PACK), 1.0, 6.0, ((1, 4), (2, 8))),
        "cotangent": bell_draw(splits[1], (MB, D, N_DP * PACK), 1.0, 6.0, ((1, 4), (2, 8))),
        "lengths": draw_lengths(jax.random.fold_in(splits[14], 71), 0),
        "source": draw_source(jax.random.fold_in(splits[14], 71), 0),
        "query_weight": bell_draw(splits[4], (D, D), D ** -0.5, 0.21875, ((0, 4), (1, 4))),
        "key_weight": bell_draw(splits[5], (D, D), D ** -0.5, 0.21875, ((0, 4), (1, 4))),
        "value_weight": bell_draw(splits[6], (D, D), D ** -0.5, 0.21875, ((0, 4), (1, 4))),
        "output_weight": bell_draw(splits[7], (D, D), (max(1, 4 * D // (BIN * N_COL))) ** -0.5, 6.0, ((0, 4), (1, 4))),
        "inner_weight": bell_draw(splits[8], (D, FF), D ** -0.5, 0.21875, ((0, 4), (1, 4))),
        "outer_weight": bell_draw(splits[9], (D, FF), FF ** -0.5, 0.109375, ((0, 4), (1, 4))),
        "first_gain": jnp.clip(1.0 + 0.1 * jax.random.normal(splits[10], (D,), jnp.float32), 0.5, 1.5),
        "first_shift": bell_draw(splits[11], (D,), 0.3, 3.0, ((0, 4),), jnp.float32),
        "second_gain": jnp.clip(1.0 + 0.1 * jax.random.normal(splits[12], (D,), jnp.float32), 0.5, 1.5),
        "second_shift": bell_draw(splits[13], (D,), 0.3, 3.0, ((0, 4),), jnp.float32),
    }


EPSILON = 1e-05
MASKED_SCORE = -1e+30

@jax.custom_vjp
def low(v):
    return lax.optimization_barrier(v.astype(jnp.bfloat16)).astype(jnp.float32)

@jax.custom_vjp
def low_back(v):
    return v

def low_keep(v):
    return (low(v), None)

def low_pass(kept, grad):
    return (grad,)

def back_keep(v):
    return (v, None)

def back_low(kept, grad):
    return (low(grad),)
low.defvjp(low_keep, low_pass)
low_back.defvjp(back_keep, back_low)

def rotate(values, positions, rotation_sign):
    row_count, feature = values.shape
    paired = values.reshape(row_count, feature // DH, DH // 2, 2)
    frequency = 10000.0 ** (-2.0 * jnp.arange(DH // 2, dtype=jnp.float32) / DH)
    angles = positions.astype(jnp.float32)[:, None] * frequency[None, :]
    cosine = jnp.cos(angles)[:, None, :]
    sine_part = rotation_sign * jnp.sin(angles)[:, None, :]
    former = paired[..., 0]
    latter = paired[..., 1]
    turned = jnp.stack([former * cosine - latter * sine_part, latter * cosine + former * sine_part], -1)
    return turned.reshape(row_count, feature)

def normalize(values, gain, shift):
    centre = lax.optimization_barrier(jnp.mean(values, -1, keepdims=True))
    centred = values - centre
    spread = lax.optimization_barrier(jnp.mean(centred * centred, -1, keepdims=True))
    return centred * lax.rsqrt(spread + EPSILON) * gain + shift

def product(left, right):
    return jnp.dot(left, right, precision=lax.Precision.HIGHEST)

def pack_layer(tokens_f, params, boundary):
    query_w, key_w, value_w, output_w, inner_w, outer_w, first_gain, first_shift, second_gain, second_shift = params
    positions = jnp.arange(PACK, dtype=jnp.int32)
    second_seq = positions >= boundary
    places = positions - jnp.where(second_seq, boundary, 0)
    queries = low(rotate(low_back(product(tokens_f, query_w)), places, 1.0))
    keys_all = low(rotate(low_back(product(tokens_f, key_w)), places, 1.0))
    values_all = low(low_back(product(tokens_f, value_w)))
    query_blocks = queries.reshape(PACK // BIN, BIN, H, DH)
    side_blocks = second_seq.reshape(PACK // BIN, BIN)
    key_heads = keys_all.reshape(PACK, H, DH)
    value_heads = values_all.reshape(PACK, H, DH)

    def attend_block(block_pair):
        block_queries, block_side = block_pair
        scores = low_back(jnp.einsum('qhd,khd->hqk', block_queries, key_heads, precision=lax.Precision.HIGHEST) * DH ** (-0.5))
        same_seq = (block_side[:, None] == second_seq[None, :])[None]
        masked = jnp.where(same_seq, scores, MASKED_SCORE)
        weights_low = low(jax.nn.softmax(masked, axis=-1))
        return jnp.einsum('hqk,khd->qhd', weights_low, value_heads, precision=lax.Precision.HIGHEST)
    attended = lax.map(jax.checkpoint(attend_block), (query_blocks, side_blocks))
    attended = low(low_back(attended.reshape(PACK, D)))
    branch = low_back(product(attended, output_w))
    hidden = normalize(tokens_f + branch, first_gain, first_shift)
    inner = low_back(product(low(hidden), inner_w))
    outer = low_back(product(low(jax.nn.gelu(inner, approximate=False)), outer_w.T))
    return normalize(hidden + outer, second_gain, second_shift)

def reference(inputs, cotangent, lengths, source, query_weight, key_weight, value_weight, output_weight, inner_weight, outer_weight, first_gain, first_shift, second_gain, second_shift):
    flat_source = source.reshape(-1)

    def to_packs(values):
        dealt = values.transpose(0, 2, 1).reshape(-1, D)[flat_source].astype(jnp.float32)
        return dealt.reshape(MB, N_DP, PACK, D).transpose(1, 0, 2, 3).reshape(N_DP * MB, PACK, D)
    token_packs = to_packs(inputs)
    cot_packs = to_packs(cotangent)
    boundaries = lengths.reshape(-1).astype(jnp.int32)
    params = tuple((member.astype(jnp.float32) for member in (query_weight, key_weight, value_weight, output_weight, inner_weight, outer_weight, first_gain, first_shift, second_gain, second_shift)))

    def one_pack(running, pack_item):
        pack_tokens, pack_cot, boundary = pack_item
        result, pullback = jax.vjp(lambda tokens_f, weights_f: pack_layer(tokens_f, weights_f, boundary), pack_tokens, params)
        grad_tokens, grad_params = pullback(pack_cot)
        running = tuple((total + piece_grad for total, piece_grad in zip(running, grad_params)))
        return (running, (result.astype(jnp.bfloat16), grad_tokens.astype(jnp.bfloat16)))
    initial = tuple((jnp.zeros_like(member) for member in params))
    summed_grads, (results, grad_inputs) = lax.scan(one_pack, initial, (token_packs, cot_packs, boundaries))

    def from_packs(values):
        dealt = values.reshape(N_DP, MB, PACK, D).transpose(1, 0, 2, 3).reshape(-1, D)
        placed = jnp.zeros((MB * N_DP * PACK, D), jnp.bfloat16).at[flat_source].set(dealt)
        return placed.reshape(MB, N_DP * PACK, D).transpose(0, 2, 1)
    return (from_packs(results), from_packs(grad_inputs), summed_grads[0], summed_grads[1], summed_grads[2], summed_grads[3], summed_grads[4], summed_grads[5], summed_grads[6], summed_grads[7], summed_grads[8], summed_grads[9])
```

```python
import jax
import jax.numpy as jnp
from jax import lax
from jax.experimental import pallas as pl
from jax.experimental.pallas import tpu as pltpu
from jax.sharding import Mesh, PartitionSpec as P

DH = 64
EPSILON = 1e-05
MASKED = -1e30
LOG2E = 1.4426950408889634
SWAP = ((0, 1), (1, 0))
ROWS = ("ya", "yb")
SHARDS = ("ya", "yb", "col")
bf16 = jnp.bfloat16
f32 = jnp.float32


def contract(left, right, dims):
    return lax.dot_general(left, right, ((dims[:1], dims[1:]), ((), ())), preferred_element_type=f32)


def swap(values, axis):
    return lax.ppermute(values, axis, SWAP)


def gather_rows(values):
    first, second = lax.axis_index("ya") == 0, lax.axis_index("yb") == 0
    other = swap(values, "ya")
    pair = jnp.stack([jnp.where(first, values, other), jnp.where(first, other, values)])
    twin = swap(pair, "yb")
    both = jnp.stack([jnp.where(second, pair, twin), jnp.where(second, twin, pair)], 1)
    return both.reshape((4,) + values.shape)


def spread_dp(values):
    if lax.axis_size("dp") == 2:
        other = swap(values, "dp")
        first = lax.axis_index("dp") == 0
        return jnp.stack([jnp.where(first, values, other), jnp.where(first, other, values)])
    return lax.all_gather(values, "dp", axis=0)


def turn(values, cosine, sine):
    lanes = values.shape[1]
    even = lax.broadcasted_iota(jnp.int32, values.shape, 1) % 2 == 0
    swapped = jnp.where(even, pltpu.roll(values, lanes - 1, 1), pltpu.roll(values, 1, 1))
    return values * cosine + swapped * sine


def project_kernel(x_ref, w_ref, cos_ref, sin_ref, q_ref, k_ref, kt_ref, v_ref, vt_ref):
    width = q_ref.shape[1]
    wide = jnp.dot(x_ref[...], w_ref[...], preferred_element_type=f32)
    turned = turn(wide[:, : 2 * width], cos_ref[...], sin_ref[...])
    q_ref[...] = turned[:, :width].astype(bf16)
    keys = turned[:, width:]
    k_ref[...] = keys.astype(bf16)
    kt_ref[...] = keys.T.astype(bf16)
    values = wide[:, 2 * width :]
    v_ref[...] = values.astype(bf16)
    vt_ref[...] = values.T.astype(bf16)


def project(tokens, weight, cosine, sine, block):
    count, feature = tokens.shape
    width = weight.shape[1] // 3
    by_row = lambda lanes: pl.BlockSpec((block, lanes), lambda i: (i, 0))
    by_col = pl.BlockSpec((width, block), lambda i: (0, i))
    row_shape = jax.ShapeDtypeStruct((count, width), bf16)
    col_shape = jax.ShapeDtypeStruct((width, count), bf16)
    return pl.pallas_call(
        project_kernel,
        grid=(count // block,),
        in_specs=[by_row(feature), pl.BlockSpec(weight.shape, lambda i: (0, 0)), by_row(2 * width), by_row(2 * width)],
        out_specs=[by_row(width), by_row(width), by_col, by_row(width), by_col],
        out_shape=[row_shape, row_shape, col_shape, row_shape, col_shape],
        name="project",
    )(tokens, weight, cosine, sine)


def head_rows(values, head):
    rows = lax.broadcasted_iota(jnp.int32, values.shape, 0)
    return jnp.where((rows >= head * DH) & (rows < (head + 1) * DH), values, jnp.zeros_like(values))


def head_lanes(values, head):
    lanes = lax.broadcasted_iota(jnp.int32, values.shape, 1)
    return jnp.where((lanes >= head * DH) & (lanes < (head + 1) * DH), values, jnp.zeros_like(values))


def forward_kernel(q_ref, k0_ref, k1_ref, vt0_ref, vt1_ref, side_q_ref, side0_ref, side1_ref, o_ref, lse_ref):
    queries = q_ref[...]
    scaling = DH ** (-0.5) * LOG2E
    same0 = side0_ref[...] == side_q_ref[...]
    same1 = side1_ref[...] == side_q_ref[...]
    for head in range(queries.shape[1] // DH):
        part = head_lanes(queries, head)
        s0 = jnp.where(same0, contract(k0_ref[...], part, (1, 1)) * scaling, MASKED)
        s1 = jnp.where(same1, contract(k1_ref[...], part, (1, 1)) * scaling, MASKED)
        highest = jnp.maximum(jnp.max(s0, 0, keepdims=True), jnp.max(s1, 0, keepdims=True))
        p0 = jnp.exp2(s0 - highest)
        p1 = jnp.exp2(s1 - highest)
        total = jnp.sum(p0, 0, keepdims=True) + jnp.sum(p1, 0, keepdims=True)
        rows = pl.ds(head * DH, DH)
        mixed = jnp.dot(vt0_ref[rows, :], p0.astype(bf16), preferred_element_type=f32) + jnp.dot(
            vt1_ref[rows, :], p1.astype(bf16), preferred_element_type=f32
        )
        o_ref[0, rows, :] = (mixed / total).astype(bf16)
        lse_ref[pl.ds(head, 1), :] = highest + jnp.log2(total)


def attend_forward(q, k, vt, side_row, side_col, block):
    count, width = q.shape
    heads = width // DH
    whole = lambda a: pl.BlockSpec(a.shape, lambda i: (0, 0))
    return pl.pallas_call(
        forward_kernel,
        grid=(count // block,),
        in_specs=[
            pl.BlockSpec((block, width), lambda i: (i, 0)),
            whole(k[0]),
            whole(k[1]),
            whole(vt[0]),
            whole(vt[1]),
            pl.BlockSpec((1, block), lambda i: (0, i)),
            whole(side_col[0]),
            whole(side_col[1]),
        ],
        out_specs=[
            pl.BlockSpec((1, width, block), lambda i: (i, 0, 0)),
            pl.BlockSpec((heads, block), lambda i: (0, i)),
        ],
        out_shape=[
            jax.ShapeDtypeStruct((count // block, width, block), bf16),
            jax.ShapeDtypeStruct((heads, count), f32),
        ],
        compiler_params=pltpu.CompilerParams(vmem_limit_bytes=50 << 20),
        name="attend_forward",
    )(q, k[0], k[1], vt[0], vt[1], side_row, side_col[0], side_col[1])


def backward_kernel(
    q_ref, k0_ref, k1_ref, kt0_ref, kt1_ref, v0_ref, v1_ref, g_ref, o_ref, lse_ref, side_q_ref, side0_ref, side1_ref,
    dq_ref, dk_ref, dv_ref,
):
    scaling = DH ** (-0.5)
    queries = q_ref[...]
    grad = g_ref[0]
    product = grad.astype(f32) * o_ref[0].astype(f32)
    sides = (side0_ref[...] == side_q_ref[...], side1_ref[...] == side_q_ref[...])

    @pl.when(pl.program_id(0) == 0)
    def _():
        dk_ref[...] = jnp.zeros_like(dk_ref)
        dv_ref[...] = jnp.zeros_like(dv_ref)

    pieces = []
    for head in range(queries.shape[1] // DH):
        part_q = head_lanes(queries, head)
        part_g = head_rows(grad, head)
        rows = pl.ds(head * DH, DH)
        delta = jnp.sum(product[head * DH : (head + 1) * DH], 0, keepdims=True)
        lse = lse_ref[pl.ds(head, 1), :]
        dq = None
        for half, (k, kt, v) in enumerate(((k0_ref, kt0_ref, v0_ref), (k1_ref, kt1_ref, v1_ref))):
            scores = jnp.where(sides[half], contract(k[...], part_q, (1, 1)) * (scaling * LOG2E), MASKED)
            probs = jnp.exp2(scores - lse)
            grad_probs = jnp.dot(v[...], part_g, preferred_element_type=f32)
            grad_scores = (probs * (grad_probs - delta)).astype(bf16)
            dv_ref[half] += contract(probs.astype(bf16), part_g, (1, 1))
            dk_ref[half] += jnp.dot(grad_scores, part_q, preferred_element_type=f32)
            piece = jnp.dot(kt[rows, :], grad_scores, preferred_element_type=f32)
            dq = piece if dq is None else dq + piece
        pieces.append(dq)
    dq_ref[...] = jnp.concatenate(pieces, 0).T * scaling


def attend_backward(q, k, kt, v, grad, out, lse, side_row, side_col, block):
    count, width = q.shape
    heads = width // DH
    whole = lambda a: pl.BlockSpec(a.shape, lambda i: (0, 0))
    turned = pl.BlockSpec((1, width, block), lambda i: (i, 0, 0))
    sums = pl.BlockSpec((2, count, width), lambda i: (0, 0, 0))
    return pl.pallas_call(
        backward_kernel,
        grid=(count // block,),
        in_specs=[
            pl.BlockSpec((block, width), lambda i: (i, 0)),
            whole(k[0]), whole(k[1]), whole(kt[0]), whole(kt[1]), whole(v[0]), whole(v[1]),
            turned, turned,
            pl.BlockSpec((heads, block), lambda i: (0, i)),
            pl.BlockSpec((1, block), lambda i: (0, i)),
            whole(side_col[0]), whole(side_col[1]),
        ],
        out_specs=[pl.BlockSpec((block, width), lambda i: (i, 0)), sums, sums],
        out_shape=[
            jax.ShapeDtypeStruct((count, width), f32),
            jax.ShapeDtypeStruct((2, count, width), f32),
            jax.ShapeDtypeStruct((2, count, width), f32),
        ],
        compiler_params=pltpu.CompilerParams(vmem_limit_bytes=56 << 20),
        name="attend_backward",
    )(q, k[0], k[1], kt[0], kt[1], v[0], v[1], grad, out, lse, side_row, side_col[0], side_col[1])


def norm_forward(values, gain, shift):
    centre = jnp.mean(values, 1, keepdims=True)
    centred = values - centre
    inverse = lax.rsqrt(jnp.mean(centred * centred, 1, keepdims=True) + EPSILON)
    normed = centred * inverse
    return normed * gain + shift, normed, inverse


def norm_backward(grad, normed, inverse, gain):
    scaled = grad * gain
    first = jnp.mean(scaled, 1, keepdims=True)
    second = jnp.mean(scaled * normed, 1, keepdims=True)
    return inverse * (scaled - first - normed * second)


def gelu_pair(values):
    cumulative = 0.5 * (1.0 + lax.erf(values * (0.5**0.5)))
    density = jnp.exp(-0.5 * values * values) * 0.3989422804014327
    return values * cumulative, cumulative + values * density


def split_three(values):
    high = values.astype(bf16)
    rest = values - high.astype(f32)
    middle = rest.astype(bf16)
    return jnp.stack([high, middle, (rest - middle.astype(f32)).astype(bf16)])


def body(
    inputs, cotangent, lengths, source, query_weight, key_weight, value_weight, output_weight, inner_weight, outer_weight,
    first_gain, first_shift, second_gain, second_shift,
):
    micro, quarter, share = inputs.shape
    dp_count, columns = lax.axis_size("dp"), lax.axis_size("col")
    pack, own = share * columns, share // 2
    feature, count = 4 * quarter, share * micro
    me, m, half, z = (lax.axis_index(a) for a in ("dp", "ya", "yb", "col"))

    qkv_weight = gather_rows(jnp.concatenate([query_weight, key_weight, value_weight], 1)).reshape(feature, -1)
    vectors = split_three(jnp.stack([first_gain, first_shift, second_gain, second_shift])).reshape(-1, inner_weight.shape[1])
    rows_of = lambda a: a.reshape(-1, inner_weight.shape[1])
    parcel = jnp.concatenate([inner_weight, outer_weight, rows_of(output_weight), vectors], 0)
    sizes = [inner_weight.shape[0], outer_weight.shape[0], rows_of(output_weight).shape[0], vectors.shape[0]]
    parcel = jnp.pad(parcel, ((0, -sum(sizes) % 16), (0, 0)))
    everywhere = lax.all_gather(parcel, SHARDS, axis=0).reshape((4, columns) + parcel.shape)
    ends = [sum(sizes[: i + 1]) for i in range(4)]
    full_inner = everywhere[:, :, : ends[0]].transpose(0, 2, 1, 3).reshape(feature, -1)
    full_outer = everywhere[:, :, ends[0] : ends[1]].transpose(0, 2, 1, 3).reshape(feature, -1)
    full_output = everywhere[:, :, ends[1] : ends[2]].reshape(4, columns, *output_weight.shape)
    full_output = full_output.transpose(1, 2, 0, 3).reshape(feature, feature)
    pieces = everywhere[:, 0, ends[2] : ends[3]].reshape(4, 3, 4, quarter).astype(f32)
    gain_one, shift_one, gain_two, shift_two = (
        (pieces[:, 0] + (pieces[:, 1] + pieces[:, 2])).transpose(1, 0, 2).reshape(4, 1, feature)
    )

    anchors = spread_dp(source)
    anchor = source.reshape(count)
    place = anchor // (dp_count * pack) * share + anchor % share
    holder = anchor % (dp_count * pack) // pack
    wide_in, wide_cot = spread_dp(inputs), spread_dp(cotangent)
    if dp_count == 2:
        pick = (holder * count + place)[:, None] == jnp.arange(dp_count * count, dtype=jnp.int32)[None, :]
        pick = pick.astype(bf16).reshape(count, dp_count, micro, share)
        deal = lambda wide: jnp.einsum("tsmj,smfj->tf", pick, wide, preferred_element_type=f32).astype(bf16)
    else:
        deal = lambda wide: wide.transpose(0, 1, 3, 2).reshape(-1, quarter)[holder * count + place]

    def to_tokens(dealt):
        moved = lax.all_to_all(dealt.reshape(4, own, quarter), ROWS, split_axis=0, concat_axis=0, tiled=True)
        return moved.transpose(1, 0, 2).reshape(own, feature)

    tokens = to_tokens(deal(wide_in))
    cot = to_tokens(deal(wide_cot))

    boundary = jnp.where(m == 0, lengths[0, 0], lengths[0, 1])
    spots = jnp.arange(columns, dtype=jnp.int32)[:, None] * share + jnp.arange(own, dtype=jnp.int32)[None, :]
    mine = (spots + half * own).reshape(-1)
    twin = (spots + (1 - half) * own).reshape(-1)
    side = lambda where: (where >= boundary).astype(f32)
    side_row = side(mine)[None, :]
    side_col = (side(mine)[:, None], side(twin)[:, None])
    frequency = 10000.0 ** (-2.0 * jnp.arange(DH // 2, dtype=f32) / DH)
    angles = (mine - jnp.where(mine >= boundary, boundary, 0)).astype(f32)[:, None] * jnp.repeat(frequency, 2)[None, :]
    signs = jnp.where(jnp.arange(DH) % 2 == 0, -1.0, 1.0)
    width = query_weight.shape[1]
    copies = 2 * width // DH
    cosine, sine = jnp.tile(jnp.cos(angles), (1, copies)), jnp.tile(jnp.sin(angles) * signs, (1, copies))

    parts = [lax.all_gather(tokens[i * own // 2 : (i + 1) * own // 2], "col", axis=0) for i in range(2)]
    tokens_full = jnp.concatenate(parts, 1).reshape(columns * own, feature)
    q, k, kt, v, vt = project(tokens_full, qkv_weight, cosine, sine, own)
    k_pair, vt_pair = (k, swap(k, "yb")), (vt, swap(vt, "yb"))
    kt_pair, v_pair = (kt, swap(kt, "yb")), (v, swap(v, "yb"))
    attended, lse = attend_forward(q, k_pair, vt_pair, side_row, side_col, own)
    over_cols = lambda a: lax.all_to_all(a, "col", split_axis=0, concat_axis=0, tiled=True)
    attended_t = over_cols(attended).reshape(feature, own)

    branch = contract(attended_t, full_output, (0, 0))
    hidden, normed_one, inverse_one = norm_forward(tokens.astype(f32) + branch, gain_one, shift_one)
    hidden_low = hidden.astype(bf16)
    inner = jnp.dot(hidden_low, full_inner, preferred_element_type=f32)
    activated, slope = gelu_pair(inner)
    activated = activated.astype(bf16)
    outer = contract(activated, full_outer, (1, 1))
    result, normed_two, inverse_two = norm_forward(hidden + outer, gain_two, shift_two)
    cot_wide = cot.astype(f32)
    grad_two = norm_backward(cot_wide, normed_two, inverse_two, gain_two)
    grad_two_low = grad_two.astype(bf16)
    grad_outer = contract(grad_two_low, activated, (0, 0))
    grad_inner_low = (jnp.dot(grad_two_low, full_outer, preferred_element_type=f32) * slope).astype(bf16)
    grad_inner = contract(hidden_low, grad_inner_low, (0, 0))
    grad_hidden = grad_two + contract(grad_inner_low, full_inner, (1, 1))
    grad_one = norm_backward(grad_hidden, normed_one, inverse_one, gain_one)
    grad_one_low = grad_one.astype(bf16)
    grad_output = jnp.dot(attended_t, grad_one_low, preferred_element_type=f32)
    grad_vectors = jnp.stack(
        [jnp.sum(grad_hidden * normed_one, 0), jnp.sum(grad_hidden, 0), jnp.sum(cot_wide * normed_two, 0), jnp.sum(cot_wide, 0)]
    )

    def shards(grad):
        cut = grad.astype(bf16).reshape(4, quarter, columns, -1).transpose(0, 2, 1, 3)
        return cut

    output_cut = grad_output.astype(bf16).reshape(columns, -1, 4, quarter).transpose(2, 0, 1, 3)
    output_cut = output_cut.reshape(4, columns, -1, inner_weight.shape[1])
    vector_cut = grad_vectors.astype(bf16).reshape(4, 4, quarter).transpose(1, 0, 2).reshape(4, 1, -1, inner_weight.shape[1])
    vector_cut = jnp.broadcast_to(vector_cut, (4, columns) + vector_cut.shape[2:])
    parcel = jnp.concatenate([shards(grad_inner), shards(grad_outer), output_cut, vector_cut], 2)
    sizes[3] = vector_cut.shape[2]
    parcel = jnp.pad(parcel, ((0, 0), (0, 0), (0, -sum(sizes) % 16), (0, 0)))
    parcel = parcel.reshape((4 * columns,) + parcel.shape[2:])
    summed = lax.psum_scatter(parcel, SHARDS, scatter_dimension=0, tiled=False)
    summed = (
        summed.astype(f32) + swap(summed, "dp").astype(f32) if dp_count == 2 else lax.psum(summed, "dp").astype(f32)
    )
    ends = [sum(sizes[: i + 1]) for i in range(4)]
    sum_inner, sum_outer = summed[: ends[0]], summed[ends[0] : ends[1]]
    sum_output = summed[ends[1] : ends[2]].reshape(output_weight.shape)
    sum_vectors = summed[ends[2] : ends[3]].reshape(4, quarter)

    grad_att = contract(full_output, grad_one_low, (1, 1)).astype(bf16).reshape(columns, width, own)
    grad_att = over_cols(grad_att)
    dq, dk, dv = attend_backward(q, k_pair, kt_pair, v_pair, grad_att, attended, lse, side_row, side_col, own)
    dk_low, dv_low = dk.astype(bf16), dv.astype(bf16)
    dk = dk[0] + swap(dk_low[1], "yb").astype(f32)
    dv = dv[0] + swap(dv_low[1], "yb").astype(f32)
    dk = dk * DH ** (-0.5)
    even = (jnp.arange(width) % 2 == 0)[None, :]

    def turn_back(values):
        swapped = jnp.where(even, jnp.roll(values, -1, 1), jnp.roll(values, 1, 1))
        return values * cosine[:, :width] - swapped * sine[:, :width]

    grad_low = jnp.concatenate([turn_back(dq), turn_back(dk), dv], 1).astype(bf16)
    grad_qkv = contract(tokens_full, grad_low, (0, 0)).astype(bf16).reshape(4, quarter, -1)
    grad_qkv = lax.psum_scatter(grad_qkv, ROWS, scatter_dimension=0, tiled=False)
    grad_qkv = (
        grad_qkv.astype(f32) + swap(grad_qkv, "dp").astype(f32) if dp_count == 2 else lax.psum(grad_qkv, "dp").astype(f32)
    )
    partial = contract(grad_low, qkv_weight, (1, 1)).astype(bf16).reshape(columns, own, feature)
    grad_tokens = grad_one + jnp.sum(over_cols(partial).astype(f32), 0)

    def to_loader(rows):
        cut = rows.astype(bf16).reshape(own, 4, quarter).transpose(1, 0, 2)
        moved = lax.all_to_all(cut, ROWS, split_axis=0, concat_axis=0, tiled=True).reshape(count, quarter)
        return spread_dp(moved)

    spot = jnp.arange(count, dtype=jnp.int32)
    wanted = spot // share * (dp_count * pack) + me * pack + z * share + spot % share
    if dp_count == 2:
        put = (anchors.reshape(-1)[:, None] == wanted[None, :]).astype(bf16)
        settle = lambda wide: contract(wide.reshape(-1, quarter), put, (0, 0)).astype(bf16)
    else:
        order = jnp.argsort(anchors.reshape(-1))
        spots_in = jnp.searchsorted(anchors.reshape(-1)[order], wanted)
        settle = lambda wide: wide.reshape(-1, quarter)[order[spots_in]].T
    shape = lambda a: a.reshape(quarter, micro, share).transpose(1, 0, 2)
    final_out = shape(settle(to_loader(result)))
    final_grad = shape(settle(to_loader(grad_tokens)))
    return (
        final_out, final_grad, grad_qkv[:, :width], grad_qkv[:, width : 2 * width], grad_qkv[:, 2 * width :],
        sum_output, sum_inner, sum_outer, sum_vectors[0], sum_vectors[1], sum_vectors[2], sum_vectors[3],
    )


def solution(mesh):
    dp, row, col = (mesh.shape[a] for a in ("dp", "row", "col"))
    fine = Mesh(mesh.devices.reshape(dp, 2, row // 2, col), ("dp", "ya", "yb", "col"))
    tokens, matrix = P(None, ROWS, ("dp", "col")), P(ROWS, "col")
    weights = (matrix, matrix, matrix, P("col", ROWS), matrix, matrix, P(ROWS), P(ROWS), P(ROWS), P(ROWS))
    return jax.shard_map(
        body,
        mesh=fine,
        in_specs=(tokens, tokens, P("dp", None), P(None, ("dp", "col"))) + weights,
        out_specs=(tokens, tokens) + weights,
        check_vma=False,
    )
```

```python
import jax
import jax.numpy as jnp
from jax import lax
from jax.experimental import pallas as pl
from jax.experimental.pallas import tpu as pltpu
from jax.sharding import Mesh, PartitionSpec as P

DH = 64
EPSILON = 1e-05
MASKED = -1e30
LOG2E = 1.4426950408889634
SWAP = ((0, 1), (1, 0))
ROWS = ("ya", "yb")
SHARDS = ("ya", "yb", "col")
bf16 = jnp.bfloat16
f32 = jnp.float32


def contract(left, right, dims):
    return lax.dot_general(left, right, ((dims[:1], dims[1:]), ((), ())), preferred_element_type=f32)


def swap(values, axis):
    return lax.ppermute(values, axis, SWAP)


def gather_rows(values):
    first, second = lax.axis_index("ya") == 0, lax.axis_index("yb") == 0
    other = swap(values, "ya")
    pair = jnp.stack([jnp.where(first, values, other), jnp.where(first, other, values)])
    twin = swap(pair, "yb")
    both = jnp.stack([jnp.where(second, pair, twin), jnp.where(second, twin, pair)], 1)
    return both.reshape((4,) + values.shape)


def spread_dp(values):
    if lax.axis_size("dp") == 2:
        other = swap(values, "dp")
        first = lax.axis_index("dp") == 0
        return jnp.stack([jnp.where(first, values, other), jnp.where(first, other, values)])
    return lax.all_gather(values, "dp", axis=0)


def turn(values, cosine, sine):
    lanes = values.shape[1]
    even = lax.broadcasted_iota(jnp.int32, values.shape, 1) % 2 == 0
    swapped = jnp.where(even, pltpu.roll(values, lanes - 1, 1), pltpu.roll(values, 1, 1))
    return values * cosine + swapped * sine


def project_kernel(x_ref, w_ref, cos_ref, sin_ref, q_ref, k_ref, kt_ref, v_ref, vt_ref):
    width = q_ref.shape[1]
    wide = jnp.dot(x_ref[...], w_ref[...], preferred_element_type=f32)
    turned = turn(wide[:, : 2 * width], cos_ref[...], sin_ref[...])
    q_ref[...] = turned[:, :width].astype(bf16)
    keys = turned[:, width:]
    k_ref[0] = keys.astype(bf16)
    kt_ref[0] = keys.T.astype(bf16)
    values = wide[:, 2 * width :]
    v_ref[0] = values.astype(bf16)
    vt_ref[0] = values.T.astype(bf16)


def project(tokens, weight, cosine, sine, block):
    count, feature = tokens.shape
    width = weight.shape[1] // 3
    by_row = lambda lanes: pl.BlockSpec((block, lanes), lambda i: (i, 0))
    by_block = pl.BlockSpec((1, block, width), lambda i: (i, 0, 0))
    by_col = pl.BlockSpec((1, width, block), lambda i: (i, 0, 0))
    row_shape = jax.ShapeDtypeStruct((count // block, block, width), bf16)
    col_shape = jax.ShapeDtypeStruct((count // block, width, block), bf16)
    return pl.pallas_call(
        project_kernel,
        grid=(count // block,),
        in_specs=[by_row(feature), pl.BlockSpec(weight.shape, lambda i: (0, 0)), by_row(2 * width), by_row(2 * width)],
        out_specs=[by_row(width), by_block, by_col, by_block, by_col],
        out_shape=[jax.ShapeDtypeStruct((count, width), bf16), row_shape, col_shape, row_shape, col_shape],
        name="project",
    )(tokens, weight, cosine, sine)


def head_rows(values, head):
    rows = lax.broadcasted_iota(jnp.int32, values.shape, 0)
    return jnp.where((rows >= head * DH) & (rows < (head + 1) * DH), values, jnp.zeros_like(values))


def head_lanes(values, head):
    lanes = lax.broadcasted_iota(jnp.int32, values.shape, 1)
    return jnp.where((lanes >= head * DH) & (lanes < (head + 1) * DH), values, jnp.zeros_like(values))


def block_sides(info_ref, query_block, key_block, columns, share, own):
    boundary, half = info_ref[0], info_ref[1]
    low_q = query_block * share + half * own
    low_k = key_block % columns * share + jnp.where(key_block < columns, half, 1 - half) * own
    first_q, second_q = low_q < boundary, low_q + own > boundary
    first_k, second_k = low_k < boundary, low_k + own > boundary
    meets = (first_q & first_k) | (second_q & second_k)
    mixed = (first_q & second_q) | (first_k & second_k)
    side_q = low_q + lax.broadcasted_iota(jnp.int32, (1, own), 1) >= boundary
    side_k = low_k + lax.broadcasted_iota(jnp.int32, (own, 1), 0) >= boundary
    return meets, mixed, side_q.astype(f32), side_k.astype(f32)


def forward_kernel(share, info_ref, q_ref, k_ref, vt_ref, o_ref, lse_ref, parts, top, total, mixed_sum):
    own, width = q_ref.shape
    columns = k_ref.shape[0] // 2
    heads = width // DH
    scaling = DH ** (-0.5) * LOG2E
    query_block = pl.program_id(0)
    for head in range(heads):
        parts[head] = head_lanes(q_ref[...], head)
    top[...] = jnp.full_like(top, MASKED)
    total[...] = jnp.zeros_like(total)
    mixed_sum[...] = jnp.zeros_like(mixed_sum)

    def visit(key_block, same):
        for head in range(heads):
            rows = pl.ds(head * DH, DH)
            line = pl.ds(head, 1)
            scores = contract(k_ref[key_block], parts[head], (1, 1)) * scaling
            if same is not None:
                scores = jnp.where(same, scores, MASKED)
            before = top[line, :]
            highest = jnp.maximum(before, jnp.max(scores, 0, keepdims=True))
            fade = jnp.exp2(before - highest)
            raised = jnp.exp2(scores - highest)
            if same is not None:
                raised = jnp.where(same, raised, 0.0)
            top[line, :] = highest
            total[line, :] = total[line, :] * fade + jnp.sum(raised, 0, keepdims=True)
            product = jnp.dot(vt_ref[key_block, rows, :], raised.astype(bf16), preferred_element_type=f32)
            mixed_sum[rows, :] = mixed_sum[rows, :] * fade + product

    def step(key_block, carry):
        meets, mixed, side_q, side_k = block_sides(info_ref, query_block, key_block, columns, share, own)

        @pl.when(meets & mixed)
        def _():
            visit(key_block, side_q == side_k)

        @pl.when(meets & jnp.logical_not(mixed))
        def _():
            visit(key_block, None)

        return carry

    lax.fori_loop(0, 2 * columns, step, 0)
    for head in range(heads):
        rows = pl.ds(head * DH, DH)
        line = pl.ds(head, 1)
        o_ref[0, rows, :] = (mixed_sum[rows, :] / total[line, :]).astype(bf16)
        lse_ref[0, line, :] = top[line, :] + jnp.log2(total[line, :])


def attend_forward(info, q, k, vt, share, own):
    count, width = q.shape
    heads = width // DH
    blocks = count // own
    whole = lambda a: pl.BlockSpec(a.shape, lambda i, s: (0, 0, 0))
    return pl.pallas_call(
        lambda *refs: forward_kernel(share, *refs),
        grid_spec=pltpu.PrefetchScalarGridSpec(
            num_scalar_prefetch=1,
            grid=(blocks,),
            in_specs=[pl.BlockSpec((own, width), lambda i, s: (i, 0)), whole(k), whole(vt)],
            out_specs=[
                pl.BlockSpec((1, width, own), lambda i, s: (i, 0, 0)),
                pl.BlockSpec((1, heads, own), lambda i, s: (i, 0, 0)),
            ],
            scratch_shapes=[
                pltpu.VMEM((heads, own, width), bf16),
                pltpu.VMEM((heads, own), f32),
                pltpu.VMEM((heads, own), f32),
                pltpu.VMEM((width, own), f32),
            ],
        ),
        out_shape=[
            jax.ShapeDtypeStruct((blocks, width, own), bf16),
            jax.ShapeDtypeStruct((blocks, heads, own), f32),
        ],
        compiler_params=pltpu.CompilerParams(vmem_limit_bytes=40 << 20),
        name="attend_forward",
    )(info, q, k, vt)


def backward_kernel(
    share, info_ref, q_ref, k_ref, kt_ref, v_ref, g_ref, o_ref, lse_ref, dq_ref, dk_ref, dv_ref, far_k_ref, far_v_ref,
    part_q, part_g, delta, sum_q, sum_k, sum_v,
):
    own, width = q_ref.shape
    columns = k_ref.shape[0] // 2
    heads = width // DH
    scaling = DH ** (-0.5)
    query_block = pl.program_id(0)
    product = g_ref[0].astype(f32) * o_ref[0].astype(f32)
    for head in range(heads):
        part_q[pl.ds(head * own, own), :] = head_lanes(q_ref[...], head)
        part_g[:, pl.ds(head * own, own)] = head_rows(g_ref[0], head)
        delta[pl.ds(head, 1), :] = jnp.sum(product[head * DH : (head + 1) * DH], 0, keepdims=True)
    sum_q[...] = jnp.zeros_like(sum_q)

    @pl.when(query_block == 0)
    def _():
        sum_k[...] = jnp.zeros_like(sum_k)
        sum_v[...] = jnp.zeros_like(sum_v)

    def visit(key_block, same):
        all_probs, all_grads = [], []
        for head in range(heads):
            scores = contract(k_ref[key_block], part_q[pl.ds(head * own, own), :], (1, 1)) * (scaling * LOG2E)
            probs = jnp.exp2(scores - lse_ref[0, pl.ds(head, 1), :])
            if same is not None:
                probs = jnp.where(same, probs, 0.0)
            slopes = jnp.dot(v_ref[key_block], part_g[:, pl.ds(head * own, own)], preferred_element_type=f32)
            grads = (probs * (slopes - delta[pl.ds(head, 1), :])).astype(bf16)
            rows = pl.ds(head * DH, DH)
            sum_q[rows, :] += jnp.dot(kt_ref[key_block, rows, :], grads, preferred_element_type=f32)
            all_probs.append(probs.astype(bf16))
            all_grads.append(grads)
        sum_v[key_block] += contract(jnp.concatenate(all_probs, 1), part_g[...], (1, 1))
        sum_k[key_block] += jnp.dot(jnp.concatenate(all_grads, 1), part_q[...], preferred_element_type=f32)

    def step(key_block, carry):
        meets, mixed, side_q, side_k = block_sides(info_ref, query_block, key_block, columns, share, own)

        @pl.when(meets & mixed)
        def _():
            visit(key_block, side_q == side_k)

        @pl.when(meets & jnp.logical_not(mixed))
        def _():
            visit(key_block, None)

        return carry

    lax.fori_loop(0, 2 * columns, step, 0)
    dq_ref[...] = sum_q[...].T * scaling

    @pl.when(query_block == pl.num_programs(0) - 1)
    def _():
        dk_ref[...] = sum_k[:columns]
        dv_ref[...] = sum_v[:columns]
        far_k_ref[...] = sum_k[columns:].astype(bf16)
        far_v_ref[...] = sum_v[columns:].astype(bf16)


def attend_backward(info, q, k, kt, v, grad, out, lse, share, own):
    count, width = q.shape
    heads = width // DH
    blocks = count // own
    whole = lambda a: pl.BlockSpec(a.shape, lambda i, s: (0, 0, 0))
    turned = pl.BlockSpec((1, width, own), lambda i, s: (i, 0, 0))
    sums = pl.BlockSpec((blocks, own, width), lambda i, s: (0, 0, 0))
    sum_shape = lambda kind: jax.ShapeDtypeStruct((blocks, own, width), kind)
    return pl.pallas_call(
        lambda *refs: backward_kernel(share, *refs),
        grid_spec=pltpu.PrefetchScalarGridSpec(
            num_scalar_prefetch=1,
            grid=(blocks,),
            in_specs=[
                pl.BlockSpec((own, width), lambda i, s: (i, 0)),
                whole(k), whole(kt), whole(v), turned, turned,
                pl.BlockSpec((1, heads, own), lambda i, s: (i, 0, 0)),
            ],
            out_specs=[pl.BlockSpec((own, width), lambda i, s: (i, 0)), sums, sums, sums, sums],
            scratch_shapes=[
                pltpu.VMEM((heads * own, width), bf16),
                pltpu.VMEM((width, heads * own), bf16),
                pltpu.VMEM((heads, own), f32),
                pltpu.VMEM((width, own), f32),
                pltpu.VMEM((2 * blocks, own, width), f32),
                pltpu.VMEM((2 * blocks, own, width), f32),
            ],
        ),
        out_shape=[jax.ShapeDtypeStruct((count, width), f32), sum_shape(f32), sum_shape(f32), sum_shape(bf16), sum_shape(bf16)],
        compiler_params=pltpu.CompilerParams(vmem_limit_bytes=50 << 20),
        name="attend_backward",
    )(info, q, k, kt, v, grad, out, lse)


def unproject_kernel(
    dq_ref, dk_ref, far_k_ref, dv_ref, far_v_ref, x_ref, w_ref, cos_ref, sin_ref, part_ref, grad_ref, total
):
    width = dq_ref.shape[1]
    step = pl.program_id(0)

    def turn_back(values):
        lanes = lax.broadcasted_iota(jnp.int32, values.shape, 1)
        ahead = jnp.concatenate([values[:, 1:], values[:, :1]], 1)
        behind = jnp.concatenate([values[:, -1:], values[:, :-1]], 1)
        return values * cos_ref[:, :width] - jnp.where(lanes % 2 == 0, ahead, behind) * sin_ref[:, :width]

    dk = (dk_ref[0] + far_k_ref[0].astype(f32)) * DH ** (-0.5)
    dv = dv_ref[0] + far_v_ref[0].astype(f32)
    low = jnp.concatenate([turn_back(dq_ref[...]), turn_back(dk), dv], 1).astype(bf16)
    part_ref[0] = contract(low, w_ref[...], (1, 1)).astype(bf16)
    piece = contract(x_ref[...], low, (0, 0))

    @pl.when(step == 0)
    def _():
        total[...] = piece

    @pl.when(step > 0)
    def _():
        total[...] += piece

    @pl.when(step == pl.num_programs(0) - 1)
    def _():
        grad_ref[...] = total[...].astype(bf16)


def unproject(dq, dk, far_k, dv, far_v, tokens, weight, cosine, sine, own):
    count, width = dq.shape
    feature = tokens.shape[1]
    flat = lambda a: pl.BlockSpec((own, a.shape[1]), lambda i: (i, 0))
    block = pl.BlockSpec((1, own, width), lambda i: (i, 0, 0))
    whole = pl.BlockSpec(weight.shape, lambda i: (0, 0))
    return pl.pallas_call(
        unproject_kernel,
        grid=(count // own,),
        in_specs=[flat(dq), block, block, block, block, flat(tokens), whole, flat(cosine), flat(sine)],
        out_specs=[pl.BlockSpec((1, own, feature), lambda i: (i, 0, 0)), whole],
        out_shape=[jax.ShapeDtypeStruct((count // own, own, feature), bf16), jax.ShapeDtypeStruct(weight.shape, bf16)],
        scratch_shapes=[pltpu.VMEM(weight.shape, f32)],
        compiler_params=pltpu.CompilerParams(vmem_limit_bytes=40 << 20),
        name="unproject",
    )(dq, dk, far_k, dv, far_v, tokens, weight, cosine, sine)


def mean_lanes(values):
    return jnp.sum(values, 1, keepdims=True) * (1.0 / values.shape[1])


def norm_forward(values, gain, shift):
    centred = values - mean_lanes(values)
    inverse = lax.rsqrt(mean_lanes(centred * centred) + EPSILON)
    normed = centred * inverse
    return normed * gain + shift, normed, inverse


def norm_backward(grad, normed, inverse, gain):
    scaled = grad * gain
    return inverse * (scaled - mean_lanes(scaled) - normed * mean_lanes(scaled * normed))


def unit(size):
    rows = lax.broadcasted_iota(jnp.int32, (size, size), 0)
    return (rows == lax.broadcasted_iota(jnp.int32, (size, size), 1)).astype(bf16)


def feed_kernel(
    att_ref, x_ref, cot_ref, w_ref,
    result_ref, grad_att_ref, grad_one_ref, hidden_ref, act_ref, gin_ref, gtwo_ref, gone_ref, sums_ref,
    w, slopes, outer, sems,
):
    rows, columns, quarter, _ = w.shape
    hidden_cols = act_ref.shape[2]
    both = 2 * hidden_cols
    spans = ((0, hidden_cols), (hidden_cols, hidden_cols), (both, w.shape[3] - both))

    def copy(kind, column):
        lanes = pl.ds(*spans[kind])
        if kind == 2:
            return pltpu.make_async_copy(w_ref.at[:, :, :, lanes], w.at[:, :, :, lanes], sems.at[kind, 0])
        return pltpu.make_async_copy(w_ref.at[:, column, :, lanes], w.at[:, column, :, lanes], sems.at[kind, column])

    copy(2, 0).start()
    for column in range(columns):
        copy(0, column).start()
        copy(1, column).start()

    def block(kind, column):
        lanes = pl.ds(*spans[kind])
        return jnp.concatenate([w[row, column, :, lanes] for row in range(rows)], 0)

    copy(2, 0).wait()
    mix = pl.ds(both, quarter)
    attended = att_ref[...]
    branch = []
    for row in range(rows):
        weight = jnp.concatenate([w[row, column, :, mix] for column in range(columns)], 0)
        branch.append(contract(attended, weight, (0, 0)))
    branch = jnp.concatenate(branch, 1)
    eye = unit(quarter)
    small = [contract(w[row, 0, :, pl.ds(both + quarter, 12)], eye, (0, 0)) for row in range(rows)]
    small = jnp.concatenate(small, 1)
    vectors = small[0:4] + (small[4:8] + small[8:12])
    gain_one, shift_one, gain_two, shift_two = (vectors[i : i + 1] for i in range(4))

    hidden, normed_one, inverse_one = norm_forward(x_ref[...].astype(f32) + branch, gain_one, shift_one)
    hidden_ref[...] = hidden.astype(bf16)
    outer[...] = jnp.zeros_like(outer)

    def forward(column, carry):
        copy(0, column).wait()
        inner = jnp.dot(hidden_ref[...], block(0, column), preferred_element_type=f32)
        cumulative = 0.5 * (1.0 + lax.erf(inner * (0.5**0.5)))
        slopes[column] = cumulative + inner * (jnp.exp(-0.5 * inner * inner) * 0.3989422804014327)
        act_ref[column] = (inner * cumulative).astype(bf16)
        copy(1, column).wait()
        outer[...] += contract(act_ref[column], block(1, column), (1, 1))
        return carry

    lax.fori_loop(0, columns, forward, 0)
    result, normed_two, inverse_two = norm_forward(hidden + outer[...], gain_two, shift_two)
    result_ref[...] = result.astype(bf16)
    cot = cot_ref[...].astype(f32)
    grad_two = norm_backward(cot, normed_two, inverse_two, gain_two)
    gtwo_ref[...] = grad_two.astype(bf16)
    outer[...] = grad_two

    def backward(column, carry):
        grad = jnp.dot(gtwo_ref[...], block(1, column), preferred_element_type=f32)
        gin_ref[column] = (grad * slopes[column]).astype(bf16)
        outer[...] += contract(gin_ref[column], block(0, column), (1, 1))
        return carry

    lax.fori_loop(0, columns, backward, 0)
    grad_hidden = outer[...]
    grad_one = norm_backward(grad_hidden, normed_one, inverse_one, gain_one)
    grad_one_ref[...] = grad_one
    gone_ref[...] = grad_one.astype(bf16)
    for column in range(columns):
        weight = jnp.concatenate([w[row, column, :, mix] for row in range(rows)], 1)
        grad_att_ref[column] = contract(weight, gone_ref[...], (1, 1)).astype(bf16)
    sums_ref[0:1, :] = jnp.sum(grad_hidden * normed_one, 0, keepdims=True)
    sums_ref[1:2, :] = jnp.sum(grad_hidden, 0, keepdims=True)
    sums_ref[2:3, :] = jnp.sum(cot * normed_two, 0, keepdims=True)
    sums_ref[3:4, :] = jnp.sum(cot, 0, keepdims=True)


def feed(attended, tokens, cot, weights):
    own, feature = tokens.shape
    rows, columns, quarter, lanes = weights.shape
    hidden_cols = feature
    vmem = pl.BlockSpec(memory_space=pltpu.VMEM)
    wide = jax.ShapeDtypeStruct((columns, own, hidden_cols), bf16)
    flat = lambda kind: jax.ShapeDtypeStruct((own, feature), kind)
    return pl.pallas_call(
        feed_kernel,
        in_specs=[vmem, vmem, vmem, pl.BlockSpec(memory_space=pl.ANY)],
        out_specs=[vmem] * 9,
        out_shape=[
            flat(bf16), jax.ShapeDtypeStruct((columns, quarter, own), bf16), flat(f32), flat(bf16), wide, wide,
            flat(bf16), flat(bf16), jax.ShapeDtypeStruct((4, feature), f32),
        ],
        scratch_shapes=[
            pltpu.VMEM(weights.shape, bf16),
            pltpu.VMEM((columns, own, hidden_cols), f32),
            pltpu.VMEM((own, feature), f32),
            pltpu.SemaphoreType.DMA((3, columns)),
        ],
        compiler_params=pltpu.CompilerParams(vmem_limit_bytes=58 << 20),
        name="feed",
    )(attended, tokens, cot, weights)


def weigh_kernel(att_ref, hidden_ref, act_ref, gin_ref, gtwo_ref, gone_ref, sums_ref, out_ref):
    rows, _, quarter, _ = out_ref.shape
    hidden_cols = act_ref.shape[2]
    inner = contract(hidden_ref[...], gin_ref[0], (0, 0)).astype(bf16)
    outer = contract(gtwo_ref[...], act_ref[0], (0, 0)).astype(bf16)
    mixed = jnp.dot(att_ref[...], gone_ref[...], preferred_element_type=f32).astype(bf16)
    eye = unit(quarter)
    for row in range(rows):
        mine = slice(row * quarter, (row + 1) * quarter)
        out_ref[row, 0, :, 0:hidden_cols] = inner[mine]
        out_ref[row, 0, :, hidden_cols : 2 * hidden_cols] = outer[mine]
        vector = contract(eye, sums_ref[:, mine].astype(bf16), (1, 1)).astype(bf16)
        rest = jnp.zeros((quarter, out_ref.shape[3] - 2 * hidden_cols - quarter - 4), bf16)
        out_ref[row, 0, :, 2 * hidden_cols :] = jnp.concatenate([mixed[:, mine], vector, rest], 1)


def weigh(attended, hidden, act, gin, gtwo, gone, sums, lanes):
    own, feature = hidden.shape
    columns = act.shape[0]
    quarter = attended.shape[0] // columns
    whole = lambda a: pl.BlockSpec(a.shape, lambda i: (0, 0))
    piece = pl.BlockSpec((1,) + act.shape[1:], lambda i: (i, 0, 0))
    return pl.pallas_call(
        weigh_kernel,
        grid=(columns,),
        in_specs=[
            pl.BlockSpec((quarter, own), lambda i: (i, 0)),
            whole(hidden), piece, piece, whole(gtwo), whole(gone), whole(sums),
        ],
        out_specs=pl.BlockSpec((feature // quarter, 1, quarter, lanes), lambda i: (0, i, 0, 0)),
        out_shape=jax.ShapeDtypeStruct((feature // quarter, columns, quarter, lanes), bf16),
        compiler_params=pltpu.CompilerParams(vmem_limit_bytes=40 << 20),
        name="weigh",
    )(attended, hidden, act, gin, gtwo, gone, sums)


def parcel_kernel(inner_ref, outer_ref, output_ref, small_ref, out_ref):
    columns = inner_ref.shape[1]
    quarter = output_ref.shape[1]
    rest = jnp.zeros((quarter, out_ref.shape[1] - 2 * columns - quarter - 12), bf16)
    out_ref[:, 0:columns] = inner_ref[...]
    out_ref[:, columns : 2 * columns] = outer_ref[...]
    small = contract(unit(quarter), small_ref[...], (1, 1)).astype(bf16)
    out_ref[:, 2 * columns :] = jnp.concatenate([output_ref[...], small, rest], 1)


def parcel(inner, outer, output, small, lanes):
    return pl.pallas_call(
        parcel_kernel,
        out_shape=jax.ShapeDtypeStruct((inner.shape[0], lanes), bf16),
        name="parcel",
    )(inner, outer, output, small)


def split_three(values):
    high = values.astype(bf16)
    rest = values - high.astype(f32)
    middle = rest.astype(bf16)
    return jnp.concatenate([high, middle, (rest - middle.astype(f32)).astype(bf16)], 0)


def keep(values, index, axis=0):
    first, second = lax.index_in_dim(values, 0, axis, False), lax.index_in_dim(values, 1, axis, False)
    chosen = index == 0
    return jnp.where(chosen, first, second), jnp.where(chosen, second, first)


def body(
    inputs, cotangent, lengths, source, query_weight, key_weight, value_weight, output_weight, inner_weight, outer_weight,
    first_gain, first_shift, second_gain, second_shift,
):
    micro, quarter, share = inputs.shape
    dp_count, columns = lax.axis_size("dp"), lax.axis_size("col")
    pack, own = share * columns, share // 2
    feature, count = 4 * quarter, share * micro
    width, hidden_cols = query_weight.shape[1], inner_weight.shape[1]
    lanes = -(-(2 * hidden_cols + quarter + 12) // 128) * 128
    me, m, half, z = (lax.axis_index(a) for a in ("dp", "ya", "yb", "col"))

    vectors = split_three(jnp.stack([first_gain, first_shift, second_gain, second_shift]))
    packed = parcel(inner_weight, outer_weight, output_weight, vectors, lanes)
    everywhere = lax.all_gather(packed, SHARDS, axis=0).reshape(4, columns, quarter, lanes)
    qkv_weight = gather_rows(jnp.concatenate([query_weight, key_weight, value_weight], 1)).reshape(feature, -1)

    anchors = spread_dp(source)
    anchor = source.reshape(count)
    place = anchor // (dp_count * pack) * share + anchor % share
    holder = anchor % (dp_count * pack) // pack
    wide_in, wide_cot = spread_dp(inputs), spread_dp(cotangent)
    if dp_count == 2:
        pick = (holder * count + place)[:, None] == jnp.arange(dp_count * count, dtype=jnp.int32)[None, :]
        pick = pick.astype(bf16).reshape(count, dp_count, micro, share)
        deal = lambda wide: jnp.einsum("tsmj,smfj->tf", pick, wide, preferred_element_type=f32).astype(bf16)
    else:
        deal = lambda wide: wide.transpose(0, 1, 3, 2).reshape(-1, quarter)[holder * count + place]

    def to_tokens(dealt):
        moved = lax.all_to_all(dealt.reshape(4, own, quarter), ROWS, split_axis=0, concat_axis=0, tiled=True)
        return moved.transpose(1, 0, 2).reshape(own, feature)

    tokens = to_tokens(deal(wide_in))
    cot = to_tokens(deal(wide_cot))

    boundary = jnp.where(m == 0, lengths[0, 0], lengths[0, 1])
    info = jnp.stack([boundary, half]).astype(jnp.int32)
    spots = jnp.arange(columns, dtype=jnp.int32)[:, None] * share + jnp.arange(own, dtype=jnp.int32)[None, :]
    mine = (spots + half * own).reshape(-1)
    frequency = 10000.0 ** (-2.0 * jnp.arange(DH // 2, dtype=f32) / DH)
    angles = (mine - jnp.where(mine >= boundary, boundary, 0)).astype(f32)[:, None] * jnp.repeat(frequency, 2)[None, :]
    signs = jnp.where(jnp.arange(DH) % 2 == 0, -1.0, 1.0)
    copies = 2 * width // DH
    cosine, sine = jnp.tile(jnp.cos(angles), (1, copies)), jnp.tile(jnp.sin(angles) * signs, (1, copies))

    parts = [lax.all_gather(tokens[i * own // 2 : (i + 1) * own // 2], "col", axis=0) for i in range(2)]
    tokens_full = jnp.concatenate(parts, 1).reshape(columns * own, feature)
    q, k, kt, v, vt = project(tokens_full, qkv_weight, cosine, sine, own)
    with_twin = lambda a: jnp.concatenate([a, swap(a, "yb")], 0)
    k, kt, v, vt = (with_twin(a) for a in (k, kt, v, vt))
    attended, lse = attend_forward(info, q, k, vt, share, own)
    over_cols = lambda a: lax.all_to_all(a, "col", split_axis=0, concat_axis=0, tiled=True)
    attended_t = over_cols(attended).reshape(feature, own)

    result, grad_att, grad_one, hidden, act, gin, gtwo, gone, sums = feed(attended_t, tokens, cot, everywhere)
    grad_att = over_cols(grad_att)
    cut = weigh(attended_t, hidden, act, gin, gtwo, gone, sums, lanes)
    summed = lax.psum_scatter(cut.reshape(4 * columns, quarter, lanes), SHARDS, scatter_dimension=0, tiled=False)

    dq, dk, dv, far_k, far_v = attend_backward(info, q, k, kt, v, grad_att, attended, lse, share, own)
    far_k, far_v = swap(far_k, "yb"), swap(far_v, "yb")
    partial, grad_qkv = unproject(dq, dk, far_k, dv, far_v, tokens_full, qkv_weight, cosine, sine, own)
    partial = over_cols(partial)
    grad_tokens = grad_one + jnp.sum(partial.astype(f32), 0)

    grad_qkv = grad_qkv.reshape(2, 2, quarter, 3 * width)
    for axis, index, place_axis in (("yb", half, 1), ("ya", m, 0)):
        kept, sent = keep(grad_qkv, index, place_axis)
        grad_qkv = (kept.astype(f32) + swap(sent, axis).astype(f32)).astype(bf16)

    def over_dp(values):
        if dp_count == 2:
            return values.astype(f32) + swap(values, "dp").astype(f32)
        return lax.psum(values, "dp").astype(f32)

    grad_qkv = over_dp(grad_qkv)
    summed = over_dp(summed)
    sum_inner, sum_outer = summed[:, :hidden_cols], summed[:, hidden_cols : 2 * hidden_cols]
    sum_output = summed[:, 2 * hidden_cols : 2 * hidden_cols + quarter]
    sum_vectors = summed[:, 2 * hidden_cols + quarter : 2 * hidden_cols + quarter + 4].T

    def to_loader(rows):
        cut = rows.astype(bf16).reshape(own, 4, quarter).transpose(1, 0, 2)
        moved = lax.all_to_all(cut, ROWS, split_axis=0, concat_axis=0, tiled=True).reshape(count, quarter)
        return spread_dp(moved)

    spot = jnp.arange(count, dtype=jnp.int32)
    wanted = spot // share * (dp_count * pack) + me * pack + z * share + spot % share
    if dp_count == 2:
        put = (anchors.reshape(-1)[:, None] == wanted[None, :]).astype(bf16)
        settle = lambda wide: contract(wide.reshape(-1, quarter), put, (0, 0)).astype(bf16)
    else:
        order = jnp.argsort(anchors.reshape(-1))
        spots_in = jnp.searchsorted(anchors.reshape(-1)[order], wanted)
        settle = lambda wide: wide.reshape(-1, quarter)[order[spots_in]].T
    shape = lambda a: a.reshape(quarter, micro, share).transpose(1, 0, 2)
    final_out = shape(settle(to_loader(result)))
    final_grad = shape(settle(to_loader(grad_tokens)))
    return (
        final_out, final_grad, grad_qkv[:, :width], grad_qkv[:, width : 2 * width], grad_qkv[:, 2 * width :],
        sum_output, sum_inner, sum_outer, sum_vectors[0], sum_vectors[1], sum_vectors[2], sum_vectors[3],
    )


def solution(mesh):
    dp, row, col = (mesh.shape[a] for a in ("dp", "row", "col"))
    fine = Mesh(mesh.devices.reshape(dp, 2, row // 2, col), ("dp", "ya", "yb", "col"))
    tokens, matrix = P(None, ROWS, ("dp", "col")), P(ROWS, "col")
    weights = (matrix, matrix, matrix, P("col", ROWS), matrix, matrix, P(ROWS), P(ROWS), P(ROWS), P(ROWS))
    return jax.shard_map(
        body,
        mesh=fine,
        in_specs=(tokens, tokens, P("dp", None), P(None, ("dp", "col"))) + weights,
        out_specs=(tokens, tokens) + weights,
        check_vma=False,
    )
```

```python
import jax
import jax.numpy as jnp
from jax import lax
from jax.experimental import pallas as pl
from jax.experimental.pallas import tpu as pltpu
from jax.sharding import Mesh, PartitionSpec as P

DH = 64
EPSILON = 1e-05
MASKED = -1e30
LOG2E = 1.4426950408889634
SWAP = ((0, 1), (1, 0))
ROWS = ("ya", "yb")
SHARDS = ("ya", "yb", "col")
bf16 = jnp.bfloat16
f32 = jnp.float32


def cost(microseconds):
    return pl.CostEstimate(flops=int(microseconds * 1e9), bytes_accessed=int(microseconds * 3e6), transcendentals=0)


def contract(left, right, dims):
    return lax.dot_general(left, right, ((dims[:1], dims[1:]), ((), ())), preferred_element_type=f32)


def swap(values, axis):
    return lax.ppermute(values, axis, SWAP)


def gather_rows(values):
    first, second = lax.axis_index("ya") == 0, lax.axis_index("yb") == 0
    other = swap(values, "ya")
    pair = jnp.stack([jnp.where(first, values, other), jnp.where(first, other, values)])
    twin = swap(pair, "yb")
    both = jnp.stack([jnp.where(second, pair, twin), jnp.where(second, twin, pair)], 1)
    return both.reshape((4,) + values.shape)


def spread_dp(values):
    if lax.axis_size("dp") == 2:
        other = swap(values, "dp")
        first = lax.axis_index("dp") == 0
        return jnp.stack([jnp.where(first, values, other), jnp.where(first, other, values)])
    return lax.all_gather(values, "dp", axis=0)


def widen(table, lanes):
    return jnp.concatenate([table] * (lanes // table.shape[1]), 1)


def turn(values, cosine, sine):
    lanes = values.shape[1]
    even = lax.broadcasted_iota(jnp.int32, values.shape, 1) % 2 == 0
    swapped = jnp.where(even, pltpu.roll(values, lanes - 1, 1), pltpu.roll(values, 1, 1))
    return values * widen(cosine, lanes) + swapped * widen(sine, lanes)


def project_kernel(blocks, *refs):
    x_refs, (w_ref, cos_ref, sin_ref) = refs[:blocks], refs[blocks : blocks + 3]
    q_ref, kv_ref, turned_ref, xt_ref = refs[-4:]
    width = q_ref.shape[2]
    for index, x_ref in enumerate(x_refs):
        wide = jnp.dot(x_ref[...], w_ref[...], preferred_element_type=f32)
        xt_ref[index] = x_ref[...].T
        turned = turn(wide[:, : 2 * width], cos_ref[index], sin_ref[index])
        q_ref[index] = turned[:, :width].astype(bf16)
        for place, part in ((index, turned[:, width:]), (blocks + index, wide[:, 2 * width :])):
            kv_ref[place] = part.astype(bf16)
            turned_ref[place] = part.T.astype(bf16)


def project(blocks, weight, cosine, sine):
    own, width, count = blocks[0].shape[0], weight.shape[1] // 3, len(blocks)
    return pl.pallas_call(
        lambda *refs: project_kernel(count, *refs),
        out_shape=[
            jax.ShapeDtypeStruct((count, own, width), bf16),
            jax.ShapeDtypeStruct((2 * count, own, width), bf16),
            jax.ShapeDtypeStruct((2 * count, width, own), bf16),
            jax.ShapeDtypeStruct((count, blocks[0].shape[1], own), bf16),
        ],
        compiler_params=pltpu.CompilerParams(vmem_limit_bytes=16 << 20),
        cost_estimate=cost(0.001),
        name="project",
    )(*blocks, weight, cosine, sine)


def head_rows(values, head):
    rows = lax.broadcasted_iota(jnp.int32, values.shape, 0)
    return jnp.where((rows >= head * DH) & (rows < (head + 1) * DH), values, jnp.zeros_like(values))


def head_lanes(values, head):
    lanes = lax.broadcasted_iota(jnp.int32, values.shape, 1)
    return jnp.where((lanes >= head * DH) & (lanes < (head + 1) * DH), values, jnp.zeros_like(values))


def block_sides(info_ref, query_block, key_block, columns, share, own):
    boundary, half, column = info_ref[0], info_ref[1], info_ref[2]
    place = lambda block: jnp.where(column >= block, column - block, column - block + columns) * share
    low_q = place(query_block) + half * own
    low_k = place(key_block)
    first_q, second_q = low_q < boundary, low_q + own > boundary
    first_k, second_k = low_k < boundary, low_k + share > boundary
    meets = (first_q & first_k) | (second_q & second_k)
    mixed = (first_q & second_q) | (first_k & second_k)
    side_q = low_q + lax.broadcasted_iota(jnp.int32, (1, own), 1) >= boundary
    rows = lax.broadcasted_iota(jnp.int32, (share, 1), 0)
    shift = jnp.where(rows < own, half * own, (1 - half) * own - own)
    side_k = low_k + rows + shift >= boundary
    return meets, mixed, side_q.astype(f32), side_k.astype(f32)


def visit_blocks(info_ref, query_block, columns, share, own, visit):
    def step(key_block, carry):
        meets, mixed, side_q, side_k = block_sides(info_ref, query_block, key_block, columns, share, own)

        @pl.when(meets & mixed)
        def _():
            visit(key_block, side_q == side_k)

        @pl.when(meets & jnp.logical_not(mixed))
        def _():
            visit(key_block, None)

        return carry

    lax.fori_loop(0, columns, step, 0)


def forward_kernel(first, share, info_ref, q_ref, k0_ref, k1_ref, vt0_ref, vt1_ref, *refs):
    columns, own, width = k0_ref.shape
    heads = width // DH
    count = (len(refs) - 4) // 2
    outs, lses, (parts, top, total, sums) = refs[:count], refs[count : 2 * count], refs[2 * count :]
    scaling = DH ** (-0.5) * LOG2E

    def visit(key_block, same):
        keys = jnp.concatenate([k0_ref[key_block], k1_ref[key_block]], 0)
        values = jnp.concatenate([vt0_ref[key_block], vt1_ref[key_block]], 1)
        for head in range(heads):
            rows = pl.ds(head * DH, DH)
            line = pl.ds(head, 1)
            scores = contract(keys, parts[head], (1, 1)) * scaling
            if same is not None:
                scores = jnp.where(same, scores, MASKED)
            before = top[line, :]
            highest = jnp.maximum(before, jnp.max(scores, 0, keepdims=True))
            fade = jnp.exp2(before - highest)
            raised = jnp.exp2(scores - highest)
            if same is not None:
                raised = jnp.where(same, raised, 0.0)
            top[line, :] = highest
            total[line, :] = total[line, :] * fade + jnp.sum(raised, 0, keepdims=True)
            product = jnp.dot(values[head * DH : (head + 1) * DH], raised.astype(bf16), preferred_element_type=f32)
            sums[rows, :] = sums[rows, :] * fade + product

    for index in range(count):
        for head in range(heads):
            parts[head] = head_lanes(q_ref[first + index], head)
        top[...] = jnp.full_like(top, MASKED)
        total[...] = jnp.zeros_like(total)
        sums[...] = jnp.zeros_like(sums)
        visit_blocks(info_ref, first + index, columns, share, own, visit)
        for head in range(heads):
            rows = pl.ds(head * DH, DH)
            line = pl.ds(head, 1)
            outs[index][rows, :] = (sums[rows, :] / total[line, :]).astype(bf16)
            lses[index][line, :] = top[line, :] + jnp.log2(total[line, :])


def attend_forward(first, count, info, q, kv, kv_twin, turned, turned_twin, share):
    columns, own, width = q.shape
    heads = width // DH
    keys = pl.BlockSpec((columns, own, width), lambda i, s: (0, 0, 0))
    values = pl.BlockSpec((columns, width, own), lambda i, s: (1, 0, 0))
    flat = lambda rows: pl.BlockSpec((rows, own), lambda i, s: (0, 0))
    outs = pl.pallas_call(
        lambda *refs: forward_kernel(first, share, *refs),
        grid_spec=pltpu.PrefetchScalarGridSpec(
            num_scalar_prefetch=1,
            grid=(1,),
            in_specs=[keys, keys, keys, values, values],
            out_specs=[flat(width)] * count + [flat(heads)] * count,
            scratch_shapes=[
                pltpu.VMEM((heads, own, width), bf16),
                pltpu.VMEM((heads, own), f32),
                pltpu.VMEM((heads, own), f32),
                pltpu.VMEM((width, own), f32),
            ],
        ),
        out_shape=[jax.ShapeDtypeStruct((width, own), bf16)] * count + [jax.ShapeDtypeStruct((heads, own), f32)] * count,
        compiler_params=pltpu.CompilerParams(vmem_limit_bytes=16 << 20),
        cost_estimate=cost(0.001),
        name="attend_forward",
    )(info, q, kv, kv_twin, turned, turned_twin)
    return outs[:count], outs[count:]


def backward_kernel(columns, share, info_ref, q_ref, kv0_ref, kv1_ref, kt0_ref, kt1_ref, *refs):
    grads, outs, lses, refs = refs[:columns], refs[columns : 2 * columns], refs[2 * columns : 3 * columns], refs[3 * columns :]
    dq_ref, dk_ref, dv_ref, far_k_ref, far_v_ref, part_q, part_g, delta, lse, sum_q, sum_k, sum_v = refs
    _, own, width = q_ref.shape
    heads = width // DH
    scaling = DH ** (-0.5)
    sum_k[...] = jnp.zeros_like(sum_k)
    sum_v[...] = jnp.zeros_like(sum_v)
    for block in range(columns):
        lse[block] = lses[block][...]
        grad = grads[block][...]
        product = grad.astype(f32) * outs[block][...].astype(f32)
        for head in range(heads):
            part_q[block, pl.ds(head * own, own), :] = head_lanes(q_ref[block], head)
            part_g[block, :, pl.ds(head * own, own)] = head_rows(grad, head)
            delta[block, pl.ds(head, 1), :] = jnp.sum(product[head * DH : (head + 1) * DH], 0, keepdims=True)

    def query_step(block, carry):
        sum_q[...] = jnp.zeros_like(sum_q)

        def visit(key_block, same):
            keys = jnp.concatenate([kv0_ref[key_block], kv1_ref[key_block]], 0)
            turned = jnp.concatenate([kt0_ref[key_block], kt1_ref[key_block]], 1)
            values = jnp.concatenate([kv0_ref[columns + key_block], kv1_ref[columns + key_block]], 0)
            all_probs, all_grads = [], []
            for head in range(heads):
                span = pl.ds(head * own, own)
                scores = contract(keys, part_q[block, span, :], (1, 1)) * (scaling * LOG2E)
                probs = jnp.exp2(scores - lse[block, pl.ds(head, 1), :])
                if same is not None:
                    probs = jnp.where(same, probs, 0.0)
                slopes = jnp.dot(values, part_g[block, :, span], preferred_element_type=f32)
                grads = (probs * (slopes - delta[block, pl.ds(head, 1), :])).astype(bf16)
                all_probs.append(probs.astype(bf16))
                all_grads.append(grads)
            for head in range(heads):
                rows = pl.ds(head * DH, DH)
                part = turned[head * DH : (head + 1) * DH]
                sum_q[rows, :] += jnp.dot(part, all_grads[head], preferred_element_type=f32)
            sum_v[key_block] += contract(jnp.concatenate(all_probs, 1), part_g[block], (1, 1))
            sum_k[key_block] += jnp.dot(jnp.concatenate(all_grads, 1), part_q[block], preferred_element_type=f32)

        visit_blocks(info_ref, block, columns, share, own, visit)
        dq_ref[block] = sum_q[...].T * scaling
        return carry

    lax.fori_loop(0, columns, query_step, 0)
    for block in range(columns):
        dk_ref[block] = sum_k[block, :own]
        dv_ref[block] = sum_v[block, :own]
        far_k_ref[block] = sum_k[block, own:].astype(bf16)
        far_v_ref[block] = sum_v[block, own:].astype(bf16)


def attend_backward(info, q, kv, kv_twin, turned, turned_twin, grads, outs, lses, share):
    columns, own, width = q.shape
    heads = width // DH
    vmem = pl.BlockSpec(memory_space=pltpu.VMEM)
    shape = lambda kind: jax.ShapeDtypeStruct((columns, own, width), kind)
    operands = [q, kv, kv_twin, turned, turned_twin, *grads, *outs, *lses]
    return pl.pallas_call(
        lambda *refs: backward_kernel(columns, share, *refs),
        in_specs=[pl.BlockSpec(memory_space=pltpu.SMEM)] + [vmem] * len(operands),
        out_specs=[vmem] * 5,
        out_shape=[shape(f32), shape(f32), shape(f32), shape(bf16), shape(bf16)],
        scratch_shapes=[
            pltpu.VMEM((columns, heads * own, width), bf16),
            pltpu.VMEM((columns, width, heads * own), bf16),
            pltpu.VMEM((columns, heads, own), f32),
            pltpu.VMEM((columns, heads, own), f32),
            pltpu.VMEM((width, own), f32),
            pltpu.VMEM((columns, share, width), f32),
            pltpu.VMEM((columns, share, width), f32),
        ],
        compiler_params=pltpu.CompilerParams(vmem_limit_bytes=28 << 20),
        cost_estimate=cost(0.001),
        name="attend_backward",
    )(info, *operands)


def unproject_kernel(
    info_ref, dq_ref, dk_ref, far_k_ref, dv_ref, far_v_ref, w_ref, cos_ref, sin_ref, xt_ref, part_ref, grad_ref, total
):
    columns = dq_ref.shape[0]
    width = dq_ref.shape[2]
    lanes = 2 * width
    even = lax.broadcasted_iota(jnp.int32, (dq_ref.shape[1], lanes), 1) % 2 == 0
    for block in range(columns):
        dk = (dk_ref[block] + far_k_ref[block].astype(f32)) * DH ** (-0.5)
        dv = dv_ref[block] + far_v_ref[block].astype(f32)
        both = jnp.concatenate([dq_ref[block], dk], 1)
        swapped = jnp.where(even, pltpu.roll(both, lanes - 1, 1), pltpu.roll(both, 1, 1))
        both = both * widen(cos_ref[block], lanes) - swapped * widen(sin_ref[block], lanes)
        low = jnp.concatenate([both, dv], 1).astype(bf16)
        column = info_ref[2] - block
        column = jnp.where(column < 0, column + columns, column)
        part_ref[column] = contract(low, w_ref[...], (1, 1)).astype(bf16)
        piece = jnp.dot(xt_ref[block], low, preferred_element_type=f32)
        if block == 0:
            total[...] = piece
        else:
            total[...] += piece
    grad_ref[...] = total[...].astype(bf16)


def unproject(info, dq, dk, far_k, dv, far_v, tokens_t, weight, cosine, sine):
    columns, own, width = dq.shape
    feature = tokens_t.shape[1]
    return pl.pallas_call(
        unproject_kernel,
        in_specs=[pl.BlockSpec(memory_space=pltpu.SMEM)] + [pl.BlockSpec(memory_space=pltpu.VMEM)] * 9,
        out_shape=[jax.ShapeDtypeStruct((columns, own, feature), bf16), jax.ShapeDtypeStruct(weight.shape, bf16)],
        scratch_shapes=[pltpu.VMEM(weight.shape, f32)],
        compiler_params=pltpu.CompilerParams(vmem_limit_bytes=20 << 20),
        cost_estimate=cost(0.001),
        name="unproject",
    )(info, dq, dk, far_k, dv, far_v, weight, cosine, sine, tokens_t)


def mean_lanes(values):
    return jnp.sum(values, 1, keepdims=True) * (1.0 / values.shape[1])


def norm_forward(values, gain, shift):
    centred = values - mean_lanes(values)
    inverse = lax.rsqrt(mean_lanes(centred * centred) + EPSILON)
    normed = centred * inverse
    return normed * gain + shift, normed, inverse


def norm_backward(grad, normed, inverse, gain):
    scaled = grad * gain
    return inverse * (scaled - mean_lanes(scaled) - normed * mean_lanes(scaled * normed))


def unit(size):
    rows = lax.broadcasted_iota(jnp.int32, (size, size), 0)
    return (rows == lax.broadcasted_iota(jnp.int32, (size, size), 1)).astype(bf16)


def feed_kernel(info_ref, x_ref, cot_ref, w_ref, *refs):
    parts, _, columns, slab, _ = w_ref.shape
    att_refs, refs = refs[:columns], refs[columns:]
    result_ref, refs, grad_atts = refs[0], refs[1 + columns :], refs[1 : 1 + columns]
    grad_one_ref, hidden_ref, act_ref, gin_ref, gtwo_ref, gone_ref, sums_ref, w, slopes, outer, sems = refs
    rows, columns, quarter, _ = w.shape

    def turned(step):
        column = info_ref[2] + step
        return jnp.where(column >= columns, column - columns, column)

    hidden_cols = act_ref.shape[2]
    both = 2 * hidden_cols
    spans = ((0, hidden_cols), (hidden_cols, hidden_cols), (both, w.shape[3] - both))

    def copies(kind):
        lanes = pl.ds(*spans[kind])
        for part in range(parts):
            target = w.at[:, :, pl.ds(part * slab, slab), lanes]
            yield pltpu.make_async_copy(w_ref.at[part, :, :, :, lanes], target, sems.at[kind, part])

    def wait(kind):
        for each in copies(kind):
            each.wait()

    for kind in (2, 0, 1):
        for each in copies(kind):
            each.start()

    def block(kind, column):
        lanes = pl.ds(*spans[kind])
        return jnp.concatenate([w[row, column, :, lanes] for row in range(rows)], 0)

    wait(2)
    mix = pl.ds(both, quarter)
    attended = jnp.concatenate([ref[...] for ref in att_refs], 0)
    branch = []
    for row in range(rows):
        weight = jnp.concatenate([w[row, turned(step), :, mix] for step in range(columns)], 0)
        branch.append(contract(attended, weight, (0, 0)))
    branch = jnp.concatenate(branch, 1)
    eye = unit(quarter)
    small = [contract(w[row, 0, :, pl.ds(both + quarter, 12)], eye, (0, 0)) for row in range(rows)]
    small = jnp.concatenate(small, 1)
    vectors = small[0:4] + (small[4:8] + small[8:12])
    gain_one, shift_one, gain_two, shift_two = (vectors[i : i + 1] for i in range(4))

    hidden, normed_one, inverse_one = norm_forward(x_ref[...].astype(f32) + branch, gain_one, shift_one)
    low = hidden.astype(bf16)
    hidden_ref[...] = low.T
    outer[...] = jnp.zeros_like(outer)

    wait(0)

    def forward(column, carry):
        inner = jnp.dot(low, block(0, column), preferred_element_type=f32)
        cumulative = 0.5 * (1.0 + lax.erf(inner * (0.5**0.5)))
        slopes[column] = cumulative + inner * (jnp.exp(-0.5 * inner * inner) * 0.3989422804014327)
        act_ref[column] = (inner * cumulative).astype(bf16)
        return carry

    lax.fori_loop(0, columns, forward, 0)
    wait(1)

    def combine(column, carry):
        outer[...] += contract(act_ref[column], block(1, column), (1, 1))
        return carry

    lax.fori_loop(0, columns, combine, 0)
    result, normed_two, inverse_two = norm_forward(hidden + outer[...], gain_two, shift_two)
    result_ref[...] = result.astype(bf16)
    cot = jnp.concatenate([cot_ref[row] for row in range(rows)], 1).astype(f32)
    grad_two = norm_backward(cot, normed_two, inverse_two, gain_two)
    grad_two_low = grad_two.astype(bf16)
    gtwo_ref[...] = grad_two_low.T
    outer[...] = grad_two

    def backward(column, carry):
        grad = jnp.dot(grad_two_low, block(1, column), preferred_element_type=f32)
        gin_ref[column] = (grad * slopes[column]).astype(bf16)
        outer[...] += contract(gin_ref[column], block(0, column), (1, 1))
        return carry

    lax.fori_loop(0, columns, backward, 0)
    grad_hidden = outer[...]
    grad_one = norm_backward(grad_hidden, normed_one, inverse_one, gain_one)
    grad_one_ref[...] = grad_one
    gone_ref[...] = grad_one.astype(bf16)
    for step in range(columns):
        weight = jnp.concatenate([w[row, turned(step), :, mix] for row in range(rows)], 1)
        grad_atts[step][...] = contract(weight, gone_ref[...], (1, 1)).astype(bf16)
    sums_ref[0:1, :] = jnp.sum(grad_hidden * normed_one, 0, keepdims=True)
    sums_ref[1:2, :] = jnp.sum(grad_hidden, 0, keepdims=True)
    sums_ref[2:3, :] = jnp.sum(cot * normed_two, 0, keepdims=True)
    sums_ref[3:4, :] = jnp.sum(cot, 0, keepdims=True)


def feed(info, attended, tokens, cot, weights):
    own, feature = tokens.shape
    parts, rows, columns, slab, lanes = weights.shape
    quarter = parts * slab
    hidden_cols = feature
    vmem, smem = pl.BlockSpec(memory_space=pltpu.VMEM), pl.BlockSpec(memory_space=pltpu.SMEM)
    wide = jax.ShapeDtypeStruct((columns, own, hidden_cols), bf16)
    flat = lambda kind: jax.ShapeDtypeStruct((own, feature), kind)
    tall = jax.ShapeDtypeStruct((feature, own), bf16)
    return pl.pallas_call(
        feed_kernel,
        in_specs=[smem, vmem, vmem, pl.BlockSpec(memory_space=pl.ANY)] + [vmem] * columns,
        out_specs=[vmem] * (8 + columns),
        out_shape=[flat(bf16)]
        + [jax.ShapeDtypeStruct((quarter, own), bf16)] * columns
        + [flat(f32), tall, wide, wide, tall, flat(bf16), jax.ShapeDtypeStruct((4, feature), f32)],
        scratch_shapes=[
            pltpu.VMEM((rows, columns, quarter, lanes), bf16),
            pltpu.VMEM((columns, own, hidden_cols), f32),
            pltpu.VMEM((own, feature), f32),
            pltpu.SemaphoreType.DMA((3, parts)),
        ],
        compiler_params=pltpu.CompilerParams(vmem_limit_bytes=34 << 20),
        cost_estimate=cost(0.001),
        name="feed",
    )(info, tokens, cot, weights, *attended)


def weigh_kernel(info_ref, hidden_ref, act_ref, gin_ref, gtwo_ref, gone_ref, sums_ref, *refs):
    att_refs, (kept_ref, sent_ref, across_ref) = refs[:-3], refs[-3:]
    _, slabs, _, slab, lanes = kept_ref.shape
    quarter = slabs * slab
    hidden_cols = act_ref.shape[2]
    columns = len(att_refs)
    step = pl.program_id(0) - info_ref[2]
    step = jnp.where(step < 0, step + columns, step)
    attended = att_refs[0][...]
    for index in range(1, columns):
        attended = jnp.where(step == index, att_refs[index][...], attended)
    inner = jnp.dot(hidden_ref[...], gin_ref[0], preferred_element_type=f32).astype(bf16)
    outer = jnp.dot(gtwo_ref[...], act_ref[0], preferred_element_type=f32).astype(bf16)
    mixed = jnp.dot(attended, gone_ref[...], preferred_element_type=f32).astype(bf16)
    eye = unit(quarter)
    away = lambda index, mine: jnp.where(index == mine, 0, 1)
    for row in range(4):
        mine = slice(row * quarter, (row + 1) * quarter)
        vector = contract(eye, sums_ref[:, mine].astype(bf16), (1, 1)).astype(bf16)
        rest = jnp.zeros((quarter, lanes - 2 * hidden_cols - quarter - 4), bf16)
        tail = jnp.concatenate([mixed[:, mine], vector, rest], 1)
        far = away(row // 2, info_ref[3])

        def write(ref, where, rows):
            ref[where + (0, slice(None), slice(0, hidden_cols))] = inner[mine][rows]
            ref[where + (0, slice(None), slice(hidden_cols, 2 * hidden_cols))] = outer[mine][rows]
            ref[where + (0, slice(None), slice(2 * hidden_cols, lanes))] = tail[rows]

        for part in range(slabs):
            place = away(part, info_ref[4]) if slabs > 1 else 0
            rows = slice(part * slab, (part + 1) * slab)
            kept = info_ref[1] == row % 2
            beyond = (far == 1) & (place == slabs - 1)

            @pl.when(kept)
            def _():
                write(kept_ref, (far, place), rows)

            @pl.when(jnp.logical_not(kept) & beyond)
            def _():
                write(across_ref, (), rows)

            @pl.when(jnp.logical_not(kept | beyond))
            def _():
                write(sent_ref, (far * slabs + place,), rows)


def weigh(info, attended, hidden, act, gin, gtwo, gone, sums, lanes, slabs):
    feature = hidden.shape[0]
    columns = act.shape[0]
    quarter = attended[0].shape[0]
    whole = lambda a: pl.BlockSpec(a.shape, lambda i, s: (0, 0))
    piece = pl.BlockSpec((1,) + act.shape[1:], lambda i, s: (i, 0, 0))
    tail = (columns, quarter // slabs, lanes)
    block = (1,) + tail[1:]
    return pl.pallas_call(
        weigh_kernel,
        grid_spec=pltpu.PrefetchScalarGridSpec(
            num_scalar_prefetch=1,
            grid=(columns,),
            in_specs=[whole(hidden), piece, piece, whole(gtwo), whole(gone), whole(sums)] + [whole(a) for a in attended],
            out_specs=[
                pl.BlockSpec((2, slabs) + block, lambda i, s: (0, 0, i, 0, 0)),
                pl.BlockSpec((2 * slabs - 1,) + block, lambda i, s: (0, i, 0, 0)),
                pl.BlockSpec(block, lambda i, s: (i, 0, 0)),
            ],
        ),
        out_shape=[jax.ShapeDtypeStruct(dims + tail, bf16) for dims in ((2, slabs), (2 * slabs - 1,), ())],
        compiler_params=pltpu.CompilerParams(vmem_limit_bytes=24 << 20),
        cost_estimate=cost(0.001),
        name="weigh",
    )(info, hidden, act, gin, gtwo, gone, sums, *attended)


def parcel_kernel(info_ref, inner_ref, outer_ref, output_ref, *refs):
    small_refs, out_ref = refs[:-1], refs[-1]
    columns = inner_ref.shape[1]
    quarter = output_ref.shape[1]
    slab = out_ref.shape[0]
    offset = info_ref[4] * slab if slab < quarter else 0
    rows = pl.ds(pl.multiple_of(offset, slab), slab)
    values = jnp.concatenate([ref[...] for ref in small_refs], 0)
    high = values.astype(bf16)
    rest = values - high.astype(f32)
    middle = rest.astype(bf16)
    last = (rest - middle.astype(f32)).astype(bf16)
    pick = lax.broadcasted_iota(jnp.int32, (slab, quarter), 0) + offset
    pick = (pick == lax.broadcasted_iota(jnp.int32, (slab, quarter), 1)).astype(bf16)
    small = jnp.concatenate([contract(pick, part, (1, 1)) for part in (high, middle, last)], 1).astype(bf16)
    fill = jnp.zeros((slab, out_ref.shape[1] - 2 * columns - quarter - 12), bf16)
    out_ref[:, 0:columns] = inner_ref[rows, :]
    out_ref[:, columns : 2 * columns] = outer_ref[rows, :]
    out_ref[:, 2 * columns :] = jnp.concatenate([output_ref[rows, :], small, fill], 1)


def parcel(info, inner, outer, output, vectors, lanes, slabs):
    vmem, smem = pl.BlockSpec(memory_space=pltpu.VMEM), pl.BlockSpec(memory_space=pltpu.SMEM)
    return pl.pallas_call(
        parcel_kernel,
        in_specs=[smem] + [vmem] * 7,
        out_shape=jax.ShapeDtypeStruct((inner.shape[0] // slabs, lanes), bf16),
        cost_estimate=cost(0.001),
        name="parcel",
    )(info, inner, outer, output, *(v.reshape(1, -1) for v in vectors))


def keep(values, index, axis=0):
    first, second = lax.index_in_dim(values, 0, axis, False), lax.index_in_dim(values, 1, axis, False)
    chosen = index == 0
    return jnp.where(chosen, first, second), jnp.where(chosen, second, first)


def tie(*values):
    return lax.optimization_barrier(values)


def shift(values, step):
    columns = lax.axis_size("col")
    if step % columns == 0:
        return values
    return lax.ppermute(values, "col", [(i, (i + step) % columns) for i in range(columns)])


def add_kernel(low_only, *refs):
    total = sum(ref[...].reshape(refs[-1].shape).astype(f32) for ref in refs[:-2])
    if low_only is None:
        refs[-1][...] = (total + refs[-2][...].astype(f32)).astype(bf16)
        return
    middle = pl.num_programs(0) // 2
    inside = (pl.program_id(0) < middle) == low_only

    @pl.when(inside)
    def _():
        refs[-1][...] = (total + refs[-2][...].astype(f32)).astype(bf16)

    @pl.when(jnp.logical_not(inside))
    def _():
        refs[-1][...] = total.astype(bf16)


def add_blocks(kept, place, *others, low_only=None):
    columns = kept.shape[2]
    block = (1,) + kept.shape[3:]
    spec = lambda lead: pl.BlockSpec((1,) * len(lead) + block, lambda i: lead + (i, 0, 0))
    arrays, specs = [kept], [spec(place)]
    for array, lead in others:
        arrays.append(array)
        specs.append(spec(lead))
    if low_only is not None:
        middle = columns // 2
        held = (lambda i: jnp.minimum(i, middle - 1)) if low_only else (lambda i: jnp.maximum(i - middle, 0))
        specs[-1] = pl.BlockSpec(block, lambda i: (held(i), 0, 0))
    return pl.pallas_call(
        lambda *refs: add_kernel(low_only, *refs),
        grid=(columns,),
        in_specs=specs,
        out_specs=spec(()),
        out_shape=jax.ShapeDtypeStruct(kept.shape[2:], bf16),
        compiler_params=pltpu.CompilerParams(vmem_limit_bytes=16 << 20),
        cost_estimate=cost(0.001),
        name="add_blocks",
    )(*arrays)


def sum_shards(kept, sent, across, mark):
    middle = kept.shape[2] // 2
    across, twin = swap(across, "yb"), swap(sent, "yb")
    half = lambda span: (kept[1, 1, span].astype(f32) + across[span].astype(f32)).astype(bf16)
    low, high = half(slice(0, middle)), half(slice(middle, None))
    mark, low, high = tie(mark, low, high)
    by_dp, by_ya = swap(low, "dp"), swap(high, "ya")

    def sides(mark):
        low, high, mark = tie(by_dp, by_ya, mark)
        far_ya = add_blocks(kept, (1, 0), (twin, (2,)), (low, ()), low_only=True)
        far_dp = add_blocks(kept, (0, 1), (twin, (1,)), (high, ()), low_only=False)
        mark, far_ya, far_dp = tie(mark, far_ya, far_dp)
        far_ya, far_dp = swap(far_ya, "ya"), swap(far_dp, "dp")

        def finish(mark):
            *parts, mark = tie(far_ya, far_dp, mark)
            own = add_blocks(kept, (0, 0), (twin, (0,)), *((part, ()) for part in parts))
            mine = lax.psum_scatter(own, "col", scatter_dimension=0, tiled=False)
            other = swap(mine, "dp")
            first = lax.axis_index("dp") == 0
            return jnp.concatenate([jnp.where(first, mine, other), jnp.where(first, other, mine)], 0).astype(f32), mark

        return mark, finish

    return mark, sides


def body(
    inputs, cotangent, lengths, source, query_weight, key_weight, value_weight, output_weight, inner_weight, outer_weight,
    first_gain, first_shift, second_gain, second_shift,
):
    micro, quarter, share = inputs.shape
    dp_count, columns = lax.axis_size("dp"), lax.axis_size("col")
    pack, own = share * columns, share // 2
    feature, count = 4 * quarter, share * micro
    width, hidden_cols = query_weight.shape[1], inner_weight.shape[1]
    lanes = -(-(2 * hidden_cols + quarter + 12) // 128) * 128
    me, m, half, z = (lax.axis_index(a) for a in ("dp", "ya", "yb", "col"))

    boundary = jnp.where(m == 0, lengths[0, 0], lengths[0, 1])
    info = jnp.stack([boundary, half, z, m, me]).astype(jnp.int32)
    slabs = 2 if dp_count == 2 else 1

    vectors = (first_gain, first_shift, second_gain, second_shift)
    anchors = spread_dp(source)
    packed = parcel(info, inner_weight, outer_weight, output_weight, vectors, lanes, slabs)
    axes = ("dp",) + SHARDS if slabs == 2 else SHARDS
    everywhere = lax.all_gather(packed, axes, axis=0).reshape(slabs, 4, columns, quarter // slabs, lanes)
    anchor = source.reshape(count)
    place = anchor // (dp_count * pack) * share + anchor % share
    holder = anchor % (dp_count * pack) // pack
    wide_in, wide_cot = spread_dp(inputs), spread_dp(cotangent)
    if dp_count == 2:
        pick = (holder * count + place)[:, None] == jnp.arange(dp_count * count, dtype=jnp.int32)[None, :]
        pick = pick.astype(bf16).reshape(count, dp_count, micro, share)
        deal = lambda wide: jnp.einsum("tsmj,smfj->tf", pick, wide, preferred_element_type=f32).astype(bf16)
    else:
        deal = lambda wide: wide.transpose(0, 1, 3, 2).reshape(-1, quarter)[holder * count + place]

    def to_tokens(dealt):
        return lax.all_to_all(dealt.reshape(4, own, quarter), ROWS, split_axis=0, concat_axis=0, tiled=True)

    dealt = deal(wide_in)
    query_weight, dealt = tie(query_weight, dealt)
    tokens = to_tokens(dealt).transpose(1, 0, 2).reshape(own, feature)
    wide_cot, tokens = tie(wide_cot, tokens)
    cot = to_tokens(deal(wide_cot))
    qkv_weight = jnp.concatenate([query_weight, key_weight, value_weight], 1)
    qkv_weight = gather_rows(qkv_weight).reshape(feature, -1)

    steps = jnp.arange(columns, dtype=jnp.int32)
    spots = ((z - steps) % columns * share + half * own)[:, None] + jnp.arange(own, dtype=jnp.int32)[None, :]
    frequency = 10000.0 ** (-2.0 * jnp.arange(DH // 2, dtype=f32) / DH)
    angles = (spots - jnp.where(spots >= boundary, boundary, 0)).astype(f32)[..., None] * jnp.tile(jnp.repeat(frequency, 2), 2)
    signs = jnp.where(jnp.arange(2 * DH) % 2 == 0, -1.0, 1.0)
    cosine, sine = jnp.cos(angles), jnp.sin(angles) * signs

    blocks = [shift(tokens, step) for step in range(columns)]
    blocks[-1], cot = tie(blocks[-1], cot)
    q, kv, turned, tokens_t = project(blocks, qkv_weight, cosine, sine)
    kv_twin, turned_twin = swap(kv, "yb"), swap(turned, "yb")
    mixed, lses = attend_forward(1, columns - 1, info, q, kv, kv_twin, turned, turned_twin, share)
    q, mixed, cot = tie(q, mixed, cot)
    last = attend_forward(0, 1, info, q, kv, kv_twin, turned, turned_twin, share)
    mixed, lses = last[0] + mixed, last[1] + lses
    attended = [shift(mixed[step], -step) for step in range(columns)]

    result, *grad_att, grad_one, hidden, act, gin, gtwo, gone, sums = feed(info, attended, tokens, cot, everywhere)
    grad_att = [shift(grad_att[step], step) for step in range(columns)]
    def to_loader(*rows):
        cut = jnp.concatenate([a.astype(bf16).reshape(own, 4, quarter).transpose(1, 0, 2) for a in rows], 2)
        cut = jnp.broadcast_to(cut[None], (dp_count,) + cut.shape).reshape(dp_count * 4, own, -1)
        moved = lax.all_to_all(cut, ("dp",) + ROWS, split_axis=0, concat_axis=0, tiled=True)
        return moved.reshape(-1, len(rows) * quarter)

    spot = jnp.arange(count, dtype=jnp.int32)
    wanted = spot // share * (dp_count * pack) + me * pack + z * share + spot % share
    if dp_count == 2:
        put = (anchors.reshape(-1)[:, None] == wanted[None, :]).astype(bf16)
        settle = lambda wide: contract(wide, put, (0, 0)).astype(bf16)
    else:
        order = jnp.argsort(anchors.reshape(-1))
        spots_in = jnp.searchsorted(anchors.reshape(-1)[order], wanted)
        settle = lambda wide: wide[order[spots_in]].T
    kept, sent, across = weigh(info, attended, hidden, act, gin, gtwo, gone, sums, lanes, slabs)
    if slabs == 2:
        grad_att, sides = sum_shards(kept, sent, across, grad_att)
    else:
        flip = lambda a, index, axis: jnp.where(index == 0, a, jnp.flip(a, axis))
        sent = jnp.stack([sent[0], across])[:, None]
        cut = flip(flip(jnp.stack([kept, sent], 1), m, 0), half, 1).reshape(4 * columns, quarter, lanes)
        summed = lax.psum_scatter(cut, SHARDS, scatter_dimension=0, tiled=False)
        summed = lax.psum(summed, "dp").astype(f32)

    dq, dk, dv, far_k, far_v = attend_backward(info, q, kv, kv_twin, turned, turned_twin, grad_att, mixed, lses, share)
    far_k, far_v = swap(far_k, "yb"), swap(far_v, "yb")
    if slabs == 2:
        dq, finish = sides(dq)
    partial, grad_qkv = unproject(info, dq, dk, far_k, dv, far_v, tokens_t, qkv_weight, cosine, sine)
    partial = lax.all_to_all(partial, "col", split_axis=0, concat_axis=0, tiled=True)
    grad_tokens = grad_one + jnp.sum(partial.astype(f32), 0)

    grad_qkv = grad_qkv.reshape(2, 2, quarter, 3 * width)
    for axis, index, place_axis in (("yb", half, 1), ("ya", m, 0)):
        kept, sent = keep(grad_qkv, index, place_axis)
        grad_qkv = (kept.astype(f32) + swap(sent, axis).astype(f32)).astype(bf16)
        if slabs == 2 and axis == "yb":
            summed, grad_qkv = finish(grad_qkv)

    def over_dp(values):
        if dp_count == 2:
            return values.astype(f32) + swap(values, "dp").astype(f32)
        return lax.psum(values, "dp").astype(f32)

    grad_qkv = over_dp(grad_qkv)
    sum_inner, sum_outer = summed[:, :hidden_cols], summed[:, hidden_cols : 2 * hidden_cols]
    sum_output = summed[:, 2 * hidden_cols : 2 * hidden_cols + quarter]
    sum_vectors = summed[:, 2 * hidden_cols + quarter : 2 * hidden_cols + quarter + 4].T

    shape = lambda a: a.reshape(quarter, micro, share).transpose(1, 0, 2)
    settled = settle(to_loader(result, grad_tokens))
    final_out, final_grad = shape(settled[:quarter]), shape(settled[quarter:])
    return (
        final_out, final_grad, grad_qkv[:, :width], grad_qkv[:, width : 2 * width], grad_qkv[:, 2 * width :],
        sum_output, sum_inner, sum_outer, sum_vectors[0], sum_vectors[1], sum_vectors[2], sum_vectors[3],
    )


def solution(mesh):
    dp, row, col = (mesh.shape[a] for a in ("dp", "row", "col"))
    fine = Mesh(mesh.devices.reshape(dp, 2, row // 2, col), ("dp", "ya", "yb", "col"))
    tokens, matrix = P(None, ROWS, ("dp", "col")), P(ROWS, "col")
    weights = (matrix, matrix, matrix, P("col", ROWS), matrix, matrix, P(ROWS), P(ROWS), P(ROWS), P(ROWS))
    return jax.shard_map(
        body,
        mesh=fine,
        in_specs=(tokens, tokens, P("dp", None), P(None, ("dp", "col"))) + weights,
        out_specs=(tokens, tokens) + weights,
        check_vma=False,
    )
```

```python
import jax
import jax.numpy as jnp
from jax import lax
from jax.experimental import pallas as pl
from jax.experimental.pallas import tpu as pltpu
from jax.sharding import Mesh, PartitionSpec as P

DH = 64
EPSILON = 1e-05
MASKED = -1e30
LOG2E = 1.4426950408889634
SWAP = ((0, 1), (1, 0))
ROWS = ("ya", "yb")
SHARDS = ("ya", "yb", "col")
bf16 = jnp.bfloat16
f32 = jnp.float32


def cost(microseconds):
    return pl.CostEstimate(flops=int(microseconds * 1e9), bytes_accessed=int(microseconds * 3e6), transcendentals=0)


def contract(left, right, dims):
    return lax.dot_general(left, right, ((dims[:1], dims[1:]), ((), ())), preferred_element_type=f32)


def swap(values, axis):
    return lax.ppermute(values, axis, SWAP)


def gather_rows(values):
    first, second = lax.axis_index("ya") == 0, lax.axis_index("yb") == 0
    other = swap(values, "ya")
    pair = jnp.stack([jnp.where(first, values, other), jnp.where(first, other, values)])
    twin = swap(pair, "yb")
    both = jnp.stack([jnp.where(second, pair, twin), jnp.where(second, twin, pair)], 1)
    return both.reshape((4,) + values.shape)


def spread_dp(values):
    if lax.axis_size("dp") == 2:
        other = swap(values, "dp")
        first = lax.axis_index("dp") == 0
        return jnp.stack([jnp.where(first, values, other), jnp.where(first, other, values)])
    return lax.all_gather(values, "dp", axis=0)


def widen(table, lanes):
    return jnp.concatenate([table] * (lanes // table.shape[1]), 1)


def turn(values, cosine, sine):
    lanes = values.shape[1]
    even = lax.broadcasted_iota(jnp.int32, values.shape, 1) % 2 == 0
    swapped = jnp.where(even, pltpu.roll(values, lanes - 1, 1), pltpu.roll(values, 1, 1))
    return values * widen(cosine, lanes) + swapped * widen(sine, lanes)


def project_kernel(blocks, *refs):
    x_refs, (w_ref, cos_ref, sin_ref) = refs[:blocks], refs[blocks : blocks + 3]
    q_ref, kv_ref, turned_ref = refs[-3:]
    width = turned_ref.shape[1]
    for index, x_ref in enumerate(x_refs):
        wide = jnp.dot(x_ref[...], w_ref[...], preferred_element_type=f32)
        turned = turn(wide[:, : 2 * width], cos_ref[index], sin_ref[index])
        parts = turned[:, :width], turned[:, width:], wide[:, 2 * width :]
        for ref, place, part in ((q_ref, index, parts[0]), (kv_ref, index, parts[1]), (kv_ref, blocks + index, parts[2])):
            ref[place] = jnp.concatenate([part, jnp.zeros((part.shape[0], ref.shape[2] - width), f32)], 1).astype(bf16)
        turned_ref[index] = parts[1].T.astype(bf16)
        turned_ref[blocks + index] = parts[2].T.astype(bf16)


def project(blocks, weight, cosine, sine):
    own, width, count = blocks[0].shape[0], weight.shape[1] // 3, len(blocks)
    padded = -(-width // 128) * 128
    return pl.pallas_call(
        lambda *refs: project_kernel(count, *refs),
        out_shape=[
            jax.ShapeDtypeStruct((count, own, padded), bf16),
            jax.ShapeDtypeStruct((2 * count, own, padded), bf16),
            jax.ShapeDtypeStruct((2 * count, width, own), bf16),
        ],
        compiler_params=pltpu.CompilerParams(vmem_limit_bytes=60 << 20),
        cost_estimate=cost(0.001),
        name="project",
    )(*blocks, weight, cosine, sine)


def head_rows(values, head):
    rows = lax.broadcasted_iota(jnp.int32, values.shape, 0)
    return jnp.where((rows >= head * DH) & (rows < (head + 1) * DH), values, jnp.zeros_like(values))


def head_lanes(values, head):
    lanes = lax.broadcasted_iota(jnp.int32, values.shape, 1)
    return jnp.where((lanes >= head * DH) & (lanes < (head + 1) * DH), values, jnp.zeros_like(values))


def block_sides(info_ref, query_block, key_block, columns, share, own):
    boundary, half, column = info_ref[0], info_ref[1], info_ref[2]
    place = lambda block: jnp.where(column >= block, column - block, column - block + columns) * share
    low_q = place(query_block) + half * own
    low_k = place(key_block)
    first_q, second_q = low_q < boundary, low_q + own > boundary
    first_k, second_k = low_k < boundary, low_k + share > boundary
    meets = (first_q & first_k) | (second_q & second_k)
    mixed = (first_q & second_q) | (first_k & second_k)
    side_q = low_q + lax.broadcasted_iota(jnp.int32, (1, own), 1) >= boundary
    rows = lax.broadcasted_iota(jnp.int32, (share, 1), 0)
    shift = jnp.where(rows < own, half * own, (1 - half) * own - own)
    side_k = low_k + rows + shift >= boundary
    return meets, mixed, side_q.astype(f32), side_k.astype(f32)


def visit_blocks(info_ref, query_block, columns, share, own, visit):
    def step(key_block, carry):
        meets, mixed, side_q, side_k = block_sides(info_ref, query_block, key_block, columns, share, own)

        @pl.when(meets & mixed)
        def _():
            visit(key_block, side_q == side_k)

        @pl.when(meets & jnp.logical_not(mixed))
        def _():
            visit(key_block, None)

        return carry

    lax.fori_loop(0, columns, step, 0)


def forward_kernel(first, share, info_ref, q_ref, k0_ref, k1_ref, vt0_ref, vt1_ref, *refs):
    columns, own, _ = k0_ref.shape
    width = vt0_ref.shape[1]
    heads = width // DH
    count = (len(refs) - 4) // 2
    outs, lses, (parts, top, total, sums) = refs[:count], refs[count : 2 * count], refs[2 * count :]
    scaling = DH ** (-0.5) * LOG2E

    def visit(key_block, same):
        keys = jnp.concatenate([k0_ref[key_block], k1_ref[key_block]], 0)
        values = jnp.concatenate([vt0_ref[key_block], vt1_ref[key_block]], 1)
        for head in range(heads):
            rows = pl.ds(head * DH, DH)
            line = pl.ds(head, 1)
            scores = contract(keys, parts[head], (1, 1)) * scaling
            if same is not None:
                scores = jnp.where(same, scores, MASKED)
            before = top[line, :]
            highest = jnp.maximum(before, jnp.max(scores, 0, keepdims=True))
            fade = jnp.exp2(before - highest)
            raised = jnp.exp2(scores - highest)
            if same is not None:
                raised = jnp.where(same, raised, 0.0)
            top[line, :] = highest
            total[line, :] = total[line, :] * fade + jnp.sum(raised, 0, keepdims=True)
            product = jnp.dot(values[head * DH : (head + 1) * DH], raised.astype(bf16), preferred_element_type=f32)
            sums[rows, :] = sums[rows, :] * fade + product

    for index in range(count):
        for head in range(heads):
            parts[head] = head_lanes(q_ref[first + index], head)
        top[...] = jnp.full_like(top, MASKED)
        total[...] = jnp.zeros_like(total)
        sums[...] = jnp.zeros_like(sums)
        visit_blocks(info_ref, first + index, columns, share, own, visit)
        for head in range(heads):
            rows = pl.ds(head * DH, DH)
            line = pl.ds(head, 1)
            outs[index][rows, :] = (sums[rows, :] / total[line, :]).astype(bf16)
            lses[index][line, :] = top[line, :] + jnp.log2(total[line, :])


def attend_forward(first, count, info, q, kv, kv_twin, turned, turned_twin, share):
    columns, own, padded = q.shape
    width = turned.shape[1]
    heads = width // DH
    keys = pl.BlockSpec((columns, own, padded), lambda i, s: (0, 0, 0))
    values = pl.BlockSpec((columns, width, own), lambda i, s: (1, 0, 0))
    flat = lambda rows: pl.BlockSpec((rows, own), lambda i, s: (0, 0))
    outs = pl.pallas_call(
        lambda *refs: forward_kernel(first, share, *refs),
        grid_spec=pltpu.PrefetchScalarGridSpec(
            num_scalar_prefetch=1,
            grid=(1,),
            in_specs=[keys, keys, keys, values, values],
            out_specs=[flat(width)] * count + [flat(heads)] * count,
            scratch_shapes=[
                pltpu.VMEM((heads, own, padded), bf16),
                pltpu.VMEM((heads, own), f32),
                pltpu.VMEM((heads, own), f32),
                pltpu.VMEM((width, own), f32),
            ],
        ),
        out_shape=[jax.ShapeDtypeStruct((width, own), bf16)] * count + [jax.ShapeDtypeStruct((heads, own), f32)] * count,
        compiler_params=pltpu.CompilerParams(vmem_limit_bytes=60 << 20),
        cost_estimate=cost(0.001),
        name="attend_forward",
    )(info, q, kv, kv_twin, turned, turned_twin)
    return outs[:count], outs[count:]


def backward_kernel(columns, share, info_ref, q_ref, kv0_ref, kv1_ref, kt0_ref, kt1_ref, *refs):
    grads, outs, lses, refs = refs[0], refs[1 : columns + 1], refs[columns + 1 : 2 * columns + 1], refs[2 * columns + 1 :]
    dq_ref, near_ref, far_ref, part_q, part_g, delta, lse, sum_q, sum_k, sum_v = refs
    own, width = q_ref.shape[1], kt0_ref.shape[1]
    heads = width // DH
    scaling = DH ** (-0.5)
    sum_k[...] = jnp.zeros_like(sum_k)
    sum_v[...] = jnp.zeros_like(sum_v)
    for block in range(columns):
        lse[block] = lses[block][...]
        column = info_ref[2] - block
        grad = grads[jnp.where(column < 0, column + columns, column)]
        spare = jnp.zeros((part_g.shape[1] - width, own), bf16)
        product = grad.astype(f32) * outs[block][...].astype(f32)
        for head in range(heads):
            part_q[block, pl.ds(head * own, own), :] = head_lanes(q_ref[block], head)
            part_g[block, :, pl.ds(head * own, own)] = jnp.concatenate([head_rows(grad, head), spare], 0)
            delta[block, pl.ds(head, 1), :] = jnp.sum(product[head * DH : (head + 1) * DH], 0, keepdims=True)

    def query_step(block, carry):
        sum_q[...] = jnp.zeros_like(sum_q)

        def visit(key_block, same):
            keys = jnp.concatenate([kv0_ref[key_block], kv1_ref[key_block]], 0)
            turned = jnp.concatenate([kt0_ref[key_block], kt1_ref[key_block]], 1)
            values = jnp.concatenate([kv0_ref[columns + key_block], kv1_ref[columns + key_block]], 0)
            all_probs, all_grads = [], []
            for head in range(heads):
                span = pl.ds(head * own, own)
                scores = contract(keys, part_q[block, span, :], (1, 1)) * (scaling * LOG2E)
                probs = jnp.exp2(scores - lse[block, pl.ds(head, 1), :])
                if same is not None:
                    probs = jnp.where(same, probs, 0.0)
                slopes = jnp.dot(values, part_g[block, :, span], preferred_element_type=f32)
                grads = (probs * (slopes - delta[block, pl.ds(head, 1), :])).astype(bf16)
                all_probs.append(probs.astype(bf16))
                all_grads.append(grads)
            for head in range(heads):
                rows = pl.ds(head * DH, DH)
                part = turned[head * DH : (head + 1) * DH]
                sum_q[rows, :] += jnp.dot(part, all_grads[head], preferred_element_type=f32)
            sum_v[key_block] += contract(jnp.concatenate(all_probs, 1), part_g[block], (1, 1))
            sum_k[key_block] += jnp.dot(jnp.concatenate(all_grads, 1), part_q[block], preferred_element_type=f32)

        visit_blocks(info_ref, block, columns, share, own, visit)
        dq_ref[block] = sum_q[...].T * scaling
        return carry

    lax.fori_loop(0, columns, query_step, 0)
    for block in range(columns):
        for place, sums in ((block, sum_k), (columns + block, sum_v)):
            near_ref[place] = sums[block, :own].astype(bf16)
            far_ref[place] = sums[block, own:].astype(bf16)


def attend_backward(info, q, kv, kv_twin, turned, turned_twin, grads, outs, lses, share):
    columns, own, padded = q.shape
    width = turned.shape[1]
    heads = width // DH
    vmem = pl.BlockSpec(memory_space=pltpu.VMEM)
    operands = [q, kv, kv_twin, turned, turned_twin, grads, *outs, *lses]
    return pl.pallas_call(
        lambda *refs: backward_kernel(columns, share, *refs),
        in_specs=[pl.BlockSpec(memory_space=pltpu.SMEM)] + [vmem] * len(operands),
        out_specs=[vmem] * 3,
        out_shape=[jax.ShapeDtypeStruct((columns, own, width), f32)]
        + [jax.ShapeDtypeStruct((2 * columns, own, padded), bf16)] * 2,
        scratch_shapes=[
            pltpu.VMEM((columns, heads * own, padded), bf16),
            pltpu.VMEM((columns, padded, heads * own), bf16),
            pltpu.VMEM((columns, heads, own), f32),
            pltpu.VMEM((columns, heads, own), f32),
            pltpu.VMEM((width, own), f32),
            pltpu.VMEM((columns, share, padded), f32),
            pltpu.VMEM((columns, share, padded), f32),
        ],
        compiler_params=pltpu.CompilerParams(vmem_limit_bytes=60 << 20),
        cost_estimate=cost(0.001),
        name="attend_backward",
    )(info, *operands)


def unproject_kernel(
    info_ref, dq_ref, near_k_ref, far_k_ref, near_v_ref, far_v_ref, w_ref, cos_ref, sin_ref, *refs
):
    x_refs, (part_ref, grad_ref, total) = refs[:-3], refs[-3:]
    step = pl.program_id(0)
    width = dq_ref.shape[2]
    lanes = 2 * width
    even = lax.broadcasted_iota(jnp.int32, (dq_ref.shape[1], lanes), 1) % 2 == 0
    dk = (near_k_ref[0, :, :width].astype(f32) + far_k_ref[0, :, :width].astype(f32)) * DH ** (-0.5)
    dv = near_v_ref[0, :, :width].astype(f32) + far_v_ref[0, :, :width].astype(f32)
    both = jnp.concatenate([dq_ref[0], dk], 1)
    swapped = jnp.where(even, pltpu.roll(both, lanes - 1, 1), pltpu.roll(both, 1, 1))
    both = both * widen(cos_ref[0], lanes) - swapped * widen(sin_ref[0], lanes)
    low = jnp.concatenate([both, dv], 1).astype(bf16)
    part_ref[0] = contract(low, w_ref[...], (1, 1)).astype(bf16)
    for block, x_ref in enumerate(x_refs):

        @pl.when(step == block)
        def _():
            piece = contract(x_ref[...], low, (0, 0))
            total[...] = piece if block == 0 else total[...] + piece

    @pl.when(step == len(x_refs) - 1)
    def _():
        grad_ref[...] = total[...].astype(bf16)


def unproject(info, dq, near, far, blocks, weight, cosine, sine):
    columns, own, width = dq.shape
    feature = blocks[0].shape[1]
    block = lambda a, first: pl.BlockSpec((1,) + a.shape[1:], lambda i, s: (first + i, 0, 0))
    whole = lambda a: pl.BlockSpec(a.shape, lambda i, s: (0, 0))
    place = lambda i, s: (jnp.where(s[2] >= i, s[2] - i, s[2] - i + columns), 0, 0)
    return pl.pallas_call(
        unproject_kernel,
        grid_spec=pltpu.PrefetchScalarGridSpec(
            num_scalar_prefetch=1,
            grid=(columns,),
            in_specs=[block(dq, 0), block(near, 0), block(far, 0), block(near, columns), block(far, columns), whole(weight)]
            + [block(cosine, 0), block(sine, 0)] + [whole(a) for a in blocks],
            out_specs=[pl.BlockSpec((1, own, feature), place), whole(weight)],
            scratch_shapes=[pltpu.VMEM(weight.shape, f32)],
        ),
        out_shape=[jax.ShapeDtypeStruct((columns, own, feature), bf16), jax.ShapeDtypeStruct(weight.shape, bf16)],
        compiler_params=pltpu.CompilerParams(vmem_limit_bytes=60 << 20),
        cost_estimate=cost(0.001),
        name="unproject",
    )(info, dq, near, far, near, far, weight, cosine, sine, *blocks)


def mean_lanes(values):
    return jnp.sum(values, 1, keepdims=True) * (1.0 / values.shape[1])


def norm_forward(values, gain, shift):
    centred = values - mean_lanes(values)
    inverse = lax.rsqrt(mean_lanes(centred * centred) + EPSILON)
    normed = centred * inverse
    return normed * gain + shift, normed, inverse


def norm_backward(grad, normed, inverse, gain):
    scaled = grad * gain
    return inverse * (scaled - mean_lanes(scaled) - normed * mean_lanes(scaled * normed))


def unit(size):
    rows = lax.broadcasted_iota(jnp.int32, (size, size), 0)
    return (rows == lax.broadcasted_iota(jnp.int32, (size, size), 1)).astype(bf16)


def feed_kernel(info_ref, x_ref, cot_ref, w_ref, *refs):
    parts, _, columns, slab, _ = w_ref.shape
    att_refs, refs = refs[:columns], refs[columns:]
    result_ref, grad_att_ref, *refs = refs
    grad_one_ref, hidden_ref, act_ref, gin_ref, gtwo_ref, gone_ref, sums_ref, w, slopes, outer, sems = refs
    rows, columns, quarter, _ = w.shape

    def turned(step):
        column = info_ref[2] + step
        return jnp.where(column >= columns, column - columns, column)

    hidden_cols = act_ref.shape[2]
    both = 2 * hidden_cols
    spans = ((0, hidden_cols), (hidden_cols, hidden_cols), (both, w.shape[3] - both))

    def copies(kind):
        lanes = pl.ds(*spans[kind])
        for part in range(parts):
            target = w.at[:, :, pl.ds(part * slab, slab), lanes]
            yield pltpu.make_async_copy(w_ref.at[part, :, :, :, lanes], target, sems.at[kind, part])

    def wait(kind):
        for each in copies(kind):
            each.wait()

    for kind in (2, 0, 1):
        for each in copies(kind):
            each.start()

    def block(kind, column):
        lanes = pl.ds(*spans[kind])
        return jnp.concatenate([w[row, column, :, lanes] for row in range(rows)], 0)

    wait(2)
    mix = pl.ds(both, quarter)
    attended = jnp.concatenate([ref[...] for ref in att_refs], 0)
    branch = []
    for row in range(rows):
        weight = jnp.concatenate([w[row, turned(step), :, mix] for step in range(columns)], 0)
        branch.append(contract(attended, weight, (0, 0)))
    branch = jnp.concatenate(branch, 1)
    eye = unit(quarter)
    small = [contract(w[row, 0, :, pl.ds(both + quarter, 12)], eye, (0, 0)) for row in range(rows)]
    small = jnp.concatenate(small, 1)
    vectors = small[0:4] + (small[4:8] + small[8:12])
    gain_one, shift_one, gain_two, shift_two = (vectors[i : i + 1] for i in range(4))

    hidden, normed_one, inverse_one = norm_forward(x_ref[...].astype(f32) + branch, gain_one, shift_one)
    low = hidden.astype(bf16)
    hidden_ref[...] = low.T
    outer[...] = jnp.zeros_like(outer)

    wait(0)

    def forward(column, carry):
        inner = jnp.dot(low, block(0, column), preferred_element_type=f32)
        cumulative = 0.5 * (1.0 + lax.erf(inner * (0.5**0.5)))
        slopes[column] = cumulative + inner * (jnp.exp(-0.5 * inner * inner) * 0.3989422804014327)
        act_ref[column] = (inner * cumulative).astype(bf16)
        return carry

    lax.fori_loop(0, columns, forward, 0)
    wait(1)

    def combine(column, carry):
        outer[...] += contract(act_ref[column], block(1, column), (1, 1))
        return carry

    lax.fori_loop(0, columns, combine, 0)
    result, normed_two, inverse_two = norm_forward(hidden + outer[...], gain_two, shift_two)
    result_ref[...] = result.astype(bf16)
    cot = cot_ref[...].astype(f32)
    grad_two = norm_backward(cot, normed_two, inverse_two, gain_two)
    grad_two_low = grad_two.astype(bf16)
    gtwo_ref[...] = grad_two_low.T
    outer[...] = grad_two

    def backward(column, carry):
        grad = jnp.dot(grad_two_low, block(1, column), preferred_element_type=f32)
        gin_ref[column] = (grad * slopes[column]).astype(bf16)
        outer[...] += contract(gin_ref[column], block(0, column), (1, 1))
        return carry

    lax.fori_loop(0, columns, backward, 0)
    grad_hidden = outer[...]
    grad_one = norm_backward(grad_hidden, normed_one, inverse_one, gain_one)
    grad_one_ref[...] = grad_one
    grad_one_low = grad_one.astype(bf16)
    for step in range(columns):
        weight = jnp.concatenate([w[row, turned(step), :, mix] for row in range(rows)], 1)
        grad_att_ref[turned(step)] = contract(weight, grad_one_low, (1, 1)).astype(bf16)
    sums = [jnp.sum(a, 0, keepdims=True) for a in (grad_hidden * normed_one, grad_hidden, cot * normed_two, cot)]
    sums = jnp.concatenate(sums, 0)
    for row in range(rows):
        mine = slice(row * quarter, (row + 1) * quarter)
        gone_ref[row] = grad_one_low[:, mine]
        sums_ref[row] = sums[:, mine].astype(bf16)


def feed(info, attended, tokens, cot, weights):
    own, feature = tokens.shape
    parts, rows, columns, slab, lanes = weights.shape
    quarter = parts * slab
    hidden_cols = feature
    vmem, smem = pl.BlockSpec(memory_space=pltpu.VMEM), pl.BlockSpec(memory_space=pltpu.SMEM)
    wide = jax.ShapeDtypeStruct((columns, own, hidden_cols), bf16)
    flat = lambda kind: jax.ShapeDtypeStruct((own, feature), kind)
    tall = jax.ShapeDtypeStruct((feature, own), bf16)
    return pl.pallas_call(
        feed_kernel,
        in_specs=[smem, vmem, vmem, pl.BlockSpec(memory_space=pltpu.HBM)] + [vmem] * columns,
        out_specs=[vmem] * 9,
        out_shape=[
            flat(bf16), jax.ShapeDtypeStruct((columns, quarter, own), bf16), flat(f32), tall, wide, wide, tall,
            jax.ShapeDtypeStruct((rows, own, quarter), bf16), jax.ShapeDtypeStruct((rows, 4, quarter), bf16),
        ],
        scratch_shapes=[
            pltpu.VMEM((rows, columns, quarter, lanes), bf16),
            pltpu.VMEM((columns, own, hidden_cols), f32),
            pltpu.VMEM((own, feature), f32),
            pltpu.SemaphoreType.DMA((3, parts)),
        ],
        compiler_params=pltpu.CompilerParams(vmem_limit_bytes=60 << 20),
        cost_estimate=cost(0.001),
        name="feed",
    )(info, tokens, cot, weights, *attended)


def weigh_kernel(twin, info_ref, hidden_ref, act_ref, gin_ref, gtwo_ref, gone_ref, sums_ref, *refs):
    att_refs, out_ref = refs[:-1], refs[-1]
    _, slabs, _, slab, lanes = out_ref.shape
    quarter = slabs * slab
    hidden_cols = act_ref.shape[2]
    columns = len(att_refs)
    step = pl.program_id(0) - info_ref[2]
    step = jnp.where(step < 0, step + columns, step)
    attended = att_refs[0][...]
    for index in range(1, columns):
        attended = jnp.where(step == index, att_refs[index][...], attended)
    core = 1 - info_ref[1] if twin else info_ref[1]
    eye = unit(quarter)
    away = lambda index, mine: jnp.where(index == mine, 0, 1)
    for pair in range(2):
        row = 2 * pair + core
        mine = pl.ds(pl.multiple_of(row * quarter, quarter), quarter)
        inner = jnp.dot(hidden_ref[mine, :], gin_ref[0], preferred_element_type=f32).astype(bf16)
        outer = jnp.dot(gtwo_ref[mine, :], act_ref[0], preferred_element_type=f32).astype(bf16)
        mixed = jnp.dot(attended, gone_ref[row], preferred_element_type=f32).astype(bf16)
        vector = contract(eye, sums_ref[row], (1, 1)).astype(bf16)
        rest = jnp.zeros((quarter, lanes - 2 * hidden_cols - quarter - 4), bf16)
        tail = jnp.concatenate([mixed, vector, rest], 1)
        far = away(pair, info_ref[3])
        for part in range(slabs):
            place = away(part, info_ref[4]) if slabs > 1 else 0
            rows = slice(part * slab, (part + 1) * slab)
            out_ref[far, place, 0, :, 0:hidden_cols] = inner[rows]
            out_ref[far, place, 0, :, hidden_cols : 2 * hidden_cols] = outer[rows]
            out_ref[far, place, 0, :, 2 * hidden_cols :] = tail[rows]


def weigh(twin, info, attended, hidden, act, gin, gtwo, gone, sums, lanes, slabs):
    columns = act.shape[0]
    quarter = attended[0].shape[0]
    whole = lambda a: pl.BlockSpec(a.shape, lambda i, s: (0,) * a.ndim)
    piece = pl.BlockSpec((1,) + act.shape[1:], lambda i, s: (i, 0, 0))
    slab = quarter // slabs
    return pl.pallas_call(
        lambda *refs: weigh_kernel(twin, *refs),
        grid_spec=pltpu.PrefetchScalarGridSpec(
            num_scalar_prefetch=1,
            grid=(columns,),
            in_specs=[whole(hidden), piece, piece, whole(gtwo), whole(gone), whole(sums)] + [whole(a) for a in attended],
            out_specs=pl.BlockSpec((2, slabs, 1, slab, lanes), lambda i, s: (0, 0, i, 0, 0)),
        ),
        out_shape=jax.ShapeDtypeStruct((2, slabs, columns, slab, lanes), bf16),
        compiler_params=pltpu.CompilerParams(vmem_limit_bytes=60 << 20),
        cost_estimate=cost(0.001),
        name="weigh",
    )(info, hidden, act, gin, gtwo, gone, sums, *attended)


def parcel_kernel(info_ref, inner_ref, outer_ref, output_ref, *refs):
    small_refs, out_ref = refs[:-1], refs[-1]
    columns = inner_ref.shape[1]
    quarter = output_ref.shape[1]
    slab = out_ref.shape[0]
    offset = info_ref[0] * slab if slab < quarter else 0
    rows = pl.ds(pl.multiple_of(offset, slab), slab)
    values = jnp.concatenate([ref[...] for ref in small_refs], 0)
    high = values.astype(bf16)
    rest = values - high.astype(f32)
    middle = rest.astype(bf16)
    last = (rest - middle.astype(f32)).astype(bf16)
    pick = lax.broadcasted_iota(jnp.int32, (slab, quarter), 0) + offset
    pick = (pick == lax.broadcasted_iota(jnp.int32, (slab, quarter), 1)).astype(bf16)
    small = jnp.concatenate([contract(pick, part, (1, 1)) for part in (high, middle, last)], 1).astype(bf16)
    fill = jnp.zeros((slab, out_ref.shape[1] - 2 * columns - quarter - 12), bf16)
    out_ref[:, 0:columns] = inner_ref[rows, :]
    out_ref[:, columns : 2 * columns] = outer_ref[rows, :]
    out_ref[:, 2 * columns :] = jnp.concatenate([output_ref[rows, :], small, fill], 1)


def parcel(part, inner, outer, output, vectors, lanes, slabs):
    vmem, smem = pl.BlockSpec(memory_space=pltpu.VMEM), pl.BlockSpec(memory_space=pltpu.SMEM)
    return pl.pallas_call(
        parcel_kernel,
        in_specs=[smem] + [vmem] * 7,
        out_shape=jax.ShapeDtypeStruct((inner.shape[0] // slabs, lanes), bf16),
        cost_estimate=cost(0.001),
        name="parcel",
    )(part, inner, outer, output, *(v.reshape(1, -1) for v in vectors))


def keep(values, index, axis=0):
    first, second = lax.index_in_dim(values, 0, axis, False), lax.index_in_dim(values, 1, axis, False)
    chosen = index == 0
    return jnp.where(chosen, first, second), jnp.where(chosen, second, first)


def tie(*values):
    return lax.optimization_barrier(values)


def shift(values, step):
    columns = lax.axis_size("col")
    if step % columns == 0:
        return values
    return lax.ppermute(values, "col", [(i, (i + step) % columns) for i in range(columns)])


def add_kernel(sums, *refs):
    count = max(index for index, *_ in sums[-1:]) + 1
    results, refs = refs[-count - 2 : -2], refs[: -count - 2] + refs[-2:]
    *sources, buffer, sems = refs
    copies, rows, first = [], [], 0
    for number, (index, start, parts) in enumerate(sums):
        row = []
        for which, lead, low, high in parts:
            target = buffer.at[pl.ds(first, high - low)]
            source = sources[which].at[lead + (pl.ds(low, high - low),)]
            copies.append(pltpu.make_async_copy(source, target, sems.at[len(copies)]))
            copies[-1].start()
            row.append((first, high - low))
            first += high - low
        rows.append((index, start, row))
    for copy in copies:
        copy.wait()
    for index, start, row in rows:
        size = row[0][1]
        total = sum(buffer[first : first + size].astype(f32) for first, _ in row)
        results[index][start : start + size] = total.astype(bf16)


def add_blocks(arrays, lengths, sums):
    hbm, vmem = pl.BlockSpec(memory_space=pltpu.HBM), pl.BlockSpec(memory_space=pltpu.VMEM)
    tail = arrays[0].shape[-2:]
    parts = [part for *_, each in sums for part in each]
    return pl.pallas_call(
        lambda *refs: add_kernel(sums, *refs),
        in_specs=[hbm] * len(arrays),
        out_specs=[vmem] * len(lengths),
        out_shape=[jax.ShapeDtypeStruct((length,) + tail, bf16) for length in lengths],
        scratch_shapes=[
            pltpu.VMEM((sum(high - low for *_, low, high in parts),) + tail, bf16),
            pltpu.SemaphoreType.DMA((len(parts),)),
        ],
        compiler_params=pltpu.CompilerParams(vmem_limit_bytes=60 << 20),
        cost_estimate=cost(0.001),
        name="add_blocks",
    )(*arrays)


def sum_shards(kept, sent, mark):
    columns = kept.shape[2]
    middle = columns // 2
    pair = kept, swap(sent, "yb")
    both = lambda lead, low, high: [(0, lead, low, high), (1, lead, low, high)]
    to_dp = [(0, 0, both((1, 1), 0, middle)), (0, middle, both((0, 1), 0, middle))]
    to_ya = [(1, 0, both((1, 1), middle, columns)), (1, middle, both((1, 0), middle, columns))]
    to_dp, to_ya = add_blocks(pair, (columns, columns), to_dp + to_ya)
    mark, to_dp, to_ya = tie(mark, to_dp, to_ya)
    by_dp, by_ya = swap(to_dp, "dp"), swap(to_ya, "ya")

    def sides(mark):
        dp, ya, mark = tie(by_dp, by_ya, mark)
        rest_ya = (0, 0, both((1, 0), 0, middle) + [(2, (), 0, middle)])
        rest_dp = (1, 0, both((0, 1), middle, columns) + [(3, (), 0, middle)])
        rest_ya, rest_dp = add_blocks(pair + (dp, ya), (middle, columns - middle), [rest_ya, rest_dp])
        rest_ya, rest_dp = swap(rest_ya, "ya"), swap(rest_dp, "dp")

        def finish(mark):
            low_ya, high_dp, mark = tie(rest_ya, rest_dp, mark)
            low = both((0, 0), 0, middle) + [(2, (), middle, columns), (4, (), 0, middle)]
            high = both((0, 0), middle, columns) + [(3, (), middle, columns), (5, (), 0, columns - middle)]
            (own,) = add_blocks(pair + (dp, ya, low_ya, high_dp), (columns,), [(0, 0, low), (0, middle, high)])
            mine = lax.psum_scatter(own, "col", scatter_dimension=0, tiled=False)
            other = swap(mine, "dp")
            first = lax.axis_index("dp") == 0
            return jnp.concatenate([jnp.where(first, mine, other), jnp.where(first, other, mine)], 0).astype(f32), mark

        return mark, finish

    return mark, sides


def body(
    inputs, cotangent, lengths, source, query_weight, key_weight, value_weight, output_weight, inner_weight, outer_weight,
    first_gain, first_shift, second_gain, second_shift,
):
    micro, quarter, share = inputs.shape
    dp_count, columns = lax.axis_size("dp"), lax.axis_size("col")
    pack, own = share * columns, share // 2
    feature, count = 4 * quarter, share * micro
    width, hidden_cols = query_weight.shape[1], inner_weight.shape[1]
    lanes = -(-(2 * hidden_cols + quarter + 12) // 128) * 128
    me, m, half, z = (lax.axis_index(a) for a in ("dp", "ya", "yb", "col"))

    boundary = jnp.where(m == 0, lengths[0, 0], lengths[0, 1])
    info = jnp.stack([boundary, half, z, m, me]).astype(jnp.int32)
    slabs = 2 if dp_count == 2 else 1

    vectors = (first_gain, first_shift, second_gain, second_shift)
    anchors = spread_dp(source)
    packed = parcel(jnp.reshape(me, (1,)).astype(jnp.int32), inner_weight, outer_weight, output_weight, vectors, lanes, slabs)
    axes = ("dp",) + SHARDS if slabs == 2 else SHARDS
    everywhere = lax.all_gather(packed, axes, axis=0).reshape(slabs, 4, columns, quarter // slabs, lanes)
    anchor = source.reshape(count)
    place = anchor // (dp_count * pack) * share + anchor % share
    holder = anchor % (dp_count * pack) // pack
    wide_in = spread_dp(inputs)

    steps = jnp.arange(columns, dtype=jnp.int32)
    spots = ((z - steps) % columns * share + half * own)[:, None] + jnp.arange(own, dtype=jnp.int32)[None, :]
    frequency = 10000.0 ** (-2.0 * jnp.arange(DH // 2, dtype=f32) / DH)
    angles = (spots - jnp.where(spots >= boundary, boundary, 0)).astype(f32)[..., None] * jnp.tile(jnp.repeat(frequency, 2), 2)
    signs = jnp.where(jnp.arange(2 * DH) % 2 == 0, -1.0, 1.0)
    cosine, sine = jnp.cos(angles), jnp.sin(angles) * signs
    wide_in, cosine, sine = tie(wide_in, cosine, sine)

    if dp_count == 2:
        pick = (holder * count + place)[:, None] == jnp.arange(dp_count * count, dtype=jnp.int32)[None, :]
        pick = pick.astype(bf16).reshape(count, dp_count, micro, share)
        deal = lambda wide: jnp.einsum("tsmj,smfj->tf", pick, wide, preferred_element_type=f32).astype(bf16)
    else:
        deal = lambda wide: wide.transpose(0, 1, 3, 2).reshape(-1, quarter)[holder * count + place]

    def to_tokens(dealt):
        return lax.all_to_all(dealt.reshape(4, own, quarter), ROWS, split_axis=0, concat_axis=0, tiled=True)

    dealt = deal(wide_in)
    tokens = to_tokens(dealt).transpose(1, 0, 2).reshape(own, feature)
    cotangent, query_weight, tokens = tie(cotangent, query_weight, tokens)
    wide_cot, tokens = tie(spread_dp(cotangent), tokens)
    blocks = [shift(tokens, step) for step in range(columns)]
    cot = to_tokens(deal(wide_cot)).transpose(1, 0, 2).reshape(own, feature)
    qkv_weight = jnp.concatenate([query_weight, key_weight, value_weight], 1)
    qkv_weight = gather_rows(qkv_weight).reshape(feature, -1)

    blocks[-1], cot, anchors = tie(blocks[-1], cot, anchors)
    q, kv, turned = project(blocks, qkv_weight, cosine, sine)
    kv_twin, turned_twin = swap(kv, "yb"), swap(turned, "yb")
    mixed, lses = attend_forward(1, columns - 1, info, q, kv, kv_twin, turned, turned_twin, share)
    q, mixed = tie(q, mixed)
    last = attend_forward(0, 1, info, q, kv, kv_twin, turned, turned_twin, share)
    mixed, lses = last[0] + mixed, last[1] + lses
    attended = [shift(mixed[step], -step) for step in range(columns)]

    result, grad_att, grad_one, hidden, act, gin, gtwo, gone, sums = feed(info, attended, tokens, cot, everywhere)
    grad_att = lax.all_to_all(grad_att, "col", split_axis=0, concat_axis=0, tiled=True)
    def to_loader(*rows):
        cut = jnp.concatenate([a.astype(bf16).reshape(own, 4, quarter).transpose(1, 0, 2) for a in rows], 2)
        cut = jnp.broadcast_to(cut[None], (dp_count,) + cut.shape).reshape(dp_count * 4, own, -1)
        moved = lax.all_to_all(cut, ("dp",) + ROWS, split_axis=0, concat_axis=0, tiled=True)
        return moved.reshape(-1, len(rows) * quarter)

    spot = jnp.arange(count, dtype=jnp.int32)
    wanted = spot // share * (dp_count * pack) + me * pack + z * share + spot % share
    if dp_count == 2:
        put = (anchors.reshape(-1)[:, None] == wanted[None, :]).astype(bf16)
        settle = lambda wide: contract(wide, put, (0, 0)).astype(bf16)
    else:
        order = jnp.argsort(anchors.reshape(-1))
        spots_in = jnp.searchsorted(anchors.reshape(-1)[order], wanted)
        settle = lambda wide: wide[order[spots_in]].T
    pieces = (hidden, act, gin, gtwo, gone, sums)
    sent = weigh(True, info, attended, *pieces, lanes, slabs)
    act, sent = tie(act, sent)
    kept = weigh(False, info, attended, hidden, act, *pieces[2:], lanes, slabs)
    if slabs == 2:
        grad_att, sides = sum_shards(kept, sent, grad_att)
    else:
        flip = lambda a, index, axis: jnp.where(index == 0, a, jnp.flip(a, axis))
        cut = flip(flip(jnp.stack([kept, sent], 1), m, 0), half, 1).reshape(4 * columns, quarter, lanes)
        summed = lax.psum_scatter(cut, SHARDS, scatter_dimension=0, tiled=False)
        summed = lax.psum(summed, "dp").astype(f32)

    dq, near, far = attend_backward(info, q, kv, kv_twin, turned, turned_twin, grad_att, mixed, lses, share)
    far = swap(far, "yb")
    partial, grad_qkv = unproject(info, dq, near, far, blocks, qkv_weight, cosine, sine)
    if slabs == 2:
        grad_qkv, finish = sides(grad_qkv)
    partial = lax.all_to_all(partial, "col", split_axis=0, concat_axis=0, tiled=True)
    grad_tokens = grad_one + jnp.sum(partial.astype(f32), 0)

    def over_dp(values):
        if dp_count == 2:
            return values.astype(f32) + swap(values, "dp").astype(f32)
        return lax.psum(values, "dp").astype(f32)

    def halve(grad, axis, index, place_axis):
        kept, sent = keep(grad, index, place_axis)
        return (kept.astype(f32) + swap(sent, axis).astype(f32)).astype(bf16)

    grad_qkv = halve(grad_qkv.reshape(2, 2, quarter, 3 * width), "yb", half, 1)
    if slabs == 2:
        summed, grad_qkv = finish(grad_qkv)
    grad_qkv = over_dp(halve(grad_qkv, "ya", m, 0))
    grad_tokens, grad_qkv = tie(grad_tokens, grad_qkv)
    sum_inner, sum_outer = summed[:, :hidden_cols], summed[:, hidden_cols : 2 * hidden_cols]
    sum_output = summed[:, 2 * hidden_cols : 2 * hidden_cols + quarter]
    sum_vectors = summed[:, 2 * hidden_cols + quarter : 2 * hidden_cols + quarter + 4].T

    shape = lambda a: a.reshape(quarter, micro, share).transpose(1, 0, 2)
    settled = settle(to_loader(result, grad_tokens))
    final_out, final_grad = shape(settled[:quarter]), shape(settled[quarter:])
    return (
        final_out, final_grad, grad_qkv[:, :width], grad_qkv[:, width : 2 * width], grad_qkv[:, 2 * width :],
        sum_output, sum_inner, sum_outer, sum_vectors[0], sum_vectors[1], sum_vectors[2], sum_vectors[3],
    )


def solution(mesh):
    dp, row, col = (mesh.shape[a] for a in ("dp", "row", "col"))
    fine = Mesh(mesh.devices.reshape(dp, 2, row // 2, col), ("dp", "ya", "yb", "col"))
    tokens, matrix = P(None, ROWS, ("dp", "col")), P(ROWS, "col")
    weights = (matrix, matrix, matrix, P("col", ROWS), matrix, matrix, P(ROWS), P(ROWS), P(ROWS), P(ROWS))
    return jax.shard_map(
        body,
        mesh=fine,
        in_specs=(tokens, tokens, P("dp", None), P(None, ("dp", "col"))) + weights,
        out_specs=(tokens, tokens) + weights,
        check_vma=False,
    )
```

```python
import jax
import jax.numpy as jnp
from jax import lax
from jax.experimental import pallas as pl
from jax.experimental.pallas import tpu as pltpu
from jax.sharding import Mesh, PartitionSpec as P

DH = 64
EPSILON = 1e-05
MASKED = -1e30
LOG2E = 1.4426950408889634
SWAP = ((0, 1), (1, 0))
ROWS = ("ya", "yb")
SHARDS = ("ya", "yb", "col")
bf16 = jnp.bfloat16
f32 = jnp.float32


def cost(microseconds):
    return pl.CostEstimate(flops=int(microseconds * 1e9), bytes_accessed=int(microseconds * 3e6), transcendentals=0)


def contract(left, right, dims):
    return lax.dot_general(left, right, ((dims[:1], dims[1:]), ((), ())), preferred_element_type=f32)


def swap(values, axis):
    return lax.ppermute(values, axis, SWAP)


def gather_rows(values):
    first, second = lax.axis_index("ya") == 0, lax.axis_index("yb") == 0
    other = swap(values, "ya")
    pair = jnp.stack([jnp.where(first, values, other), jnp.where(first, other, values)])
    twin = swap(pair, "yb")
    both = jnp.stack([jnp.where(second, pair, twin), jnp.where(second, twin, pair)], 1)
    return both.reshape((4,) + values.shape)


def spread_dp(values):
    if lax.axis_size("dp") == 2:
        other = swap(values, "dp")
        first = lax.axis_index("dp") == 0
        return jnp.stack([jnp.where(first, values, other), jnp.where(first, other, values)])
    return lax.all_gather(values, "dp", axis=0)


def widen(table, lanes):
    return jnp.concatenate([table] * (lanes // table.shape[1]), 1)


def turn(values, cosine, sine):
    lanes = values.shape[1]
    even = lax.broadcasted_iota(jnp.int32, values.shape, 1) % 2 == 0
    swapped = jnp.where(even, pltpu.roll(values, lanes - 1, 1), pltpu.roll(values, 1, 1))
    return values * widen(cosine, lanes) + swapped * widen(sine, lanes)


def project_kernel(blocks, *refs):
    x_refs, (w_ref, cos_ref, sin_ref) = refs[:blocks], refs[blocks : blocks + 3]
    q_ref, kv_ref, turned_ref = refs[-3:]
    width = turned_ref.shape[1]
    for index, x_ref in enumerate(x_refs):
        wide = jnp.dot(x_ref[...], w_ref[...], preferred_element_type=f32)
        turned = turn(wide[:, : 2 * width], cos_ref[index], sin_ref[index])
        parts = turned[:, :width], turned[:, width:], wide[:, 2 * width :]
        for ref, place, part in ((q_ref, index, parts[0]), (kv_ref, index, parts[1]), (kv_ref, blocks + index, parts[2])):
            ref[place] = jnp.concatenate([part, jnp.zeros((part.shape[0], ref.shape[2] - width), f32)], 1).astype(bf16)
        turned_ref[index] = parts[1].T.astype(bf16)
        turned_ref[blocks + index] = parts[2].T.astype(bf16)


def project(blocks, weight, cosine, sine):
    own, width, count = blocks[0].shape[0], weight.shape[1] // 3, len(blocks)
    padded = -(-width // 128) * 128
    return pl.pallas_call(
        lambda *refs: project_kernel(count, *refs),
        out_shape=[
            jax.ShapeDtypeStruct((count, own, padded), bf16),
            jax.ShapeDtypeStruct((2 * count, own, padded), bf16),
            jax.ShapeDtypeStruct((2 * count, width, own), bf16),
        ],
        compiler_params=pltpu.CompilerParams(vmem_limit_bytes=60 << 20),
        cost_estimate=cost(0.001),
        name="project",
    )(*blocks, weight, cosine, sine)


def head_rows(values, head):
    rows = lax.broadcasted_iota(jnp.int32, values.shape, 0)
    return jnp.where((rows >= head * DH) & (rows < (head + 1) * DH), values, jnp.zeros_like(values))


def head_lanes(values, head):
    lanes = lax.broadcasted_iota(jnp.int32, values.shape, 1)
    return jnp.where((lanes >= head * DH) & (lanes < (head + 1) * DH), values, jnp.zeros_like(values))


def block_sides(info_ref, query_block, key_block, columns, share, own):
    boundary, half, column = info_ref[0], info_ref[1], info_ref[2]
    place = lambda block: jnp.where(column >= block, column - block, column - block + columns) * share
    low_q = place(query_block) + half * own
    low_k = place(key_block)
    first_q, second_q = low_q < boundary, low_q + own > boundary
    first_k, second_k = low_k < boundary, low_k + share > boundary
    meets = (first_q & first_k) | (second_q & second_k)
    mixed = (first_q & second_q) | (first_k & second_k)
    side_q = low_q + lax.broadcasted_iota(jnp.int32, (1, own), 1) >= boundary
    rows = lax.broadcasted_iota(jnp.int32, (share, 1), 0)
    shift = jnp.where(rows < own, half * own, (1 - half) * own - own)
    side_k = low_k + rows + shift >= boundary
    return meets, mixed, side_q.astype(f32), side_k.astype(f32)


def visit_blocks(info_ref, query_block, columns, share, own, visit):
    def step(key_block, carry):
        meets, mixed, side_q, side_k = block_sides(info_ref, query_block, key_block, columns, share, own)

        @pl.when(meets & mixed)
        def _():
            visit(key_block, side_q == side_k)

        @pl.when(meets & jnp.logical_not(mixed))
        def _():
            visit(key_block, None)

        return carry

    lax.fori_loop(0, columns, step, 0)


def forward_kernel(first, share, info_ref, q_ref, k0_ref, k1_ref, vt0_ref, vt1_ref, *refs):
    columns, own, _ = k0_ref.shape
    width = vt0_ref.shape[1]
    heads = width // DH
    count = (len(refs) - 4) // 2
    outs, lses, (parts, top, total, sums) = refs[:count], refs[count : 2 * count], refs[2 * count :]
    scaling = DH ** (-0.5) * LOG2E

    def visit(key_block, same):
        keys = jnp.concatenate([k0_ref[key_block], k1_ref[key_block]], 0)
        values = jnp.concatenate([vt0_ref[key_block], vt1_ref[key_block]], 1)
        for head in range(heads):
            rows = pl.ds(head * DH, DH)
            line = pl.ds(head, 1)
            scores = contract(keys, parts[head], (1, 1)) * scaling
            if same is not None:
                scores = jnp.where(same, scores, MASKED)
            before = top[line, :]
            highest = jnp.maximum(before, jnp.max(scores, 0, keepdims=True))
            fade = jnp.exp2(before - highest)
            raised = jnp.exp2(scores - highest)
            if same is not None:
                raised = jnp.where(same, raised, 0.0)
            top[line, :] = highest
            total[line, :] = total[line, :] * fade + jnp.sum(raised, 0, keepdims=True)
            product = jnp.dot(values[head * DH : (head + 1) * DH], raised.astype(bf16), preferred_element_type=f32)
            sums[rows, :] = sums[rows, :] * fade + product

    for index in range(count):
        for head in range(heads):
            parts[head] = head_lanes(q_ref[first + index], head)
        top[...] = jnp.full_like(top, MASKED)
        total[...] = jnp.zeros_like(total)
        sums[...] = jnp.zeros_like(sums)
        visit_blocks(info_ref, first + index, columns, share, own, visit)
        for head in range(heads):
            rows = pl.ds(head * DH, DH)
            line = pl.ds(head, 1)
            outs[index][rows, :] = (sums[rows, :] / total[line, :]).astype(bf16)
            lses[index][line, :] = top[line, :] + jnp.log2(total[line, :])


def attend_forward(first, count, info, q, kv, kv_twin, turned, turned_twin, share):
    columns, own, padded = q.shape
    width = turned.shape[1]
    heads = width // DH
    keys = pl.BlockSpec((columns, own, padded), lambda i, s: (0, 0, 0))
    values = pl.BlockSpec((columns, width, own), lambda i, s: (1, 0, 0))
    flat = lambda rows: pl.BlockSpec((rows, own), lambda i, s: (0, 0))
    outs = pl.pallas_call(
        lambda *refs: forward_kernel(first, share, *refs),
        grid_spec=pltpu.PrefetchScalarGridSpec(
            num_scalar_prefetch=1,
            grid=(1,),
            in_specs=[keys, keys, keys, values, values],
            out_specs=[flat(width)] * count + [flat(heads)] * count,
            scratch_shapes=[
                pltpu.VMEM((heads, own, padded), bf16),
                pltpu.VMEM((heads, own), f32),
                pltpu.VMEM((heads, own), f32),
                pltpu.VMEM((width, own), f32),
            ],
        ),
        out_shape=[jax.ShapeDtypeStruct((width, own), bf16)] * count + [jax.ShapeDtypeStruct((heads, own), f32)] * count,
        compiler_params=pltpu.CompilerParams(vmem_limit_bytes=60 << 20),
        cost_estimate=cost(0.001),
        name="attend_forward",
    )(info, q, kv, kv_twin, turned, turned_twin)
    return outs[:count], outs[count:]


def backward_kernel(columns, share, info_ref, q_ref, kv0_ref, kv1_ref, kt0_ref, kt1_ref, *refs):
    grads, outs, lses, refs = refs[0], refs[1 : columns + 1], refs[columns + 1 : 2 * columns + 1], refs[2 * columns + 1 :]
    dq_ref, near_ref, *fars, part_q, part_g, delta, lse, sum_q, sum_k, sum_v = refs
    own, width = q_ref.shape[1], kt0_ref.shape[1]
    heads = width // DH
    scaling = DH ** (-0.5)
    sum_k[...] = jnp.zeros_like(sum_k)
    sum_v[...] = jnp.zeros_like(sum_v)
    for block in range(columns):
        lse[block] = lses[block][...]
        column = info_ref[2] - block
        grad = grads[jnp.where(column < 0, column + columns, column)]
        spare = jnp.zeros((part_g.shape[1] - width, own), bf16)
        product = grad.astype(f32) * outs[block][...].astype(f32)
        for head in range(heads):
            part_q[block, pl.ds(head * own, own), :] = head_lanes(q_ref[block], head)
            part_g[block, :, pl.ds(head * own, own)] = jnp.concatenate([head_rows(grad, head), spare], 0)
            delta[block, pl.ds(head, 1), :] = jnp.sum(product[head * DH : (head + 1) * DH], 0, keepdims=True)

    def query_step(block, carry):
        sum_q[...] = jnp.zeros_like(sum_q)

        def visit(key_block, same):
            keys = jnp.concatenate([kv0_ref[key_block], kv1_ref[key_block]], 0)
            turned = jnp.concatenate([kt0_ref[key_block], kt1_ref[key_block]], 1)
            values = jnp.concatenate([kv0_ref[columns + key_block], kv1_ref[columns + key_block]], 0)
            all_probs, all_grads = [], []
            for head in range(heads):
                span = pl.ds(head * own, own)
                scores = contract(keys, part_q[block, span, :], (1, 1)) * (scaling * LOG2E)
                probs = jnp.exp2(scores - lse[block, pl.ds(head, 1), :])
                if same is not None:
                    probs = jnp.where(same, probs, 0.0)
                slopes = jnp.dot(values, part_g[block, :, span], preferred_element_type=f32)
                grads = (probs * (slopes - delta[block, pl.ds(head, 1), :])).astype(bf16)
                all_probs.append(probs.astype(bf16))
                all_grads.append(grads)
            for head in range(heads):
                rows = pl.ds(head * DH, DH)
                part = turned[head * DH : (head + 1) * DH]
                sum_q[rows, :] += jnp.dot(part, all_grads[head], preferred_element_type=f32)
            sum_v[key_block] += contract(jnp.concatenate(all_probs, 1), part_g[block], (1, 1))
            sum_k[key_block] += jnp.dot(jnp.concatenate(all_grads, 1), part_q[block], preferred_element_type=f32)

        visit_blocks(info_ref, block, columns, share, own, visit)
        dq_ref[block] = sum_q[...].T * scaling
        return carry

    lax.fori_loop(0, columns, query_step, 0)
    for block in range(columns):
        for place, sums, far_ref in ((block, sum_k, fars[0]), (columns + block, sum_v, fars[1])):
            near_ref[place] = sums[block, :own].astype(bf16)
            far_ref[block] = sums[block, own:].astype(bf16)


def attend_backward(info, q, kv, kv_twin, turned, turned_twin, grads, outs, lses, share):
    columns, own, padded = q.shape
    width = turned.shape[1]
    heads = width // DH
    vmem = pl.BlockSpec(memory_space=pltpu.VMEM)
    operands = [q, kv, kv_twin, turned, turned_twin, grads, *outs, *lses]
    return pl.pallas_call(
        lambda *refs: backward_kernel(columns, share, *refs),
        in_specs=[pl.BlockSpec(memory_space=pltpu.SMEM)] + [vmem] * len(operands),
        out_specs=[vmem] * 4,
        out_shape=[jax.ShapeDtypeStruct((columns, own, width), f32)]
        + [jax.ShapeDtypeStruct((many, own, padded), bf16) for many in (2 * columns, columns, columns)],
        scratch_shapes=[
            pltpu.VMEM((columns, heads * own, padded), bf16),
            pltpu.VMEM((columns, padded, heads * own), bf16),
            pltpu.VMEM((columns, heads, own), f32),
            pltpu.VMEM((columns, heads, own), f32),
            pltpu.VMEM((width, own), f32),
            pltpu.VMEM((columns, share, padded), f32),
            pltpu.VMEM((columns, share, padded), f32),
        ],
        compiler_params=pltpu.CompilerParams(vmem_limit_bytes=60 << 20),
        cost_estimate=cost(0.001),
        name="attend_backward",
    )(info, *operands)


def unproject_kernel(info_ref, dq_ref, near_k_ref, far_k_ref, near_v_ref, far_v_ref, w_ref, cos_ref, sin_ref, part_ref, low_ref):
    width = dq_ref.shape[2]
    lanes = 2 * width
    even = lax.broadcasted_iota(jnp.int32, (dq_ref.shape[1], lanes), 1) % 2 == 0
    dk = (near_k_ref[0, :, :width].astype(f32) + far_k_ref[0, :, :width].astype(f32)) * DH ** (-0.5)
    dv = near_v_ref[0, :, :width].astype(f32) + far_v_ref[0, :, :width].astype(f32)
    both = jnp.concatenate([dq_ref[0], dk], 1)
    swapped = jnp.where(even, pltpu.roll(both, lanes - 1, 1), pltpu.roll(both, 1, 1))
    both = both * widen(cos_ref[0], lanes) - swapped * widen(sin_ref[0], lanes)
    low = jnp.concatenate([both, dv], 1).astype(bf16)
    low_ref[0] = low
    part_ref[0] = contract(low, w_ref[...], (1, 1)).astype(bf16)


def unproject(info, dq, near, far_k, far_v, weight, cosine, sine):
    columns, own, width = dq.shape
    feature = weight.shape[0]
    block = lambda a, first: pl.BlockSpec((1,) + a.shape[1:], lambda i, s: (first + i, 0, 0))
    whole = lambda a: pl.BlockSpec(a.shape, lambda i, s: (0, 0))
    place = lambda i, s: (jnp.where(s[2] >= i, s[2] - i, s[2] - i + columns), 0, 0)
    low = jax.ShapeDtypeStruct((columns, own, weight.shape[1]), bf16)
    return pl.pallas_call(
        unproject_kernel,
        grid_spec=pltpu.PrefetchScalarGridSpec(
            num_scalar_prefetch=1,
            grid=(columns,),
            in_specs=[block(dq, 0), block(near, 0), block(far_k, 0), block(near, columns), block(far_v, 0), whole(weight)]
            + [block(cosine, 0), block(sine, 0)],
            out_specs=[pl.BlockSpec((1, own, feature), place), block(low, 0)],
        ),
        out_shape=[jax.ShapeDtypeStruct((columns, own, feature), bf16), low],
        compiler_params=pltpu.CompilerParams(vmem_limit_bytes=60 << 20),
        cost_estimate=cost(0.001),
        name="unproject",
    )(info, dq, near, far_k, near, far_v, weight, cosine, sine)


def project_grad_kernel(low_ref, *refs):
    x_refs, (grad_ref,) = refs[:-1], refs[-1:]
    total = None
    for block, x_ref in enumerate(x_refs):
        piece = contract(x_ref[...], low_ref[block], (0, 0))
        total = piece if total is None else total + piece
    grad_ref[...] = total.astype(bf16)


def project_grad(low, blocks):
    return pl.pallas_call(
        project_grad_kernel,
        out_shape=jax.ShapeDtypeStruct((blocks[0].shape[1], low.shape[2]), bf16),
        compiler_params=pltpu.CompilerParams(vmem_limit_bytes=60 << 20),
        cost_estimate=cost(0.001),
        name="project_grad",
    )(low, *blocks)


def mean_lanes(values):
    return jnp.sum(values, 1, keepdims=True) * (1.0 / values.shape[1])


def norm_forward(values, gain, shift):
    centred = values - mean_lanes(values)
    inverse = lax.rsqrt(mean_lanes(centred * centred) + EPSILON)
    normed = centred * inverse
    return normed * gain + shift, normed, inverse


def norm_backward(grad, normed, inverse, gain):
    scaled = grad * gain
    return inverse * (scaled - mean_lanes(scaled) - normed * mean_lanes(scaled * normed))


def unit(size):
    rows = lax.broadcasted_iota(jnp.int32, (size, size), 0)
    return (rows == lax.broadcasted_iota(jnp.int32, (size, size), 1)).astype(bf16)


def feed_kernel(info_ref, x_ref, cot_ref, w_ref, *refs):
    parts, _, columns, slab, _ = w_ref.shape
    att_refs, refs = refs[:columns], refs[columns:]
    result_ref, grad_att_ref, *refs = refs
    grad_one_ref, hidden_ref, act_ref, gin_ref, gtwo_ref, gone_ref, sums_ref, w, slopes, outer, sems = refs
    rows, columns, quarter, _ = w.shape

    def turned(step):
        column = info_ref[2] + step
        return jnp.where(column >= columns, column - columns, column)

    hidden_cols = act_ref.shape[2]
    both = 2 * hidden_cols
    spans = ((0, hidden_cols), (hidden_cols, hidden_cols), (both, w.shape[3] - both))

    def copies(kind):
        lanes = pl.ds(*spans[kind])
        for part in range(parts):
            target = w.at[:, :, pl.ds(part * slab, slab), lanes]
            yield pltpu.make_async_copy(w_ref.at[part, :, :, :, lanes], target, sems.at[kind, part])

    def wait(kind):
        for each in copies(kind):
            each.wait()

    for kind in (2, 0, 1):
        for each in copies(kind):
            each.start()

    def block(kind, column):
        lanes = pl.ds(*spans[kind])
        return jnp.concatenate([w[row, column, :, lanes] for row in range(rows)], 0)

    wait(2)
    mix = pl.ds(both, quarter)
    attended = jnp.concatenate([ref[...] for ref in att_refs], 0)
    branch = []
    for row in range(rows):
        weight = jnp.concatenate([w[row, turned(step), :, mix] for step in range(columns)], 0)
        branch.append(contract(attended, weight, (0, 0)))
    branch = jnp.concatenate(branch, 1)
    eye = unit(quarter)
    small = [contract(w[row, 0, :, pl.ds(both + quarter, 12)], eye, (0, 0)) for row in range(rows)]
    small = jnp.concatenate(small, 1)
    vectors = small[0:4] + (small[4:8] + small[8:12])
    gain_one, shift_one, gain_two, shift_two = (vectors[i : i + 1] for i in range(4))

    hidden, normed_one, inverse_one = norm_forward(x_ref[...].astype(f32) + branch, gain_one, shift_one)
    low = hidden.astype(bf16)
    hidden_ref[...] = low.T
    outer[...] = jnp.zeros_like(outer)

    wait(0)

    def forward(column, carry):
        inner = jnp.dot(low, block(0, column), preferred_element_type=f32)
        cumulative = 0.5 * (1.0 + lax.erf(inner * (0.5**0.5)))
        slopes[column] = cumulative + inner * (jnp.exp(-0.5 * inner * inner) * 0.3989422804014327)
        act_ref[column] = (inner * cumulative).astype(bf16)
        return carry

    lax.fori_loop(0, columns, forward, 0)
    wait(1)

    def combine(column, carry):
        outer[...] += contract(act_ref[column], block(1, column), (1, 1))
        return carry

    lax.fori_loop(0, columns, combine, 0)
    result, normed_two, inverse_two = norm_forward(hidden + outer[...], gain_two, shift_two)
    result_ref[...] = result.astype(bf16)
    cot = cot_ref[...].astype(f32)
    grad_two = norm_backward(cot, normed_two, inverse_two, gain_two)
    grad_two_low = grad_two.astype(bf16)
    gtwo_ref[...] = grad_two_low.T
    outer[...] = grad_two

    def backward(column, carry):
        grad = jnp.dot(grad_two_low, block(1, column), preferred_element_type=f32)
        gin_ref[column] = (grad * slopes[column]).astype(bf16)
        outer[...] += contract(gin_ref[column], block(0, column), (1, 1))
        return carry

    lax.fori_loop(0, columns, backward, 0)
    grad_hidden = outer[...]
    grad_one = norm_backward(grad_hidden, normed_one, inverse_one, gain_one)
    grad_one_ref[...] = grad_one
    grad_one_low = grad_one.astype(bf16)
    for step in range(columns):
        weight = jnp.concatenate([w[row, turned(step), :, mix] for row in range(rows)], 1)
        grad_att_ref[turned(step)] = contract(weight, grad_one_low, (1, 1)).astype(bf16)
    sums = [jnp.sum(a, 0, keepdims=True) for a in (grad_hidden * normed_one, grad_hidden, cot * normed_two, cot)]
    sums = jnp.concatenate(sums, 0)
    for row in range(rows):
        mine = slice(row * quarter, (row + 1) * quarter)
        gone_ref[row] = grad_one_low[:, mine]
        sums_ref[row] = sums[:, mine].astype(bf16)


def feed(info, attended, tokens, cot, weights):
    own, feature = tokens.shape
    parts, rows, columns, slab, lanes = weights.shape
    quarter = parts * slab
    hidden_cols = feature
    vmem, smem = pl.BlockSpec(memory_space=pltpu.VMEM), pl.BlockSpec(memory_space=pltpu.SMEM)
    wide = jax.ShapeDtypeStruct((columns, own, hidden_cols), bf16)
    flat = lambda kind: jax.ShapeDtypeStruct((own, feature), kind)
    tall = jax.ShapeDtypeStruct((feature, own), bf16)
    return pl.pallas_call(
        feed_kernel,
        in_specs=[smem, vmem, vmem, pl.BlockSpec(memory_space=pltpu.HBM)] + [vmem] * columns,
        out_specs=[vmem] * 9,
        out_shape=[
            flat(bf16), jax.ShapeDtypeStruct((columns, quarter, own), bf16), flat(f32), tall, wide, wide, tall,
            jax.ShapeDtypeStruct((rows, own, quarter), bf16), jax.ShapeDtypeStruct((rows, 4, quarter), bf16),
        ],
        scratch_shapes=[
            pltpu.VMEM((rows, columns, quarter, lanes), bf16),
            pltpu.VMEM((columns, own, hidden_cols), f32),
            pltpu.VMEM((own, feature), f32),
            pltpu.SemaphoreType.DMA((3, parts)),
        ],
        compiler_params=pltpu.CompilerParams(vmem_limit_bytes=60 << 20),
        cost_estimate=cost(0.001),
        name="feed",
    )(info, tokens, cot, weights, *attended)


def weigh_kernel(twin, info_ref, hidden_ref, act_ref, gin_ref, gtwo_ref, gone_ref, sums_ref, *refs):
    att_refs, out_ref = refs[:-1], refs[-1]
    _, slabs, _, slab, lanes = out_ref.shape
    quarter = slabs * slab
    hidden_cols = act_ref.shape[2]
    columns = len(att_refs)
    step = pl.program_id(0) - info_ref[2]
    step = jnp.where(step < 0, step + columns, step)
    attended = att_refs[0][...]
    for index in range(1, columns):
        attended = jnp.where(step == index, att_refs[index][...], attended)
    core = 1 - info_ref[1] if twin else info_ref[1]
    eye = unit(quarter)
    away = lambda index, mine: jnp.where(index == mine, 0, 1)
    for pair in range(2):
        row = 2 * pair + core
        mine = pl.ds(pl.multiple_of(row * quarter, quarter), quarter)
        inner = jnp.dot(hidden_ref[mine, :], gin_ref[0], preferred_element_type=f32).astype(bf16)
        outer = jnp.dot(gtwo_ref[mine, :], act_ref[0], preferred_element_type=f32).astype(bf16)
        mixed = jnp.dot(attended, gone_ref[row], preferred_element_type=f32).astype(bf16)
        vector = contract(eye, sums_ref[row], (1, 1)).astype(bf16)
        rest = jnp.zeros((quarter, lanes - 2 * hidden_cols - quarter - 4), bf16)
        tail = jnp.concatenate([mixed, vector, rest], 1)
        far = away(pair, info_ref[3])
        for part in range(slabs):
            place = away(part, info_ref[4]) if slabs > 1 else 0
            rows = slice(part * slab, (part + 1) * slab)
            out_ref[far, place, 0, :, 0:hidden_cols] = inner[rows]
            out_ref[far, place, 0, :, hidden_cols : 2 * hidden_cols] = outer[rows]
            out_ref[far, place, 0, :, 2 * hidden_cols :] = tail[rows]


def weigh(twin, info, attended, hidden, act, gin, gtwo, gone, sums, lanes, slabs):
    columns = act.shape[0]
    quarter = attended[0].shape[0]
    whole = lambda a: pl.BlockSpec(a.shape, lambda i, s: (0,) * a.ndim)
    piece = pl.BlockSpec((1,) + act.shape[1:], lambda i, s: (i, 0, 0))
    slab = quarter // slabs
    return pl.pallas_call(
        lambda *refs: weigh_kernel(twin, *refs),
        grid_spec=pltpu.PrefetchScalarGridSpec(
            num_scalar_prefetch=1,
            grid=(columns,),
            in_specs=[whole(hidden), piece, piece, whole(gtwo), whole(gone), whole(sums)] + [whole(a) for a in attended],
            out_specs=pl.BlockSpec((2, slabs, 1, slab, lanes), lambda i, s: (0, 0, i, 0, 0)),
        ),
        out_shape=jax.ShapeDtypeStruct((2, slabs, columns, slab, lanes), bf16),
        compiler_params=pltpu.CompilerParams(vmem_limit_bytes=60 << 20),
        cost_estimate=cost(0.001),
        name="weigh",
    )(info, hidden, act, gin, gtwo, gone, sums, *attended)


def parcel_kernel(info_ref, inner_ref, outer_ref, output_ref, *refs):
    small_refs, out_ref = refs[:-1], refs[-1]
    columns = inner_ref.shape[1]
    quarter = output_ref.shape[1]
    slab = out_ref.shape[0]
    offset = info_ref[0] * slab if slab < quarter else 0
    rows = pl.ds(pl.multiple_of(offset, slab), slab)
    values = jnp.concatenate([ref[...] for ref in small_refs], 0)
    high = values.astype(bf16)
    rest = values - high.astype(f32)
    middle = rest.astype(bf16)
    last = (rest - middle.astype(f32)).astype(bf16)
    pick = lax.broadcasted_iota(jnp.int32, (slab, quarter), 0) + offset
    pick = (pick == lax.broadcasted_iota(jnp.int32, (slab, quarter), 1)).astype(bf16)
    small = jnp.concatenate([contract(pick, part, (1, 1)) for part in (high, middle, last)], 1).astype(bf16)
    fill = jnp.zeros((slab, out_ref.shape[1] - 2 * columns - quarter - 12), bf16)
    out_ref[:, 0:columns] = inner_ref[rows, :]
    out_ref[:, columns : 2 * columns] = outer_ref[rows, :]
    out_ref[:, 2 * columns :] = jnp.concatenate([output_ref[rows, :], small, fill], 1)


def parcel(part, inner, outer, output, vectors, lanes, slabs):
    vmem, smem = pl.BlockSpec(memory_space=pltpu.VMEM), pl.BlockSpec(memory_space=pltpu.SMEM)
    return pl.pallas_call(
        parcel_kernel,
        in_specs=[smem] + [vmem] * 7,
        out_shape=jax.ShapeDtypeStruct((inner.shape[0] // slabs, lanes), bf16),
        cost_estimate=cost(0.001),
        name="parcel",
    )(part, inner, outer, output, *(v.reshape(1, -1) for v in vectors))


def keep(values, index, axis=0):
    first, second = lax.index_in_dim(values, 0, axis, False), lax.index_in_dim(values, 1, axis, False)
    chosen = index == 0
    return jnp.where(chosen, first, second), jnp.where(chosen, second, first)


def tie(*values):
    return lax.optimization_barrier(values)


def shift(values, step):
    columns = lax.axis_size("col")
    if step % columns == 0:
        return values
    return lax.ppermute(values, "col", [(i, (i + step) % columns) for i in range(columns)])


def add_kernel(count, sums, *refs):
    results, (*sources, buffer, held, sems, ends) = refs[-count - 4 : -4], refs[: -count - 4] + refs[-4:]
    rows, first, number = [], 0, 0
    for index, start, parts in sums:
        row = []
        for which, lead, low, high in parts:
            source = sources[which].at[lead + (pl.ds(low, high - low),)]
            copy = pltpu.make_async_copy(source, buffer.at[pl.ds(first, high - low)], sems.at[number])
            copy.start()
            row.append((first, high - low, copy))
            first, number = first + high - low, number + 1
        rows.append(row)
    copies, first = [], 0
    for place, ((index, start, _), row) in enumerate(zip(sums, rows)):
        size = row[0][1]
        for *_, copy in row:
            copy.wait()
        total = sum(buffer[at : at + size].astype(f32) for at, *_ in row)
        held[first : first + size] = total.astype(bf16)
        target = results[index].at[pl.ds(start, size)]
        copies.append(pltpu.make_async_copy(held.at[pl.ds(first, size)], target, ends.at[place]))
        copies[-1].start()
        first += size
    for copy in copies:
        copy.wait()


def add_blocks(arrays, lengths, sums):
    hbm = pl.BlockSpec(memory_space=pltpu.HBM)
    tail = arrays[0].shape[-2:]
    parts = [part for *_, each in sums for part in each]
    return pl.pallas_call(
        lambda *refs: add_kernel(len(lengths), sums, *refs),
        in_specs=[hbm] * len(arrays),
        out_specs=[hbm] * len(lengths),
        out_shape=[jax.ShapeDtypeStruct((length,) + tail, bf16) for length in lengths],
        scratch_shapes=[
            pltpu.VMEM((sum(high - low for *_, low, high in parts),) + tail, bf16),
            pltpu.VMEM((sum(lengths),) + tail, bf16),
            pltpu.SemaphoreType.DMA((len(parts),)),
            pltpu.SemaphoreType.DMA((len(sums),)),
        ],
        compiler_params=pltpu.CompilerParams(vmem_limit_bytes=60 << 20),
        cost_estimate=cost(0.001),
        name="add_blocks",
    )(*arrays)


def open_kernel(swapped_ref, mine_ref, other_ref, *outs):
    slab = mine_ref.shape[0]
    hidden_cols, quarter = outs[0].shape[1], outs[2].shape[1]
    spans = (0, hidden_cols), (hidden_cols, hidden_cols), (2 * hidden_cols, quarter)

    def write(first, second):
        for (start, size), out in zip(spans, outs):
            out[0:slab, :] = first[:, start : start + size].astype(f32)
            out[slab : 2 * slab, :] = second[:, start : start + size].astype(f32)
        last = jnp.concatenate([first[:, 2 * hidden_cols + quarter :], second[:, 2 * hidden_cols + quarter :]], 0)
        outs[3][...] = contract(last[:, 0:4], unit(2 * slab), (0, 0))

    @pl.when(swapped_ref[0] == 0)
    def _():
        write(mine_ref[...], other_ref[...])

    @pl.when(swapped_ref[0] != 0)
    def _():
        write(other_ref[...], mine_ref[...])


def open_shards(part, mine, other, hidden_cols, quarter):
    vmem, smem = pl.BlockSpec(memory_space=pltpu.VMEM), pl.BlockSpec(memory_space=pltpu.SMEM)
    lanes = hidden_cols, hidden_cols, quarter
    return pl.pallas_call(
        open_kernel,
        in_specs=[smem, vmem, vmem],
        out_shape=[jax.ShapeDtypeStruct((quarter, a), f32) for a in lanes] + [jax.ShapeDtypeStruct((4, quarter), f32)],
        compiler_params=pltpu.CompilerParams(vmem_limit_bytes=16 << 20),
        cost_estimate=cost(0.001),
        name="open_shards",
    )(part, mine, other)


def sum_shards(kept, sent, mark):
    columns = kept.shape[2]
    middle = columns // 2
    pair = kept, swap(sent, "yb")
    both = lambda lead, low, high: [(0, lead, low, high), (1, lead, low, high)]
    to_dp = [(0, 0, both((1, 1), 0, middle)), (0, middle, both((0, 1), 0, middle))]
    to_ya = [(1, 0, both((1, 1), middle, columns)), (1, middle, both((1, 0), middle, columns))]
    to_dp, to_ya = add_blocks(pair, (columns, columns), to_dp + to_ya)
    mark, to_dp, to_ya = tie(mark, to_dp, to_ya)
    by_dp, by_ya = swap(to_dp, "dp"), swap(to_ya, "ya")

    def sides(mark):
        dp, ya, mark = tie(by_dp, by_ya, mark)
        rest_ya = (0, 0, both((1, 0), 0, middle) + [(2, (), 0, middle)])
        rest_dp = (1, 0, both((0, 1), middle, columns) + [(3, (), 0, middle)])
        rest_ya, rest_dp = add_blocks(pair + (dp, ya), (middle, columns - middle), [rest_ya, rest_dp])
        mark, rest_ya, rest_dp = tie(mark, rest_ya, rest_dp)
        rest_ya, rest_dp = swap(rest_ya, "ya"), swap(rest_dp, "dp")

        def finish(mark):
            low_ya, high_dp, mark = tie(rest_ya, rest_dp, mark)
            low = both((0, 0), 0, middle) + [(2, (), middle, columns), (4, (), 0, middle)]
            high = both((0, 0), middle, columns) + [(3, (), middle, columns), (5, (), 0, columns - middle)]
            (own,) = add_blocks(pair + (dp, ya, low_ya, high_dp), (columns,), [(0, 0, low), (0, middle, high)])
            own, mark = tie(own, mark)
            mine = lax.psum_scatter(own, "col", scatter_dimension=0, tiled=False)
            other = swap(mine, "dp")
            return (mine, other), mark

        return mark, finish

    return mark, sides


def body(
    inputs, cotangent, lengths, source, query_weight, key_weight, value_weight, output_weight, inner_weight, outer_weight,
    first_gain, first_shift, second_gain, second_shift,
):
    micro, quarter, share = inputs.shape
    dp_count, columns = lax.axis_size("dp"), lax.axis_size("col")
    pack, own = share * columns, share // 2
    feature, count = 4 * quarter, share * micro
    width, hidden_cols = query_weight.shape[1], inner_weight.shape[1]
    lanes = -(-(2 * hidden_cols + quarter + 12) // 128) * 128
    me, m, half, z = (lax.axis_index(a) for a in ("dp", "ya", "yb", "col"))

    boundary = jnp.where(m == 0, lengths[0, 0], lengths[0, 1])
    info = jnp.stack([boundary, half, z, m, me]).astype(jnp.int32)
    slabs = 2 if dp_count == 2 else 1

    vectors = (first_gain, first_shift, second_gain, second_shift)
    anchors = spread_dp(source)
    packed = parcel(jnp.reshape(me, (1,)).astype(jnp.int32), inner_weight, outer_weight, output_weight, vectors, lanes, slabs)
    axes = ("dp",) + SHARDS if slabs == 2 else SHARDS
    everywhere = lax.all_gather(packed, axes, axis=0).reshape(slabs, 4, columns, quarter // slabs, lanes)
    anchor = source.reshape(count)
    place = anchor // (dp_count * pack) * share + anchor % share
    holder = anchor % (dp_count * pack) // pack
    wide_in = spread_dp(inputs)

    steps = jnp.arange(columns, dtype=jnp.int32)
    spots = ((z - steps) % columns * share + half * own)[:, None] + jnp.arange(own, dtype=jnp.int32)[None, :]
    frequency = 10000.0 ** (-2.0 * jnp.arange(DH // 2, dtype=f32) / DH)
    angles = (spots - jnp.where(spots >= boundary, boundary, 0)).astype(f32)[..., None] * jnp.tile(jnp.repeat(frequency, 2), 2)
    signs = jnp.where(jnp.arange(2 * DH) % 2 == 0, -1.0, 1.0)
    cosine, sine = jnp.cos(angles), jnp.sin(angles) * signs
    wide_in, cosine, sine = tie(wide_in, cosine, sine)

    if dp_count == 2:
        pick = (holder * count + place)[:, None] == jnp.arange(dp_count * count, dtype=jnp.int32)[None, :]
        pick = pick.astype(bf16).reshape(count, dp_count, micro, share)
        deal = lambda wide: jnp.einsum("tsmj,smfj->tf", pick, wide, preferred_element_type=f32).astype(bf16)
    else:
        deal = lambda wide: wide.transpose(0, 1, 3, 2).reshape(-1, quarter)[holder * count + place]

    def to_tokens(dealt):
        return lax.all_to_all(dealt.reshape(4, own, quarter), ROWS, split_axis=0, concat_axis=0, tiled=True)

    dealt = deal(wide_in)
    cotangent, query_weight, dealt = tie(cotangent, query_weight, dealt)
    tokens = to_tokens(dealt).transpose(1, 0, 2).reshape(own, feature)
    wide_cot, tokens = tie(spread_dp(cotangent), tokens)
    blocks = [shift(tokens, step) for step in range(columns)]
    cot = to_tokens(deal(wide_cot)).transpose(1, 0, 2).reshape(own, feature)
    qkv_weight = jnp.concatenate([query_weight, key_weight, value_weight], 1)
    qkv_weight = gather_rows(qkv_weight).reshape(feature, -1)

    blocks[-1], cot, anchors = tie(blocks[-1], cot, anchors)
    q, kv, turned = project(blocks, qkv_weight, cosine, sine)
    kv_twin, turned_twin = swap(kv, "yb"), swap(turned, "yb")
    mixed, lses = attend_forward(1, columns - 1, info, q, kv, kv_twin, turned, turned_twin, share)
    q, mixed = tie(q, mixed)
    last = attend_forward(0, 1, info, q, kv, kv_twin, turned, turned_twin, share)
    mixed, lses = last[0] + mixed, last[1] + lses
    attended = [shift(mixed[step], -step) for step in range(columns)]

    result, grad_att, grad_one, hidden, act, gin, gtwo, gone, sums = feed(info, attended, tokens, cot, everywhere)
    grad_att = lax.all_to_all(grad_att, "col", split_axis=0, concat_axis=0, tiled=True)
    def to_loader(*rows):
        cut = jnp.concatenate([a.astype(bf16).reshape(own, 4, quarter).transpose(1, 0, 2) for a in rows], 2)
        cut = jnp.broadcast_to(cut[None], (dp_count,) + cut.shape).reshape(dp_count * 4, own, -1)
        moved = lax.all_to_all(cut, ("dp",) + ROWS, split_axis=0, concat_axis=0, tiled=True)
        return moved.reshape(-1, len(rows) * quarter)

    spot = jnp.arange(count, dtype=jnp.int32)
    wanted = spot // share * (dp_count * pack) + me * pack + z * share + spot % share
    if dp_count == 2:
        put = (anchors.reshape(-1)[:, None] == wanted[None, :]).astype(bf16)
        settle = lambda wide: contract(wide, put, (0, 0)).astype(bf16)
    else:
        order = jnp.argsort(anchors.reshape(-1))
        spots_in = jnp.searchsorted(anchors.reshape(-1)[order], wanted)
        settle = lambda wide: wide[order[spots_in]].T
    pieces = (hidden, act, gin, gtwo, gone, sums)
    sent = weigh(True, info, attended, *pieces, lanes, slabs)
    act, sent = tie(act, sent)
    kept = weigh(False, info, attended, hidden, act, *pieces[2:], lanes, slabs)
    if slabs == 2:
        grad_att, sides = sum_shards(kept, sent, grad_att)
    else:
        flip = lambda a, index, axis: jnp.where(index == 0, a, jnp.flip(a, axis))
        cut = flip(flip(jnp.stack([kept, sent], 1), m, 0), half, 1).reshape(4 * columns, quarter, lanes)
        summed = lax.psum_scatter(cut, SHARDS, scatter_dimension=0, tiled=False)
        summed = lax.psum(summed, "dp").astype(f32)

    dq, near, *far = attend_backward(info, q, kv, kv_twin, turned, turned_twin, grad_att, mixed, lses, share)
    partial, low = unproject(info, dq, near, *(swap(each, "yb") for each in far), qkv_weight, cosine, sine)
    if slabs == 2:
        low, finish = sides(low)
    grad_qkv = project_grad(low, blocks)
    partial = lax.all_to_all(partial, "col", split_axis=0, concat_axis=0, tiled=True)
    grad_tokens = grad_one + jnp.sum(partial.astype(f32), 0)

    def over_dp(values):
        if dp_count == 2:
            return values.astype(f32) + swap(values, "dp").astype(f32)
        return lax.psum(values, "dp").astype(f32)

    def halve(grad, axis, index, place_axis):
        kept, sent = keep(grad, index, place_axis)
        return (kept.astype(f32) + swap(sent, axis).astype(f32)).astype(bf16)

    if slabs == 2:
        summed, grad_qkv = finish(grad_qkv)
    grad_qkv = halve(grad_qkv.reshape(2, 2, quarter, 3 * width), "yb", half, 1)
    grad_qkv = halve(grad_qkv, "ya", m, 0)
    grad_tokens, grad_qkv = tie(grad_tokens, grad_qkv)
    if slabs == 1:
        grad_qkv = over_dp(grad_qkv)
        sum_inner, sum_outer = summed[:, :hidden_cols], summed[:, hidden_cols : 2 * hidden_cols]
        sum_output = summed[:, 2 * hidden_cols : 2 * hidden_cols + quarter]
        sum_vectors = summed[:, 2 * hidden_cols + quarter : 2 * hidden_cols + quarter + 4].T

    shape = lambda a: a.reshape(quarter, micro, share).transpose(1, 0, 2)
    moved = to_loader(result, grad_tokens)
    if slabs == 2:
        (mine, other), (moved, mine, grad_qkv) = summed, tie(moved, summed[0], grad_qkv)
        grad_qkv = over_dp(grad_qkv)
        part = jnp.reshape(me, (1,)).astype(jnp.int32)
        sum_inner, sum_outer, sum_output, sum_vectors = open_shards(part, mine, other, hidden_cols, quarter)
    settled = settle(moved)
    final_out, final_grad = shape(settled[:quarter]), shape(settled[quarter:])
    return (
        final_out, final_grad, grad_qkv[:, :width], grad_qkv[:, width : 2 * width], grad_qkv[:, 2 * width :],
        sum_output, sum_inner, sum_outer, sum_vectors[0], sum_vectors[1], sum_vectors[2], sum_vectors[3],
    )


def solution(mesh):
    dp, row, col = (mesh.shape[a] for a in ("dp", "row", "col"))
    fine = Mesh(mesh.devices.reshape(dp, 2, row // 2, col), ("dp", "ya", "yb", "col"))
    tokens, matrix = P(None, ROWS, ("dp", "col")), P(ROWS, "col")
    weights = (matrix, matrix, matrix, P("col", ROWS), matrix, matrix, P(ROWS), P(ROWS), P(ROWS), P(ROWS))
    return jax.shard_map(
        body,
        mesh=fine,
        in_specs=(tokens, tokens, P("dp", None), P(None, ("dp", "col"))) + weights,
        out_specs=(tokens, tokens) + weights,
        check_vma=False,
    )
```

```python
import jax
import jax.numpy as jnp
from jax import lax
from jax.experimental import pallas as pl
from jax.experimental.pallas import tpu as pltpu
from jax.sharding import Mesh, PartitionSpec as P

DH = 64
EPSILON = 1e-05
MASKED = -1e30
LOG2E = 1.4426950408889634
SWAP = ((0, 1), (1, 0))
ROWS = ("ya", "yb")
SHARDS = ("ya", "yb", "col")
bf16 = jnp.bfloat16
f32 = jnp.float32


def cost(microseconds):
    return pl.CostEstimate(flops=int(microseconds * 1e9), bytes_accessed=int(microseconds * 3e6), transcendentals=0)


def contract(left, right, dims):
    return lax.dot_general(left, right, ((dims[:1], dims[1:]), ((), ())), preferred_element_type=f32)


def swap(values, axis):
    return lax.ppermute(values, axis, SWAP)


def gather_rows(values):
    first, second = lax.axis_index("ya") == 0, lax.axis_index("yb") == 0
    other = swap(values, "ya")
    pair = jnp.stack([jnp.where(first, values, other), jnp.where(first, other, values)])
    twin = swap(pair, "yb")
    both = jnp.stack([jnp.where(second, pair, twin), jnp.where(second, twin, pair)], 1)
    return both.reshape((4,) + values.shape)


def spread_dp(values):
    if lax.axis_size("dp") == 2:
        other = swap(values, "dp")
        first = lax.axis_index("dp") == 0
        return jnp.stack([jnp.where(first, values, other), jnp.where(first, other, values)])
    return lax.all_gather(values, "dp", axis=0)


def widen(table, lanes):
    return jnp.concatenate([table] * (lanes // table.shape[1]), 1)


def turn(values, cosine, sine):
    lanes = values.shape[1]
    even = lax.broadcasted_iota(jnp.int32, values.shape, 1) % 2 == 0
    swapped = jnp.where(even, pltpu.roll(values, lanes - 1, 1), pltpu.roll(values, 1, 1))
    return values * widen(cosine, lanes) + swapped * widen(sine, lanes)


def project_kernel(blocks, *refs):
    x_refs, (w_ref, cos_ref, sin_ref) = refs[:blocks], refs[blocks : blocks + 3]
    q_ref, kv_ref, turned_ref = refs[-3:]
    width = turned_ref.shape[1]
    for index, x_ref in enumerate(x_refs):
        wide = jnp.dot(x_ref[...], w_ref[...], preferred_element_type=f32)
        turned = turn(wide[:, : 2 * width], cos_ref[index], sin_ref[index])
        parts = turned[:, :width], turned[:, width:], wide[:, 2 * width :]
        for ref, place, part in ((q_ref, index, parts[0]), (kv_ref, index, parts[1]), (kv_ref, blocks + index, parts[2])):
            ref[place] = jnp.concatenate([part, jnp.zeros((part.shape[0], ref.shape[2] - width), f32)], 1).astype(bf16)
        turned_ref[index] = parts[1].T.astype(bf16)
        turned_ref[blocks + index] = parts[2].T.astype(bf16)


def project(blocks, weight, cosine, sine):
    own, width, count = blocks[0].shape[0], weight.shape[1] // 3, len(blocks)
    padded = -(-width // 128) * 128
    return pl.pallas_call(
        lambda *refs: project_kernel(count, *refs),
        out_shape=[
            jax.ShapeDtypeStruct((count, own, padded), bf16),
            jax.ShapeDtypeStruct((2 * count, own, padded), bf16),
            jax.ShapeDtypeStruct((2 * count, width, own), bf16),
        ],
        compiler_params=pltpu.CompilerParams(vmem_limit_bytes=60 << 20),
        cost_estimate=cost(0.001),
        name="project",
    )(*blocks, weight, cosine, sine)


def head_rows(values, head):
    rows = lax.broadcasted_iota(jnp.int32, values.shape, 0)
    return jnp.where((rows >= head * DH) & (rows < (head + 1) * DH), values, jnp.zeros_like(values))


def head_lanes(values, head):
    lanes = lax.broadcasted_iota(jnp.int32, values.shape, 1)
    return jnp.where((lanes >= head * DH) & (lanes < (head + 1) * DH), values, jnp.zeros_like(values))


def block_sides(info_ref, query_block, key_block, columns, share, own):
    boundary, half, column = info_ref[0], info_ref[1], info_ref[2]
    place = lambda block: jnp.where(column >= block, column - block, column - block + columns) * share
    low_q = place(query_block) + half * own
    low_k = place(key_block)
    first_q, second_q = low_q < boundary, low_q + own > boundary
    first_k, second_k = low_k < boundary, low_k + share > boundary
    meets = (first_q & first_k) | (second_q & second_k)
    mixed = (first_q & second_q) | (first_k & second_k)
    side_q = low_q + lax.broadcasted_iota(jnp.int32, (1, own), 1) >= boundary
    rows = lax.broadcasted_iota(jnp.int32, (share, 1), 0)
    shift = jnp.where(rows < own, half * own, (1 - half) * own - own)
    side_k = low_k + rows + shift >= boundary
    return meets, mixed, side_q.astype(f32), side_k.astype(f32)


def visit_blocks(info_ref, query_block, columns, share, own, visit):
    def step(key_block, carry):
        meets, mixed, side_q, side_k = block_sides(info_ref, query_block, key_block, columns, share, own)

        @pl.when(meets & mixed)
        def _():
            visit(key_block, side_q == side_k)

        @pl.when(meets & jnp.logical_not(mixed))
        def _():
            visit(key_block, None)

        return carry

    lax.fori_loop(0, columns, step, 0)


def forward_kernel(first, share, info_ref, q_ref, k0_ref, k1_ref, vt0_ref, vt1_ref, *refs):
    columns, own, _ = k0_ref.shape
    width = vt0_ref.shape[1]
    heads = width // DH
    count = (len(refs) - 4) // 2
    outs, lses, (parts, top, total, sums) = refs[:count], refs[count : 2 * count], refs[2 * count :]
    scaling = DH ** (-0.5) * LOG2E

    def visit(key_block, same):
        keys = jnp.concatenate([k0_ref[key_block], k1_ref[key_block]], 0)
        values = jnp.concatenate([vt0_ref[key_block], vt1_ref[key_block]], 1)
        for head in range(heads):
            rows = pl.ds(head * DH, DH)
            line = pl.ds(head, 1)
            scores = contract(keys, parts[head], (1, 1)) * scaling
            if same is not None:
                scores = jnp.where(same, scores, MASKED)
            before = top[line, :]
            highest = jnp.maximum(before, jnp.max(scores, 0, keepdims=True))
            fade = jnp.exp2(before - highest)
            raised = jnp.exp2(scores - highest)
            if same is not None:
                raised = jnp.where(same, raised, 0.0)
            top[line, :] = highest
            total[line, :] = total[line, :] * fade + jnp.sum(raised, 0, keepdims=True)
            product = jnp.dot(values[head * DH : (head + 1) * DH], raised.astype(bf16), preferred_element_type=f32)
            sums[rows, :] = sums[rows, :] * fade + product

    for index in range(count):
        for head in range(heads):
            parts[head] = head_lanes(q_ref[first + index], head)
        top[...] = jnp.full_like(top, MASKED)
        total[...] = jnp.zeros_like(total)
        sums[...] = jnp.zeros_like(sums)
        visit_blocks(info_ref, first + index, columns, share, own, visit)
        for head in range(heads):
            rows = pl.ds(head * DH, DH)
            line = pl.ds(head, 1)
            outs[index][rows, :] = (sums[rows, :] / total[line, :]).astype(bf16)
            lses[index][line, :] = top[line, :] + jnp.log2(total[line, :])


def attend_forward(first, count, info, q, kv, kv_twin, turned, turned_twin, share):
    columns, own, padded = q.shape
    width = turned.shape[1]
    heads = width // DH
    keys = pl.BlockSpec((columns, own, padded), lambda i, s: (0, 0, 0))
    values = pl.BlockSpec((columns, width, own), lambda i, s: (1, 0, 0))
    flat = lambda rows: pl.BlockSpec((rows, own), lambda i, s: (0, 0))
    outs = pl.pallas_call(
        lambda *refs: forward_kernel(first, share, *refs),
        grid_spec=pltpu.PrefetchScalarGridSpec(
            num_scalar_prefetch=1,
            grid=(1,),
            in_specs=[keys, keys, keys, values, values],
            out_specs=[flat(width)] * count + [flat(heads)] * count,
            scratch_shapes=[
                pltpu.VMEM((heads, own, padded), bf16),
                pltpu.VMEM((heads, own), f32),
                pltpu.VMEM((heads, own), f32),
                pltpu.VMEM((width, own), f32),
            ],
        ),
        out_shape=[jax.ShapeDtypeStruct((width, own), bf16)] * count + [jax.ShapeDtypeStruct((heads, own), f32)] * count,
        compiler_params=pltpu.CompilerParams(vmem_limit_bytes=60 << 20),
        cost_estimate=cost(0.001),
        name="attend_forward",
    )(info, q, kv, kv_twin, turned, turned_twin)
    return outs[:count], outs[count:]


def backward_kernel(columns, share, info_ref, q_ref, kv0_ref, kv1_ref, kt0_ref, kt1_ref, *refs):
    grads, outs, lses, refs = refs[0], refs[1 : columns + 1], refs[columns + 1 : 2 * columns + 1], refs[2 * columns + 1 :]
    dq_ref, near_ref, *fars, part_q, part_g, delta, lse, sum_q, sum_k, sum_v = refs
    own, width = q_ref.shape[1], kt0_ref.shape[1]
    heads = width // DH
    scaling = DH ** (-0.5)
    sum_k[...] = jnp.zeros_like(sum_k)
    sum_v[...] = jnp.zeros_like(sum_v)
    for block in range(columns):
        lse[block] = lses[block][...]
        column = info_ref[2] - block
        grad = grads[jnp.where(column < 0, column + columns, column)]
        spare = jnp.zeros((part_g.shape[1] - width, own), bf16)
        product = grad.astype(f32) * outs[block][...].astype(f32)
        for head in range(heads):
            part_q[block, pl.ds(head * own, own), :] = head_lanes(q_ref[block], head)
            part_g[block, :, pl.ds(head * own, own)] = jnp.concatenate([head_rows(grad, head), spare], 0)
            delta[block, pl.ds(head, 1), :] = jnp.sum(product[head * DH : (head + 1) * DH], 0, keepdims=True)

    def query_step(block, carry):
        sum_q[...] = jnp.zeros_like(sum_q)

        def visit(key_block, same):
            keys = jnp.concatenate([kv0_ref[key_block], kv1_ref[key_block]], 0)
            turned = jnp.concatenate([kt0_ref[key_block], kt1_ref[key_block]], 1)
            values = jnp.concatenate([kv0_ref[columns + key_block], kv1_ref[columns + key_block]], 0)
            all_probs, all_grads = [], []
            for head in range(heads):
                span = pl.ds(head * own, own)
                scores = contract(keys, part_q[block, span, :], (1, 1)) * (scaling * LOG2E)
                probs = jnp.exp2(scores - lse[block, pl.ds(head, 1), :])
                if same is not None:
                    probs = jnp.where(same, probs, 0.0)
                slopes = jnp.dot(values, part_g[block, :, span], preferred_element_type=f32)
                grads = (probs * (slopes - delta[block, pl.ds(head, 1), :])).astype(bf16)
                all_probs.append(probs.astype(bf16))
                all_grads.append(grads)
            for head in range(heads):
                rows = pl.ds(head * DH, DH)
                part = turned[head * DH : (head + 1) * DH]
                sum_q[rows, :] += jnp.dot(part, all_grads[head], preferred_element_type=f32)
            sum_v[key_block] += contract(jnp.concatenate(all_probs, 1), part_g[block], (1, 1))
            sum_k[key_block] += jnp.dot(jnp.concatenate(all_grads, 1), part_q[block], preferred_element_type=f32)

        visit_blocks(info_ref, block, columns, share, own, visit)
        dq_ref[block] = sum_q[...].T * scaling
        return carry

    lax.fori_loop(0, columns, query_step, 0)
    for block in range(columns):
        for place, sums, far_ref in ((block, sum_k, fars[0]), (columns + block, sum_v, fars[1])):
            near_ref[place] = sums[block, :own].astype(bf16)
            far_ref[block] = sums[block, own:].astype(bf16)


def attend_backward(info, q, kv, kv_twin, turned, turned_twin, grads, outs, lses, share):
    columns, own, padded = q.shape
    width = turned.shape[1]
    heads = width // DH
    vmem = pl.BlockSpec(memory_space=pltpu.VMEM)
    operands = [q, kv, kv_twin, turned, turned_twin, grads, *outs, *lses]
    return pl.pallas_call(
        lambda *refs: backward_kernel(columns, share, *refs),
        in_specs=[pl.BlockSpec(memory_space=pltpu.SMEM)] + [vmem] * len(operands),
        out_specs=[vmem] * 4,
        out_shape=[jax.ShapeDtypeStruct((columns, own, width), f32)]
        + [jax.ShapeDtypeStruct((many, own, padded), bf16) for many in (2 * columns, columns, columns)],
        scratch_shapes=[
            pltpu.VMEM((columns, heads * own, padded), bf16),
            pltpu.VMEM((columns, padded, heads * own), bf16),
            pltpu.VMEM((columns, heads, own), f32),
            pltpu.VMEM((columns, heads, own), f32),
            pltpu.VMEM((width, own), f32),
            pltpu.VMEM((columns, share, padded), f32),
            pltpu.VMEM((columns, share, padded), f32),
        ],
        compiler_params=pltpu.CompilerParams(vmem_limit_bytes=60 << 20),
        cost_estimate=cost(0.001),
        name="attend_backward",
    )(info, *operands)


def unproject_kernel(info_ref, dq_ref, near_k_ref, far_k_ref, near_v_ref, far_v_ref, w_ref, cos_ref, sin_ref, part_ref, low_ref):
    width = dq_ref.shape[2]
    lanes = 2 * width
    even = lax.broadcasted_iota(jnp.int32, (dq_ref.shape[1], lanes), 1) % 2 == 0
    dk = (near_k_ref[0, :, :width].astype(f32) + far_k_ref[0, :, :width].astype(f32)) * DH ** (-0.5)
    dv = near_v_ref[0, :, :width].astype(f32) + far_v_ref[0, :, :width].astype(f32)
    both = jnp.concatenate([dq_ref[0], dk], 1)
    swapped = jnp.where(even, pltpu.roll(both, lanes - 1, 1), pltpu.roll(both, 1, 1))
    both = both * widen(cos_ref[0], lanes) - swapped * widen(sin_ref[0], lanes)
    low = jnp.concatenate([both, dv], 1).astype(bf16)
    low_ref[0] = low
    part_ref[0] = contract(low, w_ref[...], (1, 1)).astype(bf16)


def unproject(info, dq, near, far_k, far_v, weight, cosine, sine):
    columns, own, width = dq.shape
    feature = weight.shape[0]
    block = lambda a, first: pl.BlockSpec((1,) + a.shape[1:], lambda i, s: (first + i, 0, 0))
    whole = lambda a: pl.BlockSpec(a.shape, lambda i, s: (0, 0))
    place = lambda i, s: (jnp.where(s[2] >= i, s[2] - i, s[2] - i + columns), 0, 0)
    low = jax.ShapeDtypeStruct((columns, own, weight.shape[1]), bf16)
    return pl.pallas_call(
        unproject_kernel,
        grid_spec=pltpu.PrefetchScalarGridSpec(
            num_scalar_prefetch=1,
            grid=(columns,),
            in_specs=[block(dq, 0), block(near, 0), block(far_k, 0), block(near, columns), block(far_v, 0), whole(weight)]
            + [block(cosine, 0), block(sine, 0)],
            out_specs=[pl.BlockSpec((1, own, feature), place), block(low, 0)],
        ),
        out_shape=[jax.ShapeDtypeStruct((columns, own, feature), bf16), low],
        compiler_params=pltpu.CompilerParams(vmem_limit_bytes=60 << 20),
        cost_estimate=cost(0.001),
        name="unproject",
    )(info, dq, near, far_k, near, far_v, weight, cosine, sine)


def project_grad_kernel(low_ref, *refs):
    x_refs, (grad_ref,) = refs[:-1], refs[-1:]
    total = None
    for block, x_ref in enumerate(x_refs):
        piece = contract(x_ref[...], low_ref[block], (0, 0))
        total = piece if total is None else total + piece
    grad_ref[...] = total.astype(bf16)


def project_grad(low, blocks):
    return pl.pallas_call(
        project_grad_kernel,
        out_shape=jax.ShapeDtypeStruct((blocks[0].shape[1], low.shape[2]), bf16),
        compiler_params=pltpu.CompilerParams(vmem_limit_bytes=60 << 20),
        cost_estimate=cost(0.001),
        name="project_grad",
    )(low, *blocks)


def mean_lanes(values):
    return jnp.sum(values, 1, keepdims=True) * (1.0 / values.shape[1])


def norm_forward(values, gain, shift):
    centred = values - mean_lanes(values)
    inverse = lax.rsqrt(mean_lanes(centred * centred) + EPSILON)
    normed = centred * inverse
    return normed * gain + shift, normed, inverse


def norm_backward(grad, normed, inverse, gain):
    scaled = grad * gain
    return inverse * (scaled - mean_lanes(scaled) - normed * mean_lanes(scaled * normed))


def unit(size):
    rows = lax.broadcasted_iota(jnp.int32, (size, size), 0)
    return (rows == lax.broadcasted_iota(jnp.int32, (size, size), 1)).astype(bf16)


def feed_kernel(info_ref, x_ref, cot_ref, w_ref, *refs):
    parts, _, columns, slab, _ = w_ref.shape
    att_refs, refs = refs[:columns], refs[columns:]
    result_ref, grad_att_ref, grad_one_ref, hidden_ref, act_out, gin_out, gtwo_ref, gone_ref, sums_ref, sent_ref, *refs = refs
    w, slopes, outer, act_ref, gin_ref, stage, sems, ends = refs
    rows, columns, quarter, _ = w.shape
    act_copy = pltpu.make_async_copy(act_ref, act_out, ends.at[0])
    gin_copy = pltpu.make_async_copy(gin_ref, gin_out, ends.at[1])

    def turned(step):
        column = info_ref[2] + step
        return jnp.where(column >= columns, column - columns, column)

    hidden_cols = act_ref.shape[2]
    both = 2 * hidden_cols
    spans = ((0, hidden_cols), (hidden_cols, hidden_cols), (both, w.shape[3] - both))

    def copies(kind):
        lanes = pl.ds(*spans[kind])
        for part in range(parts):
            target = w.at[:, :, pl.ds(part * slab, slab), lanes]
            yield pltpu.make_async_copy(w_ref.at[part, :, :, :, lanes], target, sems.at[kind, part])

    def wait(kind):
        for each in copies(kind):
            each.wait()

    for kind in (2, 0, 1):
        for each in copies(kind):
            each.start()

    def block(kind, column):
        lanes = pl.ds(*spans[kind])
        return jnp.concatenate([w[row, column, :, lanes] for row in range(rows)], 0)

    wait(2)
    mix = pl.ds(both, quarter)
    attended = jnp.concatenate([ref[...] for ref in att_refs], 0)
    branch = []
    for row in range(rows):
        weight = jnp.concatenate([w[row, turned(step), :, mix] for step in range(columns)], 0)
        branch.append(contract(attended, weight, (0, 0)))
    branch = jnp.concatenate(branch, 1)
    eye = unit(quarter)
    small = [contract(w[row, 0, :, pl.ds(both + quarter, 12)], eye, (0, 0)) for row in range(rows)]
    small = jnp.concatenate(small, 1)
    vectors = small[0:4] + (small[4:8] + small[8:12])
    gain_one, shift_one, gain_two, shift_two = (vectors[i : i + 1] for i in range(4))

    hidden, normed_one, inverse_one = norm_forward(x_ref[...].astype(f32) + branch, gain_one, shift_one)
    low = hidden.astype(bf16)
    hidden_ref[...] = low.T
    outer[...] = jnp.zeros_like(outer)

    wait(0)

    def forward(column, carry):
        inner = jnp.dot(low, block(0, column), preferred_element_type=f32)
        cumulative = 0.5 * (1.0 + lax.erf(inner * (0.5**0.5)))
        slopes[column] = cumulative + inner * (jnp.exp(-0.5 * inner * inner) * 0.3989422804014327)
        act_ref[column] = (inner * cumulative).astype(bf16)
        return carry

    lax.fori_loop(0, columns, forward, 0)
    act_copy.start()
    wait(1)

    def combine(column, carry):
        outer[...] += contract(act_ref[column], block(1, column), (1, 1))
        return carry

    lax.fori_loop(0, columns, combine, 0)
    result, normed_two, inverse_two = norm_forward(hidden + outer[...], gain_two, shift_two)
    result_ref[...] = result.astype(bf16)
    cot = cot_ref[...].astype(f32)
    grad_two = norm_backward(cot, normed_two, inverse_two, gain_two)
    grad_two_low = grad_two.astype(bf16)
    gtwo_ref[...] = grad_two_low.T
    outer[...] = grad_two

    def backward(column, carry):
        grad = jnp.dot(grad_two_low, block(1, column), preferred_element_type=f32)
        gin_ref[column] = (grad * slopes[column]).astype(bf16)
        outer[...] += contract(gin_ref[column], block(0, column), (1, 1))
        return carry

    lax.fori_loop(0, columns, backward, 0)
    gin_copy.start()
    grad_hidden = outer[...]
    grad_one = norm_backward(grad_hidden, normed_one, inverse_one, gain_one)
    grad_one_ref[...] = grad_one
    grad_one_low = grad_one.astype(bf16)
    for step in range(columns):
        weight = jnp.concatenate([w[row, turned(step), :, mix] for row in range(rows)], 1)
        grad_att_ref[turned(step)] = contract(weight, grad_one_low, (1, 1)).astype(bf16)
    sums = [jnp.sum(a, 0, keepdims=True) for a in (grad_hidden * normed_one, grad_hidden, cot * normed_two, cot)]
    sums = jnp.concatenate(sums, 0)
    for row in range(rows):
        mine = slice(row * quarter, (row + 1) * quarter)
        gone_ref[row] = grad_one_low[:, mine]
        sums_ref[row] = sums[:, mine].astype(bf16)

    copies_out = []
    for column in range(columns):
        slot = column % 2
        if column > 1:
            copies_out[column - 2].wait()
        attended = attended_block(info_ref, att_refs, column)
        operands = attended, act_ref[column], gin_ref[column], hidden_ref, gtwo_ref, gone_ref, sums_ref
        weigh_block(1 - info_ref[1], info_ref, *operands, stage.at[slot])
        copies_out.append(pltpu.make_async_copy(stage.at[slot], sent_ref.at[:, :, column], ends.at[2 + slot]))
        copies_out[-1].start()
    for copy in copies_out[-2:] + [act_copy, gin_copy]:
        copy.wait()


def feed(info, attended, tokens, cot, weights, slabs):
    own, feature = tokens.shape
    parts, rows, columns, slab, lanes = weights.shape
    quarter = parts * slab
    hidden_cols = feature
    vmem, smem = pl.BlockSpec(memory_space=pltpu.VMEM), pl.BlockSpec(memory_space=pltpu.SMEM)
    hbm = pl.BlockSpec(memory_space=pltpu.HBM)
    wide = jax.ShapeDtypeStruct((columns, own, hidden_cols), bf16)
    flat = lambda kind: jax.ShapeDtypeStruct((own, feature), kind)
    tall = jax.ShapeDtypeStruct((feature, own), bf16)
    return pl.pallas_call(
        feed_kernel,
        in_specs=[smem, vmem, vmem, pl.BlockSpec(memory_space=pltpu.HBM)] + [vmem] * columns,
        out_specs=[vmem] * 4 + [hbm] * 2 + [vmem] * 3 + [hbm],
        out_shape=[
            flat(bf16), jax.ShapeDtypeStruct((columns, quarter, own), bf16), flat(f32), tall, wide, wide, tall,
            jax.ShapeDtypeStruct((rows, own, quarter), bf16), jax.ShapeDtypeStruct((rows, 4, quarter), bf16),
            jax.ShapeDtypeStruct((2, slabs, columns, quarter // slabs, lanes), bf16),
        ],
        scratch_shapes=[
            pltpu.VMEM((rows, columns, quarter, lanes), bf16),
            pltpu.VMEM((columns, own, hidden_cols), f32),
            pltpu.VMEM((own, feature), f32),
            pltpu.VMEM(wide.shape, bf16),
            pltpu.VMEM(wide.shape, bf16),
            pltpu.VMEM((2, 2, slabs, quarter // slabs, lanes), bf16),
            pltpu.SemaphoreType.DMA((3, parts)),
            pltpu.SemaphoreType.DMA((4,)),
        ],
        compiler_params=pltpu.CompilerParams(vmem_limit_bytes=60 << 20),
        cost_estimate=cost(0.001),
        name="feed",
    )(info, tokens, cot, weights, *attended)


def weigh_block(core, info_ref, attended, act, gin, hidden_ref, gtwo_ref, gone_ref, sums_ref, out):
    _, slabs, slab, lanes = out.shape
    quarter = slabs * slab
    hidden_cols = act.shape[1]
    eye = unit(quarter)
    away = lambda index, mine: jnp.where(index == mine, 0, 1)
    for pair in range(2):
        row = 2 * pair + core
        mine = pl.ds(pl.multiple_of(row * quarter, quarter), quarter)
        inner = jnp.dot(hidden_ref[mine, :], gin, preferred_element_type=f32).astype(bf16)
        outer = jnp.dot(gtwo_ref[mine, :], act, preferred_element_type=f32).astype(bf16)
        mixed = jnp.dot(attended, gone_ref[row], preferred_element_type=f32).astype(bf16)
        vector = contract(eye, sums_ref[row], (1, 1)).astype(bf16)
        rest = jnp.zeros((quarter, lanes - 2 * hidden_cols - quarter - 4), bf16)
        tail = jnp.concatenate([mixed, vector, rest], 1)
        far = away(pair, info_ref[3])
        for part in range(slabs):
            place = away(part, info_ref[4]) if slabs > 1 else 0
            rows = slice(part * slab, (part + 1) * slab)
            out[far, place, :, 0:hidden_cols] = inner[rows]
            out[far, place, :, hidden_cols : 2 * hidden_cols] = outer[rows]
            out[far, place, :, 2 * hidden_cols :] = tail[rows]


def attended_block(info_ref, att_refs, column):
    step = column - info_ref[2]
    step = jnp.where(step < 0, step + len(att_refs), step)
    attended = att_refs[0][...]
    for index in range(1, len(att_refs)):
        attended = jnp.where(step == index, att_refs[index][...], attended)
    return attended


def weigh_kernel(info_ref, hidden_ref, act_ref, gin_ref, gtwo_ref, gone_ref, sums_ref, *refs):
    att_refs, out_ref = refs[:-1], refs[-1]
    attended = attended_block(info_ref, att_refs, pl.program_id(0))
    operands = attended, act_ref[0], gin_ref[0], hidden_ref, gtwo_ref, gone_ref, sums_ref
    weigh_block(info_ref[1], info_ref, *operands, out_ref.at[:, :, 0])


def weigh(info, attended, hidden, act, gin, gtwo, gone, sums, lanes, slabs):
    columns = act.shape[0]
    quarter = attended[0].shape[0]
    whole = lambda a: pl.BlockSpec(a.shape, lambda i, s: (0,) * a.ndim)
    piece = pl.BlockSpec((1,) + act.shape[1:], lambda i, s: (i, 0, 0))
    slab = quarter // slabs
    return pl.pallas_call(
        weigh_kernel,
        grid_spec=pltpu.PrefetchScalarGridSpec(
            num_scalar_prefetch=1,
            grid=(columns,),
            in_specs=[whole(hidden), piece, piece, whole(gtwo), whole(gone), whole(sums)] + [whole(a) for a in attended],
            out_specs=pl.BlockSpec((2, slabs, 1, slab, lanes), lambda i, s: (0, 0, i, 0, 0)),
        ),
        out_shape=jax.ShapeDtypeStruct((2, slabs, columns, slab, lanes), bf16),
        compiler_params=pltpu.CompilerParams(vmem_limit_bytes=60 << 20),
        cost_estimate=cost(0.001),
        name="weigh",
    )(info, hidden, act, gin, gtwo, gone, sums, *attended)


def parcel_kernel(info_ref, inner_ref, outer_ref, output_ref, *refs):
    small_refs, out_ref = refs[:-1], refs[-1]
    columns = inner_ref.shape[1]
    quarter = output_ref.shape[1]
    slab = out_ref.shape[0]
    offset = info_ref[0] * slab if slab < quarter else 0
    rows = pl.ds(pl.multiple_of(offset, slab), slab)
    values = jnp.concatenate([ref[...] for ref in small_refs], 0)
    high = values.astype(bf16)
    rest = values - high.astype(f32)
    middle = rest.astype(bf16)
    last = (rest - middle.astype(f32)).astype(bf16)
    pick = lax.broadcasted_iota(jnp.int32, (slab, quarter), 0) + offset
    pick = (pick == lax.broadcasted_iota(jnp.int32, (slab, quarter), 1)).astype(bf16)
    small = jnp.concatenate([contract(pick, part, (1, 1)) for part in (high, middle, last)], 1).astype(bf16)
    fill = jnp.zeros((slab, out_ref.shape[1] - 2 * columns - quarter - 12), bf16)
    out_ref[:, 0:columns] = inner_ref[rows, :]
    out_ref[:, columns : 2 * columns] = outer_ref[rows, :]
    out_ref[:, 2 * columns :] = jnp.concatenate([output_ref[rows, :], small, fill], 1)


def parcel(part, inner, outer, output, vectors, lanes, slabs):
    vmem, smem = pl.BlockSpec(memory_space=pltpu.VMEM), pl.BlockSpec(memory_space=pltpu.SMEM)
    return pl.pallas_call(
        parcel_kernel,
        in_specs=[smem] + [vmem] * 7,
        out_shape=jax.ShapeDtypeStruct((inner.shape[0] // slabs, lanes), bf16),
        cost_estimate=cost(0.001),
        name="parcel",
    )(part, inner, outer, output, *(v.reshape(1, -1) for v in vectors))


def keep(values, index, axis=0):
    first, second = lax.index_in_dim(values, 0, axis, False), lax.index_in_dim(values, 1, axis, False)
    chosen = index == 0
    return jnp.where(chosen, first, second), jnp.where(chosen, second, first)


def tie(*values):
    return lax.optimization_barrier(values)


def shift(values, step):
    columns = lax.axis_size("col")
    if step % columns == 0:
        return values
    return lax.ppermute(values, "col", [(i, (i + step) % columns) for i in range(columns)])


def add_kernel(count, sums, *refs):
    results, (*sources, buffer, held, sems, ends) = refs[-count - 4 : -4], refs[: -count - 4] + refs[-4:]
    rows, first, number = [], 0, 0
    for index, start, parts in sums:
        row = []
        for which, lead, low, high in parts:
            source = sources[which].at[lead + (pl.ds(low, high - low),)]
            copy = pltpu.make_async_copy(source, buffer.at[pl.ds(first, high - low)], sems.at[number])
            copy.start()
            row.append((first, high - low, copy))
            first, number = first + high - low, number + 1
        rows.append(row)
    copies, first = [], 0
    for place, ((index, start, _), row) in enumerate(zip(sums, rows)):
        size = row[0][1]
        for *_, copy in row:
            copy.wait()
        total = sum(buffer[at : at + size].astype(f32) for at, *_ in row)
        held[first : first + size] = total.astype(bf16)
        target = results[index].at[pl.ds(start, size)]
        copies.append(pltpu.make_async_copy(held.at[pl.ds(first, size)], target, ends.at[place]))
        copies[-1].start()
        first += size
    for copy in copies:
        copy.wait()


def add_blocks(arrays, lengths, sums):
    hbm = pl.BlockSpec(memory_space=pltpu.HBM)
    tail = arrays[0].shape[-2:]
    parts = [part for *_, each in sums for part in each]
    return pl.pallas_call(
        lambda *refs: add_kernel(len(lengths), sums, *refs),
        in_specs=[hbm] * len(arrays),
        out_specs=[hbm] * len(lengths),
        out_shape=[jax.ShapeDtypeStruct((length,) + tail, bf16) for length in lengths],
        scratch_shapes=[
            pltpu.VMEM((sum(high - low for *_, low, high in parts),) + tail, bf16),
            pltpu.VMEM((sum(lengths),) + tail, bf16),
            pltpu.SemaphoreType.DMA((len(parts),)),
            pltpu.SemaphoreType.DMA((len(sums),)),
        ],
        compiler_params=pltpu.CompilerParams(vmem_limit_bytes=60 << 20),
        cost_estimate=cost(0.001),
        name="add_blocks",
    )(*arrays)


def open_kernel(hidden_cols, part_ref, mine_ref, other_ref, *outs):
    *outs, sums_ref, query_ref, key_ref, value_ref = outs
    slab, quarter = mine_ref.shape[0], outs[2].shape[1]
    spans = (0, hidden_cols), (hidden_cols, hidden_cols), (2 * hidden_cols, quarter)
    lanes = mine_ref.shape[1] - 6 * quarter

    def write(first, second):
        for (start, size), out in zip(spans, outs):
            out[0:slab, :] = first[:, start : start + size].astype(f32)
            out[slab : 2 * slab, :] = second[:, start : start + size].astype(f32)
        start = 2 * hidden_cols + quarter
        last = jnp.concatenate([first[:, start:lanes], second[:, start:lanes]], 0)
        sums_ref[...] = contract(last[:, 0:4], unit(2 * slab), (0, 0))

    @pl.when(part_ref[0] == 0)
    def _():
        write(mine_ref[...], other_ref[...])

    @pl.when(part_ref[0] != 0)
    def _():
        write(other_ref[...], mine_ref[...])

    total = mine_ref[:, lanes:].astype(f32) + other_ref[:, lanes:].astype(f32)
    for index, ref in enumerate((query_ref, key_ref, value_ref)):
        for half in range(2):
            start = (3 * half + index) * quarter
            ref[half * slab : (half + 1) * slab, :] = total[:, start : start + quarter]


def open_shards(part, mine, other, hidden_cols, quarter):
    vmem, smem = pl.BlockSpec(memory_space=pltpu.VMEM), pl.BlockSpec(memory_space=pltpu.SMEM)
    rows = hidden_cols, hidden_cols, quarter
    shape = lambda *dims: jax.ShapeDtypeStruct(dims, f32)
    return pl.pallas_call(
        lambda *refs: open_kernel(hidden_cols, *refs),
        in_specs=[smem, vmem, vmem],
        out_shape=[shape(quarter, a) for a in rows] + [shape(4, quarter)] + [shape(quarter, quarter)] * 3,
        compiler_params=pltpu.CompilerParams(vmem_limit_bytes=16 << 20),
        cost_estimate=cost(0.001),
        name="open_shards",
    )(part, mine, other)


def sum_shards(kept, sent, mark):
    columns = kept.shape[2]
    middle = columns // 2
    pair = kept, swap(sent, "yb")
    both = lambda lead, low, high: [(0, lead, low, high), (1, lead, low, high)]
    to_dp = [(0, 0, both((1, 1), 0, middle)), (0, middle, both((0, 1), 0, middle))]
    to_ya = [(1, 0, both((1, 1), middle, columns)), (1, middle, both((1, 0), middle, columns))]
    to_dp, to_ya = add_blocks(pair, (columns, columns), to_dp + to_ya)
    mark, to_dp, to_ya = tie(mark, to_dp, to_ya)
    by_dp, by_ya = swap(to_dp, "dp"), swap(to_ya, "ya")

    def sides(mark):
        dp, ya, mark = tie(by_dp, by_ya, mark)
        rest_ya = (0, 0, both((1, 0), 0, middle) + [(2, (), 0, middle)])
        rest_dp = (1, 0, both((0, 1), middle, columns) + [(3, (), 0, middle)])
        rest_ya, rest_dp = add_blocks(pair + (dp, ya), (middle, columns - middle), [rest_ya, rest_dp])
        mark, rest_ya, rest_dp = tie(mark, rest_ya, rest_dp)
        rest_ya, rest_dp = swap(rest_ya, "ya"), swap(rest_dp, "dp")

        def finish(mark):
            low_ya, high_dp, mark = tie(rest_ya, rest_dp, mark)
            low = both((0, 0), 0, middle) + [(2, (), middle, columns), (4, (), 0, middle)]
            high = both((0, 0), middle, columns) + [(3, (), middle, columns), (5, (), 0, columns - middle)]
            (own,) = add_blocks(pair + (dp, ya, low_ya, high_dp), (columns,), [(0, 0, low), (0, middle, high)])
            own, mark = tie(own, mark)
            mine = lax.psum_scatter(own, "col", scatter_dimension=0, tiled=False)
            return mine, mark

        return mark, finish

    return mark, sides


def body(
    inputs, cotangent, lengths, source, query_weight, key_weight, value_weight, output_weight, inner_weight, outer_weight,
    first_gain, first_shift, second_gain, second_shift,
):
    micro, quarter, share = inputs.shape
    dp_count, columns = lax.axis_size("dp"), lax.axis_size("col")
    pack, own = share * columns, share // 2
    feature, count = 4 * quarter, share * micro
    width, hidden_cols = query_weight.shape[1], inner_weight.shape[1]
    lanes = -(-(2 * hidden_cols + quarter + 12) // 128) * 128
    me, m, half, z = (lax.axis_index(a) for a in ("dp", "ya", "yb", "col"))

    boundary = jnp.where(m == 0, lengths[0, 0], lengths[0, 1])
    info = jnp.stack([boundary, half, z, m, me]).astype(jnp.int32)
    slabs = 2 if dp_count == 2 else 1

    vectors = (first_gain, first_shift, second_gain, second_shift)
    anchors = spread_dp(source)
    packed = parcel(jnp.reshape(me, (1,)).astype(jnp.int32), inner_weight, outer_weight, output_weight, vectors, lanes, slabs)
    axes = ("dp",) + SHARDS if slabs == 2 else SHARDS
    everywhere = lax.all_gather(packed, axes, axis=0).reshape(slabs, 4, columns, quarter // slabs, lanes)
    anchor = source.reshape(count)
    place = anchor // (dp_count * pack) * share + anchor % share
    holder = anchor % (dp_count * pack) // pack
    wide_in = spread_dp(inputs)

    steps = jnp.arange(columns, dtype=jnp.int32)
    spots = ((z - steps) % columns * share + half * own)[:, None] + jnp.arange(own, dtype=jnp.int32)[None, :]
    frequency = 10000.0 ** (-2.0 * jnp.arange(DH // 2, dtype=f32) / DH)
    angles = (spots - jnp.where(spots >= boundary, boundary, 0)).astype(f32)[..., None] * jnp.tile(jnp.repeat(frequency, 2), 2)
    signs = jnp.where(jnp.arange(2 * DH) % 2 == 0, -1.0, 1.0)
    cosine, sine = jnp.cos(angles), jnp.sin(angles) * signs
    wide_in, cosine, sine = tie(wide_in, cosine, sine)

    if dp_count == 2:
        pick = (holder * count + place)[:, None] == jnp.arange(dp_count * count, dtype=jnp.int32)[None, :]
        pick = pick.astype(bf16).reshape(count, dp_count, micro, share)
        deal = lambda wide: jnp.einsum("tsmj,smfj->tf", pick, wide, preferred_element_type=f32).astype(bf16)
    else:
        deal = lambda wide: wide.transpose(0, 1, 3, 2).reshape(-1, quarter)[holder * count + place]

    def to_tokens(dealt):
        return lax.all_to_all(dealt.reshape(4, own, quarter), ROWS, split_axis=0, concat_axis=0, tiled=True)

    dealt = deal(wide_in)
    cotangent, dealt = tie(cotangent, dealt)
    tokens = to_tokens(dealt).transpose(1, 0, 2).reshape(own, feature)
    wide_cot, tokens = tie(spread_dp(cotangent), tokens)
    blocks = [shift(tokens, step) for step in range(columns)]
    cot = to_tokens(deal(wide_cot)).transpose(1, 0, 2).reshape(own, feature)
    qkv_weight = jnp.concatenate([query_weight, key_weight, value_weight], 1)
    qkv_weight = gather_rows(qkv_weight).reshape(feature, -1)

    blocks[-1], cot, anchors = tie(blocks[-1], cot, anchors)
    q, kv, turned = project(blocks, qkv_weight, cosine, sine)
    kv_twin, turned_twin = swap(kv, "yb"), swap(turned, "yb")
    mixed, lses = attend_forward(1, columns - 1, info, q, kv, kv_twin, turned, turned_twin, share)
    q, mixed = tie(q, mixed)
    last = attend_forward(0, 1, info, q, kv, kv_twin, turned, turned_twin, share)
    mixed, lses = last[0] + mixed, last[1] + lses
    attended = [shift(mixed[step], -step) for step in range(columns)]

    result, grad_att, grad_one, *pieces, sent = feed(info, attended, tokens, cot, everywhere, slabs)
    grad_att = lax.all_to_all(grad_att, "col", split_axis=0, concat_axis=0, tiled=True)
    def to_loader(*rows):
        cut = jnp.concatenate([a.astype(bf16).reshape(own, 4, quarter).transpose(1, 0, 2) for a in rows], 2)
        cut = jnp.broadcast_to(cut[None], (dp_count,) + cut.shape).reshape(dp_count * 4, own, -1)
        moved = lax.all_to_all(cut, ("dp",) + ROWS, split_axis=0, concat_axis=0, tiled=True)
        return moved.reshape(-1, len(rows) * quarter)

    spot = jnp.arange(count, dtype=jnp.int32)
    wanted = spot // share * (dp_count * pack) + me * pack + z * share + spot % share
    if dp_count == 2:
        put = (anchors.reshape(-1)[:, None] == wanted[None, :]).astype(bf16)
        settle = lambda wide: contract(wide, put, (0, 0)).astype(bf16)
    else:
        order = jnp.argsort(anchors.reshape(-1))
        spots_in = jnp.searchsorted(anchors.reshape(-1)[order], wanted)
        settle = lambda wide: wide[order[spots_in]].T
    kept = weigh(info, attended, *pieces, lanes, slabs)
    if slabs == 2:
        grad_att, sides = sum_shards(kept, sent, grad_att)
    else:
        flip = lambda a, index, axis: jnp.where(index == 0, a, jnp.flip(a, axis))
        cut = flip(flip(jnp.stack([kept, sent], 1), m, 0), half, 1).reshape(4 * columns, quarter, lanes)
        summed = lax.psum_scatter(cut, SHARDS, scatter_dimension=0, tiled=False)
        summed = lax.psum(summed, "dp").astype(f32)

    dq, near, *far = attend_backward(info, q, kv, kv_twin, turned, turned_twin, grad_att, mixed, lses, share)
    partial, low = unproject(info, dq, near, *(swap(each, "yb") for each in far), qkv_weight, cosine, sine)
    if slabs == 2:
        low, finish = sides(low)
    grad_qkv = project_grad(low, blocks)
    partial = lax.all_to_all(partial, "col", split_axis=0, concat_axis=0, tiled=True)
    grad_tokens = grad_one + jnp.sum(partial.astype(f32), 0)

    def over_dp(values):
        if dp_count == 2:
            return values.astype(f32) + swap(values, "dp").astype(f32)
        return lax.psum(values, "dp").astype(f32)

    def halve(grad, axis, index, place_axis):
        kept, sent = keep(grad, index, place_axis)
        return (kept.astype(f32) + swap(sent, axis).astype(f32)).astype(bf16)

    if slabs == 2:
        summed, grad_qkv = finish(grad_qkv)
    grad_qkv = halve(grad_qkv.reshape(2, 2, quarter, 3 * width), "yb", half, 1)
    grad_qkv = halve(grad_qkv, "ya", m, 0)
    grad_tokens, grad_qkv = tie(grad_tokens, grad_qkv)
    if slabs == 1:
        grad_qkv = over_dp(grad_qkv)
        sum_qkv = [grad_qkv[:, i * width : (i + 1) * width] for i in range(3)]
        sum_inner, sum_outer = summed[:, :hidden_cols], summed[:, hidden_cols : 2 * hidden_cols]
        sum_output = summed[:, 2 * hidden_cols : 2 * hidden_cols + quarter]
        sum_vectors = summed[:, 2 * hidden_cols + quarter : 2 * hidden_cols + quarter + 4].T

    shape = lambda a: a.reshape(quarter, micro, share).transpose(1, 0, 2)
    moved = to_loader(result, grad_tokens)
    if slabs == 2:
        slab = quarter // 2
        mine = jnp.concatenate([summed, grad_qkv[:slab], grad_qkv[slab:]], 1)
        other = swap(mine, "dp")
        moved, summed = tie(moved, summed)
        part = jnp.reshape(me, (1,)).astype(jnp.int32)
        sum_inner, sum_outer, sum_output, sum_vectors, *sum_qkv = open_shards(part, mine, other, hidden_cols, quarter)
    settled = settle(moved)
    final_out, final_grad = shape(settled[:quarter]), shape(settled[quarter:])
    return (
        final_out, final_grad, *sum_qkv,
        sum_output, sum_inner, sum_outer, sum_vectors[0], sum_vectors[1], sum_vectors[2], sum_vectors[3],
    )


def solution(mesh):
    dp, row, col = (mesh.shape[a] for a in ("dp", "row", "col"))
    fine = Mesh(mesh.devices.reshape(dp, 2, row // 2, col), ("dp", "ya", "yb", "col"))
    tokens, matrix = P(None, ROWS, ("dp", "col")), P(ROWS, "col")
    weights = (matrix, matrix, matrix, P("col", ROWS), matrix, matrix, P(ROWS), P(ROWS), P(ROWS), P(ROWS))
    return jax.shard_map(
        body,
        mesh=fine,
        in_specs=(tokens, tokens, P("dp", None), P(None, ("dp", "col"))) + weights,
        out_specs=(tokens, tokens) + weights,
        check_vma=False,
    )
```

```python
import jax
import jax.numpy as jnp
from jax import lax
from jax.experimental import pallas as pl
from jax.experimental.pallas import tpu as pltpu
from jax.sharding import Mesh, PartitionSpec as P

DH = 64
EPSILON = 1e-05
MASKED = -1e30
LOG2E = 1.4426950408889634
SWAP = ((0, 1), (1, 0))
ROWS = ("ya", "yb")
SHARDS = ("ya", "yb", "col")
bf16 = jnp.bfloat16
f32 = jnp.float32


def cost(microseconds):
    return pl.CostEstimate(flops=int(microseconds * 1e9), bytes_accessed=int(microseconds * 3e6), transcendentals=0)


def contract(left, right, dims):
    return lax.dot_general(left, right, ((dims[:1], dims[1:]), ((), ())), preferred_element_type=f32)


def swap(values, axis):
    return lax.ppermute(values, axis, SWAP)


def gather_rows(values):
    first, second = lax.axis_index("ya") == 0, lax.axis_index("yb") == 0
    other = swap(values, "ya")
    pair = jnp.stack([jnp.where(first, values, other), jnp.where(first, other, values)])
    twin = swap(pair, "yb")
    both = jnp.stack([jnp.where(second, pair, twin), jnp.where(second, twin, pair)], 1)
    return both.reshape((4,) + values.shape)


def spread_dp(values):
    if lax.axis_size("dp") == 2:
        other = swap(values, "dp")
        first = lax.axis_index("dp") == 0
        return jnp.stack([jnp.where(first, values, other), jnp.where(first, other, values)])
    return lax.all_gather(values, "dp", axis=0)


def widen(table, lanes):
    return jnp.concatenate([table] * (lanes // table.shape[1]), 1)


def turn(values, cosine, sine):
    lanes = values.shape[1]
    even = lax.broadcasted_iota(jnp.int32, values.shape, 1) % 2 == 0
    swapped = jnp.where(even, pltpu.roll(values, lanes - 1, 1), pltpu.roll(values, 1, 1))
    return values * widen(cosine, lanes) + swapped * widen(sine, lanes)


def project_kernel(blocks, *refs):
    x_refs, (w_ref, cos_ref, sin_ref) = refs[:blocks], refs[blocks : blocks + 3]
    q_ref, kv_ref, turned_ref = refs[-3:]
    width = turned_ref.shape[1]
    for index, x_ref in enumerate(x_refs):
        wide = jnp.dot(x_ref[...], w_ref[...], preferred_element_type=f32)
        turned = turn(wide[:, : 2 * width], cos_ref[index], sin_ref[index])
        parts = turned[:, :width], turned[:, width:], wide[:, 2 * width :]
        for ref, place, part in ((q_ref, index, parts[0]), (kv_ref, index, parts[1]), (kv_ref, blocks + index, parts[2])):
            ref[place] = jnp.concatenate([part, jnp.zeros((part.shape[0], ref.shape[2] - width), f32)], 1).astype(bf16)
        turned_ref[index] = parts[1].T.astype(bf16)
        turned_ref[blocks + index] = parts[2].T.astype(bf16)


def project(blocks, weight, cosine, sine):
    own, width, count = blocks[0].shape[0], weight.shape[1] // 3, len(blocks)
    padded = -(-width // 128) * 128
    return pl.pallas_call(
        lambda *refs: project_kernel(count, *refs),
        out_shape=[
            jax.ShapeDtypeStruct((count, own, padded), bf16),
            jax.ShapeDtypeStruct((2 * count, own, padded), bf16),
            jax.ShapeDtypeStruct((2 * count, width, own), bf16),
        ],
        compiler_params=pltpu.CompilerParams(vmem_limit_bytes=60 << 20),
        cost_estimate=cost(0.001),
        name="project",
    )(*blocks, weight, cosine, sine)


def head_rows(values, head):
    rows = lax.broadcasted_iota(jnp.int32, values.shape, 0)
    return jnp.where((rows >= head * DH) & (rows < (head + 1) * DH), values, jnp.zeros_like(values))


def head_lanes(values, head):
    lanes = lax.broadcasted_iota(jnp.int32, values.shape, 1)
    return jnp.where((lanes >= head * DH) & (lanes < (head + 1) * DH), values, jnp.zeros_like(values))


def block_sides(info_ref, query_block, key_block, columns, share, own):
    boundary, half, column = info_ref[0], info_ref[1], info_ref[2]
    place = lambda block: jnp.where(column >= block, column - block, column - block + columns) * share
    low_q = place(query_block) + half * own
    low_k = place(key_block)
    first_q, second_q = low_q < boundary, low_q + own > boundary
    first_k, second_k = low_k < boundary, low_k + share > boundary
    meets = (first_q & first_k) | (second_q & second_k)
    mixed = (first_q & second_q) | (first_k & second_k)
    side_q = low_q + lax.broadcasted_iota(jnp.int32, (1, own), 1) >= boundary
    rows = lax.broadcasted_iota(jnp.int32, (share, 1), 0)
    shift = jnp.where(rows < own, half * own, (1 - half) * own - own)
    side_k = low_k + rows + shift >= boundary
    return meets, mixed, side_q.astype(f32), side_k.astype(f32)


def visit_blocks(info_ref, query_block, columns, share, own, visit):
    def step(key_block, carry):
        meets, mixed, side_q, side_k = block_sides(info_ref, query_block, key_block, columns, share, own)

        @pl.when(meets & mixed)
        def _():
            visit(key_block, side_q == side_k)

        @pl.when(meets & jnp.logical_not(mixed))
        def _():
            visit(key_block, None)

        return carry

    lax.fori_loop(0, columns, step, 0)


def forward_kernel(first, share, info_ref, q_ref, k0_ref, k1_ref, vt0_ref, vt1_ref, *refs):
    columns, own, _ = k0_ref.shape
    width = vt0_ref.shape[1]
    heads = width // DH
    count = (len(refs) - 4) // 2
    outs, lses, (parts, top, total, sums) = refs[:count], refs[count : 2 * count], refs[2 * count :]
    scaling = DH ** (-0.5) * LOG2E

    def visit(key_block, same):
        keys = jnp.concatenate([k0_ref[key_block], k1_ref[key_block]], 0)
        values = jnp.concatenate([vt0_ref[key_block], vt1_ref[key_block]], 1)
        scores = [contract(keys, parts[head], (1, 1)) * scaling for head in range(heads)]
        if same is not None:
            scores = [jnp.where(same, each, MASKED) for each in scores]
        before = top[...]
        highest = jnp.maximum(before, jnp.concatenate([jnp.max(each, 0, keepdims=True) for each in scores], 0))
        fade = jnp.exp2(before - highest)
        raised = [jnp.exp2(each - highest[head : head + 1]) for head, each in enumerate(scores)]
        if same is not None:
            raised = [jnp.where(same, each, 0.0) for each in raised]
        top[...] = highest
        total[...] = total[...] * fade + jnp.concatenate([jnp.sum(each, 0, keepdims=True) for each in raised], 0)
        products = [
            jnp.dot(values[head * DH : (head + 1) * DH], each.astype(bf16), preferred_element_type=f32)
            for head, each in enumerate(raised)
        ]
        fades = [jnp.broadcast_to(fade[head : head + 1], (DH, fade.shape[1])) for head in range(heads)]
        sums[...] = sums[...] * jnp.concatenate(fades, 0) + jnp.concatenate(products, 0)

    for index in range(count):
        for head in range(heads):
            parts[head] = head_lanes(q_ref[first + index], head)
        top[...] = jnp.full_like(top, MASKED)
        total[...] = jnp.zeros_like(total)
        sums[...] = jnp.zeros_like(sums)
        visit_blocks(info_ref, first + index, columns, share, own, visit)
        for head in range(heads):
            rows = pl.ds(head * DH, DH)
            line = pl.ds(head, 1)
            outs[index][rows, :] = (sums[rows, :] / total[line, :]).astype(bf16)
            lses[index][line, :] = top[line, :] + jnp.log2(total[line, :])


def attend_forward(first, count, info, q, kv, kv_twin, turned, turned_twin, share):
    columns, own, padded = q.shape
    width = turned.shape[1]
    heads = width // DH
    keys = pl.BlockSpec((columns, own, padded), lambda i, s: (0, 0, 0))
    values = pl.BlockSpec((columns, width, own), lambda i, s: (1, 0, 0))
    flat = lambda rows: pl.BlockSpec((rows, own), lambda i, s: (0, 0))
    outs = pl.pallas_call(
        lambda *refs: forward_kernel(first, share, *refs),
        grid_spec=pltpu.PrefetchScalarGridSpec(
            num_scalar_prefetch=1,
            grid=(1,),
            in_specs=[keys, keys, keys, values, values],
            out_specs=[flat(width)] * count + [flat(heads)] * count,
            scratch_shapes=[
                pltpu.VMEM((heads, own, padded), bf16),
                pltpu.VMEM((heads, own), f32),
                pltpu.VMEM((heads, own), f32),
                pltpu.VMEM((width, own), f32),
            ],
        ),
        out_shape=[jax.ShapeDtypeStruct((width, own), bf16)] * count + [jax.ShapeDtypeStruct((heads, own), f32)] * count,
        compiler_params=pltpu.CompilerParams(vmem_limit_bytes=60 << 20),
        cost_estimate=cost(0.001),
        name="attend_forward",
    )(info, q, kv, kv_twin, turned, turned_twin)
    return outs[:count], outs[count:]


def backward_kernel(columns, share, info_ref, q_ref, kv0_ref, kv1_ref, kt0_ref, kt1_ref, *refs):
    grads, outs, lses, refs = refs[0], refs[1 : columns + 1], refs[columns + 1 : 2 * columns + 1], refs[2 * columns + 1 :]
    dq_ref, near_ref, *fars, part_q, part_g, delta, lse, sum_q, sum_k, sum_v = refs
    own, width = q_ref.shape[1], kt0_ref.shape[1]
    heads = width // DH
    scaling = DH ** (-0.5)
    sum_k[...] = jnp.zeros_like(sum_k)
    sum_v[...] = jnp.zeros_like(sum_v)
    for block in range(columns):
        lse[block] = lses[block][...]
        column = info_ref[2] - block
        grad = grads[jnp.where(column < 0, column + columns, column)]
        spare = jnp.zeros((part_g.shape[1] - width, own), bf16)
        product = grad.astype(f32) * outs[block][...].astype(f32)
        for head in range(heads):
            part_q[block, pl.ds(head * own, own), :] = head_lanes(q_ref[block], head)
            part_g[block, :, pl.ds(head * own, own)] = jnp.concatenate([head_rows(grad, head), spare], 0)
            delta[block, pl.ds(head, 1), :] = jnp.sum(product[head * DH : (head + 1) * DH], 0, keepdims=True)

    def query_step(block, carry):
        sum_q[...] = jnp.zeros_like(sum_q)

        def visit(key_block, same):
            keys = jnp.concatenate([kv0_ref[key_block], kv1_ref[key_block]], 0)
            turned = jnp.concatenate([kt0_ref[key_block], kt1_ref[key_block]], 1)
            values = jnp.concatenate([kv0_ref[columns + key_block], kv1_ref[columns + key_block]], 0)
            all_probs, all_grads = [], []
            for head in range(heads):
                span = pl.ds(head * own, own)
                scores = contract(keys, part_q[block, span, :], (1, 1)) * (scaling * LOG2E)
                probs = jnp.exp2(scores - lse[block, pl.ds(head, 1), :])
                if same is not None:
                    probs = jnp.where(same, probs, 0.0)
                slopes = jnp.dot(values, part_g[block, :, span], preferred_element_type=f32)
                grads = (probs * (slopes - delta[block, pl.ds(head, 1), :])).astype(bf16)
                all_probs.append(probs.astype(bf16))
                all_grads.append(grads)
            for head in range(heads):
                rows = pl.ds(head * DH, DH)
                part = turned[head * DH : (head + 1) * DH]
                sum_q[rows, :] += jnp.dot(part, all_grads[head], preferred_element_type=f32)
            sum_v[key_block] += contract(jnp.concatenate(all_probs, 1), part_g[block], (1, 1))
            sum_k[key_block] += jnp.dot(jnp.concatenate(all_grads, 1), part_q[block], preferred_element_type=f32)

        visit_blocks(info_ref, block, columns, share, own, visit)
        dq_ref[block] = sum_q[...].T * scaling
        return carry

    lax.fori_loop(0, columns, query_step, 0)
    for block in range(columns):
        for place, sums, far_ref in ((block, sum_k, fars[0]), (columns + block, sum_v, fars[1])):
            near_ref[place] = sums[block, :own].astype(bf16)
            far_ref[block] = sums[block, own:].astype(bf16)


def attend_backward(info, q, kv, kv_twin, turned, turned_twin, grads, outs, lses, share):
    columns, own, padded = q.shape
    width = turned.shape[1]
    heads = width // DH
    vmem = pl.BlockSpec(memory_space=pltpu.VMEM)
    operands = [q, kv, kv_twin, turned, turned_twin, grads, *outs, *lses]
    return pl.pallas_call(
        lambda *refs: backward_kernel(columns, share, *refs),
        in_specs=[pl.BlockSpec(memory_space=pltpu.SMEM)] + [vmem] * len(operands),
        out_specs=[vmem] * 4,
        out_shape=[jax.ShapeDtypeStruct((columns, own, width), f32)]
        + [jax.ShapeDtypeStruct((many, own, padded), bf16) for many in (2 * columns, columns, columns)],
        scratch_shapes=[
            pltpu.VMEM((columns, heads * own, padded), bf16),
            pltpu.VMEM((columns, padded, heads * own), bf16),
            pltpu.VMEM((columns, heads, own), f32),
            pltpu.VMEM((columns, heads, own), f32),
            pltpu.VMEM((width, own), f32),
            pltpu.VMEM((columns, share, padded), f32),
            pltpu.VMEM((columns, share, padded), f32),
        ],
        compiler_params=pltpu.CompilerParams(vmem_limit_bytes=48 << 20),
        cost_estimate=cost(0.001),
        name="attend_backward",
    )(info, *operands)


def unproject_kernel(info_ref, dq_ref, near_k_ref, far_k_ref, near_v_ref, far_v_ref, w_ref, cos_ref, sin_ref, part_ref, low_ref):
    width = dq_ref.shape[2]
    lanes = 2 * width
    even = lax.broadcasted_iota(jnp.int32, (dq_ref.shape[1], lanes), 1) % 2 == 0
    dk = (near_k_ref[0, :, :width].astype(f32) + far_k_ref[0, :, :width].astype(f32)) * DH ** (-0.5)
    dv = near_v_ref[0, :, :width].astype(f32) + far_v_ref[0, :, :width].astype(f32)
    both = jnp.concatenate([dq_ref[0], dk], 1)
    swapped = jnp.where(even, pltpu.roll(both, lanes - 1, 1), pltpu.roll(both, 1, 1))
    both = both * widen(cos_ref[0], lanes) - swapped * widen(sin_ref[0], lanes)
    low = jnp.concatenate([both, dv], 1).astype(bf16)
    low_ref[0] = low
    part_ref[0] = contract(low, w_ref[...], (1, 1)).astype(bf16)


def unproject(info, dq, near, far_k, far_v, weight, cosine, sine):
    columns, own, width = dq.shape
    feature = weight.shape[0]
    block = lambda a, first: pl.BlockSpec((1,) + a.shape[1:], lambda i, s: (first + i, 0, 0))
    whole = lambda a: pl.BlockSpec(a.shape, lambda i, s: (0, 0))
    place = lambda i, s: (jnp.where(s[2] >= i, s[2] - i, s[2] - i + columns), 0, 0)
    low = jax.ShapeDtypeStruct((columns, own, weight.shape[1]), bf16)
    return pl.pallas_call(
        unproject_kernel,
        grid_spec=pltpu.PrefetchScalarGridSpec(
            num_scalar_prefetch=1,
            grid=(columns,),
            in_specs=[block(dq, 0), block(near, 0), block(far_k, 0), block(near, columns), block(far_v, 0), whole(weight)]
            + [block(cosine, 0), block(sine, 0)],
            out_specs=[pl.BlockSpec((1, own, feature), place), block(low, 0)],
        ),
        out_shape=[jax.ShapeDtypeStruct((columns, own, feature), bf16), low],
        compiler_params=pltpu.CompilerParams(vmem_limit_bytes=40 << 20),
        cost_estimate=cost(0.001),
        name="unproject",
    )(info, dq, near, far_k, near, far_v, weight, cosine, sine)


def project_grad_kernel(low_ref, *refs):
    x_refs, (grad_ref,) = refs[:-1], refs[-1:]
    total = None
    for block, x_ref in enumerate(x_refs):
        piece = contract(x_ref[...], low_ref[block], (0, 0))
        total = piece if total is None else total + piece
    grad_ref[...] = total.astype(bf16)


def project_grad(low, blocks):
    return pl.pallas_call(
        project_grad_kernel,
        out_shape=jax.ShapeDtypeStruct((blocks[0].shape[1], low.shape[2]), bf16),
        compiler_params=pltpu.CompilerParams(vmem_limit_bytes=40 << 20),
        cost_estimate=cost(0.001),
        name="project_grad",
    )(low, *blocks)


def mean_lanes(values):
    return jnp.sum(values, 1, keepdims=True) * (1.0 / values.shape[1])


def norm_forward(values, gain, shift):
    centred = values - mean_lanes(values)
    inverse = lax.rsqrt(mean_lanes(centred * centred) + EPSILON)
    normed = centred * inverse
    return normed * gain + shift, normed, inverse


def norm_backward(grad, normed, inverse, gain):
    scaled = grad * gain
    return inverse * (scaled - mean_lanes(scaled) - normed * mean_lanes(scaled * normed))


def unit(size):
    rows = lax.broadcasted_iota(jnp.int32, (size, size), 0)
    return (rows == lax.broadcasted_iota(jnp.int32, (size, size), 1)).astype(bf16)


def feed_kernel(info_ref, x_ref, cot_ref, w_ref, *refs):
    parts, _, columns, slab, _ = w_ref.shape
    att_refs, refs = refs[:columns], refs[columns:]
    result_ref, grad_att_ref, grad_one_ref, hidden_ref, act_out, gin_out, gtwo_ref, gone_ref, sums_ref, sent_ref, *refs = refs
    w, slopes, outer, act_ref, gin_ref, stage, sems, ends = refs
    rows, columns, quarter, _ = w.shape
    act_copy = pltpu.make_async_copy(act_ref, act_out, ends.at[0])
    gin_copy = pltpu.make_async_copy(gin_ref, gin_out, ends.at[1])

    def turned(step):
        column = info_ref[2] + step
        return jnp.where(column >= columns, column - columns, column)

    hidden_cols = act_ref.shape[2]
    both = 2 * hidden_cols
    spans = ((0, hidden_cols), (hidden_cols, hidden_cols), (both, w.shape[3] - both))

    def copies(kind):
        lanes = pl.ds(*spans[kind])
        for part in range(parts):
            target = w.at[:, :, pl.ds(part * slab, slab), lanes]
            yield pltpu.make_async_copy(w_ref.at[part, :, :, :, lanes], target, sems.at[kind, part])

    def wait(kind):
        for each in copies(kind):
            each.wait()

    for kind in (2, 0, 1):
        for each in copies(kind):
            each.start()

    def block(kind, column):
        lanes = pl.ds(*spans[kind])
        return jnp.concatenate([w[row, column, :, lanes] for row in range(rows)], 0)

    wait(2)
    mix = pl.ds(both, quarter)
    attended = jnp.concatenate([ref[...] for ref in att_refs], 0)
    branch = []
    for row in range(rows):
        weight = jnp.concatenate([w[row, turned(step), :, mix] for step in range(columns)], 0)
        branch.append(contract(attended, weight, (0, 0)))
    branch = jnp.concatenate(branch, 1)
    eye = unit(quarter)
    small = [contract(w[row, 0, :, pl.ds(both + quarter, 12)], eye, (0, 0)) for row in range(rows)]
    small = jnp.concatenate(small, 1)
    vectors = small[0:4] + (small[4:8] + small[8:12])
    gain_one, shift_one, gain_two, shift_two = (vectors[i : i + 1] for i in range(4))

    hidden, normed_one, inverse_one = norm_forward(x_ref[...].astype(f32) + branch, gain_one, shift_one)
    low = hidden.astype(bf16)
    hidden_ref[...] = low.T
    outer[...] = jnp.zeros_like(outer)

    wait(0)

    def forward(column, carry):
        inner = jnp.dot(low, block(0, column), preferred_element_type=f32)
        cumulative = 0.5 * (1.0 + lax.erf(inner * (0.5**0.5)))
        slopes[column] = cumulative + inner * (jnp.exp(-0.5 * inner * inner) * 0.3989422804014327)
        act_ref[column] = (inner * cumulative).astype(bf16)
        return carry

    lax.fori_loop(0, columns, forward, 0)
    act_copy.start()
    wait(1)

    def combine(column, carry):
        outer[...] += contract(act_ref[column], block(1, column), (1, 1))
        return carry

    lax.fori_loop(0, columns, combine, 0)
    result, normed_two, inverse_two = norm_forward(hidden + outer[...], gain_two, shift_two)
    result_ref[...] = result.astype(bf16)
    cot = cot_ref[...].astype(f32)
    grad_two = norm_backward(cot, normed_two, inverse_two, gain_two)
    grad_two_low = grad_two.astype(bf16)
    gtwo_ref[...] = grad_two_low.T
    outer[...] = grad_two

    def backward(column, carry):
        grad = jnp.dot(grad_two_low, block(1, column), preferred_element_type=f32)
        gin_ref[column] = (grad * slopes[column]).astype(bf16)
        outer[...] += contract(gin_ref[column], block(0, column), (1, 1))
        return carry

    lax.fori_loop(0, columns, backward, 0)
    gin_copy.start()
    grad_hidden = outer[...]
    grad_one = norm_backward(grad_hidden, normed_one, inverse_one, gain_one)
    grad_one_ref[...] = grad_one
    grad_one_low = grad_one.astype(bf16)
    for step in range(columns):
        weight = jnp.concatenate([w[row, turned(step), :, mix] for row in range(rows)], 1)
        grad_att_ref[turned(step)] = contract(weight, grad_one_low, (1, 1)).astype(bf16)
    sums = [jnp.sum(a, 0, keepdims=True) for a in (grad_hidden * normed_one, grad_hidden, cot * normed_two, cot)]
    sums = jnp.concatenate(sums, 0)
    for row in range(rows):
        mine = slice(row * quarter, (row + 1) * quarter)
        gone_ref[row] = grad_one_low[:, mine]
        sums_ref[row] = sums[:, mine].astype(bf16)

    copies_out = []
    for column in range(columns):
        slot = column % 2
        if column > 1:
            copies_out[column - 2].wait()
        attended = attended_block(info_ref, att_refs, column)
        operands = attended, act_ref[column], gin_ref[column], hidden_ref, gtwo_ref, gone_ref, sums_ref
        weigh_block(1 - info_ref[1], info_ref, *operands, stage.at[slot])
        copies_out.append(pltpu.make_async_copy(stage.at[slot], sent_ref.at[:, :, column], ends.at[2 + slot]))
        copies_out[-1].start()
    for copy in copies_out[-2:] + [act_copy, gin_copy]:
        copy.wait()


def feed(info, attended, tokens, cot, weights, slabs):
    own, feature = tokens.shape
    parts, rows, columns, slab, lanes = weights.shape
    quarter = parts * slab
    hidden_cols = feature
    vmem, smem = pl.BlockSpec(memory_space=pltpu.VMEM), pl.BlockSpec(memory_space=pltpu.SMEM)
    hbm = pl.BlockSpec(memory_space=pltpu.HBM)
    wide = jax.ShapeDtypeStruct((columns, own, hidden_cols), bf16)
    flat = lambda kind: jax.ShapeDtypeStruct((own, feature), kind)
    tall = jax.ShapeDtypeStruct((feature, own), bf16)
    return pl.pallas_call(
        feed_kernel,
        in_specs=[smem, vmem, vmem, pl.BlockSpec(memory_space=pltpu.HBM)] + [vmem] * columns,
        out_specs=[vmem] * 4 + [hbm] * 2 + [vmem] * 3 + [hbm],
        out_shape=[
            flat(bf16), jax.ShapeDtypeStruct((columns, quarter, own), bf16), flat(f32), tall, wide, wide, tall,
            jax.ShapeDtypeStruct((rows, own, quarter), bf16), jax.ShapeDtypeStruct((rows, 4, quarter), bf16),
            jax.ShapeDtypeStruct((2, slabs, columns, quarter // slabs, lanes), bf16),
        ],
        scratch_shapes=[
            pltpu.VMEM((rows, columns, quarter, lanes), bf16),
            pltpu.VMEM((columns, own, hidden_cols), f32),
            pltpu.VMEM((own, feature), f32),
            pltpu.VMEM(wide.shape, bf16),
            pltpu.VMEM(wide.shape, bf16),
            pltpu.VMEM((2, 2, slabs, quarter // slabs, lanes), bf16),
            pltpu.SemaphoreType.DMA((3, parts)),
            pltpu.SemaphoreType.DMA((4,)),
        ],
        compiler_params=pltpu.CompilerParams(vmem_limit_bytes=60 << 20),
        cost_estimate=cost(0.001),
        name="feed",
    )(info, tokens, cot, weights, *attended)


def weigh_block(core, info_ref, attended, act, gin, hidden_ref, gtwo_ref, gone_ref, sums_ref, out):
    _, slabs, slab, lanes = out.shape
    quarter = slabs * slab
    hidden_cols = act.shape[1]
    eye = unit(quarter)
    away = lambda index, mine: jnp.where(index == mine, 0, 1)
    rows = [2 * pair + core for pair in range(2)]
    spans = [pl.ds(pl.multiple_of(row * quarter, quarter), quarter) for row in rows]
    both = lambda ref: jnp.concatenate([ref[span, :] for span in spans], 0)
    inner = jnp.dot(both(hidden_ref), gin, preferred_element_type=f32).astype(bf16)
    outer = jnp.dot(both(gtwo_ref), act, preferred_element_type=f32).astype(bf16)
    for pair, row in enumerate(rows):
        mixed = jnp.dot(attended, gone_ref[row], preferred_element_type=f32).astype(bf16)
        vector = contract(eye, sums_ref[row], (1, 1)).astype(bf16)
        rest = jnp.zeros((quarter, lanes - 2 * hidden_cols - quarter - 4), bf16)
        tail = jnp.concatenate([mixed, vector, rest], 1)
        far = away(pair, info_ref[3])
        for part in range(slabs):
            place = away(part, info_ref[4]) if slabs > 1 else 0
            low = pair * quarter + part * slab
            out[far, place, :, 0:hidden_cols] = inner[low : low + slab]
            out[far, place, :, hidden_cols : 2 * hidden_cols] = outer[low : low + slab]
            out[far, place, :, 2 * hidden_cols :] = tail[part * slab : (part + 1) * slab]


def attended_block(info_ref, att_refs, column):
    step = column - info_ref[2]
    step = jnp.where(step < 0, step + len(att_refs), step)
    attended = att_refs[0][...]
    for index in range(1, len(att_refs)):
        attended = jnp.where(step == index, att_refs[index][...], attended)
    return attended


def weigh_kernel(info_ref, hidden_ref, act_ref, gin_ref, gtwo_ref, gone_ref, sums_ref, *refs):
    att_refs, out_ref = refs[:-1], refs[-1]
    attended = attended_block(info_ref, att_refs, pl.program_id(0))
    operands = attended, act_ref[0], gin_ref[0], hidden_ref, gtwo_ref, gone_ref, sums_ref
    weigh_block(info_ref[1], info_ref, *operands, out_ref.at[:, :, 0])


def weigh(info, attended, hidden, act, gin, gtwo, gone, sums, lanes, slabs):
    columns = act.shape[0]
    quarter = attended[0].shape[0]
    whole = lambda a: pl.BlockSpec(a.shape, lambda i, s: (0,) * a.ndim)
    piece = pl.BlockSpec((1,) + act.shape[1:], lambda i, s: (i, 0, 0))
    slab = quarter // slabs
    return pl.pallas_call(
        weigh_kernel,
        grid_spec=pltpu.PrefetchScalarGridSpec(
            num_scalar_prefetch=1,
            grid=(columns,),
            in_specs=[whole(hidden), piece, piece, whole(gtwo), whole(gone), whole(sums)] + [whole(a) for a in attended],
            out_specs=pl.BlockSpec((2, slabs, 1, slab, lanes), lambda i, s: (0, 0, i, 0, 0)),
        ),
        out_shape=jax.ShapeDtypeStruct((2, slabs, columns, slab, lanes), bf16),
        compiler_params=pltpu.CompilerParams(vmem_limit_bytes=60 << 20),
        cost_estimate=cost(0.001),
        name="weigh",
    )(info, hidden, act, gin, gtwo, gone, sums, *attended)


def parcel_kernel(info_ref, inner_ref, outer_ref, output_ref, *refs):
    small_refs, out_ref = refs[:-1], refs[-1]
    columns = inner_ref.shape[1]
    quarter = output_ref.shape[1]
    slab = out_ref.shape[0]
    offset = info_ref[0] * slab if slab < quarter else 0
    rows = pl.ds(pl.multiple_of(offset, slab), slab)
    values = jnp.concatenate([ref[...] for ref in small_refs], 0)
    high = values.astype(bf16)
    rest = values - high.astype(f32)
    middle = rest.astype(bf16)
    last = (rest - middle.astype(f32)).astype(bf16)
    pick = lax.broadcasted_iota(jnp.int32, (slab, quarter), 0) + offset
    pick = (pick == lax.broadcasted_iota(jnp.int32, (slab, quarter), 1)).astype(bf16)
    small = jnp.concatenate([contract(pick, part, (1, 1)) for part in (high, middle, last)], 1).astype(bf16)
    fill = jnp.zeros((slab, out_ref.shape[1] - 2 * columns - quarter - 12), bf16)
    out_ref[:, 0:columns] = inner_ref[rows, :]
    out_ref[:, columns : 2 * columns] = outer_ref[rows, :]
    out_ref[:, 2 * columns :] = jnp.concatenate([output_ref[rows, :], small, fill], 1)


def parcel(part, inner, outer, output, vectors, lanes, slabs):
    vmem, smem = pl.BlockSpec(memory_space=pltpu.VMEM), pl.BlockSpec(memory_space=pltpu.SMEM)
    return pl.pallas_call(
        parcel_kernel,
        in_specs=[smem] + [vmem] * 7,
        out_shape=jax.ShapeDtypeStruct((inner.shape[0] // slabs, lanes), bf16),
        cost_estimate=cost(0.001),
        name="parcel",
    )(part, inner, outer, output, *(v.reshape(1, -1) for v in vectors))


def keep(values, index, axis=0):
    first, second = lax.index_in_dim(values, 0, axis, False), lax.index_in_dim(values, 1, axis, False)
    chosen = index == 0
    return jnp.where(chosen, first, second), jnp.where(chosen, second, first)


def tie(*values):
    return lax.optimization_barrier(values)


def shift(values, step):
    columns = lax.axis_size("col")
    if step % columns == 0:
        return values
    return lax.ppermute(values, "col", [(i, (i + step) % columns) for i in range(columns)])


def add_kernel(count, sums, *refs):
    results, (*sources, buffer, held, sems, ends) = refs[-count - 4 : -4], refs[: -count - 4] + refs[-4:]
    rows, first, number = [], 0, 0
    for index, start, parts in sums:
        row = []
        for which, lead, low, high in parts:
            source = sources[which].at[lead + (pl.ds(low, high - low),)]
            copy = pltpu.make_async_copy(source, buffer.at[pl.ds(first, high - low)], sems.at[number])
            copy.start()
            row.append((first, high - low, copy))
            first, number = first + high - low, number + 1
        rows.append(row)
    copies, first = [], 0
    for place, ((index, start, _), row) in enumerate(zip(sums, rows)):
        size = row[0][1]
        for *_, copy in row:
            copy.wait()
        total = sum(buffer[at : at + size].astype(f32) for at, *_ in row)
        held[first : first + size] = total.astype(bf16)
        target = results[index].at[pl.ds(start, size)]
        copies.append(pltpu.make_async_copy(held.at[pl.ds(first, size)], target, ends.at[place]))
        copies[-1].start()
        first += size
    for copy in copies:
        copy.wait()


def add_blocks(arrays, lengths, sums):
    hbm = pl.BlockSpec(memory_space=pltpu.HBM)
    tail = arrays[0].shape[-2:]
    parts = [part for *_, each in sums for part in each]
    return pl.pallas_call(
        lambda *refs: add_kernel(len(lengths), sums, *refs),
        in_specs=[hbm] * len(arrays),
        out_specs=[hbm] * len(lengths),
        out_shape=[jax.ShapeDtypeStruct((length,) + tail, bf16) for length in lengths],
        scratch_shapes=[
            pltpu.VMEM((sum(high - low for *_, low, high in parts),) + tail, bf16),
            pltpu.VMEM((sum(lengths),) + tail, bf16),
            pltpu.SemaphoreType.DMA((len(parts),)),
            pltpu.SemaphoreType.DMA((len(sums),)),
        ],
        compiler_params=pltpu.CompilerParams(vmem_limit_bytes=60 << 20),
        cost_estimate=cost(0.001),
        name="add_blocks",
    )(*arrays)


def open_kernel(hidden_cols, part_ref, mine_ref, other_ref, *outs):
    *outs, sums_ref, query_ref, key_ref, value_ref = outs
    slab, quarter = mine_ref.shape[0], outs[2].shape[1]
    spans = (0, hidden_cols), (hidden_cols, hidden_cols), (2 * hidden_cols, quarter)
    lanes = mine_ref.shape[1] - 6 * quarter

    def write(first, second):
        for (start, size), out in zip(spans, outs):
            out[0:slab, :] = first[:, start : start + size].astype(f32)
            out[slab : 2 * slab, :] = second[:, start : start + size].astype(f32)
        start = 2 * hidden_cols + quarter
        last = jnp.concatenate([first[:, start:lanes], second[:, start:lanes]], 0)
        sums_ref[...] = contract(last[:, 0:4], unit(2 * slab), (0, 0))

    @pl.when(part_ref[0] == 0)
    def _():
        write(mine_ref[...], other_ref[...])

    @pl.when(part_ref[0] != 0)
    def _():
        write(other_ref[...], mine_ref[...])

    total = mine_ref[:, lanes:].astype(f32) + other_ref[:, lanes:].astype(f32)
    for index, ref in enumerate((query_ref, key_ref, value_ref)):
        for half in range(2):
            start = (3 * half + index) * quarter
            ref[half * slab : (half + 1) * slab, :] = total[:, start : start + quarter]


def open_shards(part, mine, other, hidden_cols, quarter):
    vmem, smem = pl.BlockSpec(memory_space=pltpu.VMEM), pl.BlockSpec(memory_space=pltpu.SMEM)
    rows = hidden_cols, hidden_cols, quarter
    shape = lambda *dims: jax.ShapeDtypeStruct(dims, f32)
    return pl.pallas_call(
        lambda *refs: open_kernel(hidden_cols, *refs),
        in_specs=[smem, vmem, vmem],
        out_shape=[shape(quarter, a) for a in rows] + [shape(4, quarter)] + [shape(quarter, quarter)] * 3,
        compiler_params=pltpu.CompilerParams(vmem_limit_bytes=16 << 20),
        cost_estimate=cost(0.001),
        name="open_shards",
    )(part, mine, other)


def sum_shards(kept, sent, mark):
    columns = kept.shape[2]
    middle = columns // 2
    pair = kept, swap(sent, "yb")
    both = lambda lead, low, high: [(0, lead, low, high), (1, lead, low, high)]
    to_dp = [(0, 0, both((1, 1), 0, middle)), (0, middle, both((0, 1), 0, middle))]
    to_ya = [(1, 0, both((1, 1), middle, columns)), (1, middle, both((1, 0), middle, columns))]
    to_dp, to_ya = add_blocks(pair, (columns, columns), to_dp + to_ya)
    mark, to_dp, to_ya = tie(mark, to_dp, to_ya)
    by_dp, by_ya = swap(to_dp, "dp"), swap(to_ya, "ya")

    def sides(mark):
        dp, ya, mark = tie(by_dp, by_ya, mark)
        rest_ya = (0, 0, both((1, 0), 0, middle) + [(2, (), 0, middle)])
        rest_dp = (1, 0, both((0, 1), middle, columns) + [(3, (), 0, middle)])
        rest_ya, rest_dp = add_blocks(pair + (dp, ya), (middle, columns - middle), [rest_ya, rest_dp])
        mark, rest_ya, rest_dp = tie(mark, rest_ya, rest_dp)
        rest_ya, rest_dp = swap(rest_ya, "ya"), swap(rest_dp, "dp")

        def finish(mark):
            low_ya, high_dp, mark = tie(rest_ya, rest_dp, mark)
            low = both((0, 0), 0, middle) + [(2, (), middle, columns), (4, (), 0, middle)]
            high = both((0, 0), middle, columns) + [(3, (), middle, columns), (5, (), 0, columns - middle)]
            (own,) = add_blocks(pair + (dp, ya, low_ya, high_dp), (columns,), [(0, 0, low), (0, middle, high)])
            own, mark = tie(own, mark)
            mine = lax.psum_scatter(own, "col", scatter_dimension=0, tiled=False)
            return mine, mark

        return mark, finish

    return mark, sides


def body(
    inputs, cotangent, lengths, source, query_weight, key_weight, value_weight, output_weight, inner_weight, outer_weight,
    first_gain, first_shift, second_gain, second_shift,
):
    micro, quarter, share = inputs.shape
    dp_count, columns = lax.axis_size("dp"), lax.axis_size("col")
    pack, own = share * columns, share // 2
    feature, count = 4 * quarter, share * micro
    width, hidden_cols = query_weight.shape[1], inner_weight.shape[1]
    lanes = -(-(2 * hidden_cols + quarter + 12) // 128) * 128
    me, m, half, z = (lax.axis_index(a) for a in ("dp", "ya", "yb", "col"))

    boundary = jnp.where(m == 0, lengths[0, 0], lengths[0, 1])
    info = jnp.stack([boundary, half, z, m, me]).astype(jnp.int32)
    slabs = 2 if dp_count == 2 else 1

    vectors = (first_gain, first_shift, second_gain, second_shift)
    anchors = spread_dp(source)
    packed = parcel(jnp.reshape(me, (1,)).astype(jnp.int32), inner_weight, outer_weight, output_weight, vectors, lanes, slabs)
    axes = ("dp",) + SHARDS if slabs == 2 else SHARDS
    everywhere = lax.all_gather(packed, axes, axis=0).reshape(slabs, 4, columns, quarter // slabs, lanes)
    anchor = source.reshape(count)
    place = anchor // (dp_count * pack) * share + anchor % share
    holder = anchor % (dp_count * pack) // pack
    wide_in = spread_dp(inputs)

    steps = jnp.arange(columns, dtype=jnp.int32)
    spots = ((z - steps) % columns * share + half * own)[:, None] + jnp.arange(own, dtype=jnp.int32)[None, :]
    frequency = 10000.0 ** (-2.0 * jnp.arange(DH // 2, dtype=f32) / DH)
    angles = (spots - jnp.where(spots >= boundary, boundary, 0)).astype(f32)[..., None] * jnp.tile(jnp.repeat(frequency, 2), 2)
    signs = jnp.where(jnp.arange(2 * DH) % 2 == 0, -1.0, 1.0)
    cosine, sine = jnp.cos(angles), jnp.sin(angles) * signs
    wide_in, cosine, sine = tie(wide_in, cosine, sine)

    if dp_count == 2:
        pick = (holder * count + place)[:, None] == jnp.arange(dp_count * count, dtype=jnp.int32)[None, :]
        pick = pick.astype(bf16).reshape(count, dp_count, micro, share)
        deal = lambda wide: jnp.einsum("tsmj,smfj->tf", pick, wide, preferred_element_type=f32).astype(bf16)
    else:
        deal = lambda wide: wide.transpose(0, 1, 3, 2).reshape(-1, quarter)[holder * count + place]

    def to_tokens(dealt):
        return lax.all_to_all(dealt.reshape(4, own, quarter), ROWS, split_axis=0, concat_axis=0, tiled=True)

    dealt = deal(wide_in)
    cotangent, dealt = tie(cotangent, dealt)
    tokens = to_tokens(dealt).transpose(1, 0, 2).reshape(own, feature)
    wide_cot, tokens = tie(spread_dp(cotangent), tokens)
    blocks = [shift(tokens, step) for step in range(columns)]
    cot = to_tokens(deal(wide_cot)).transpose(1, 0, 2).reshape(own, feature)
    qkv_weight = jnp.concatenate([query_weight, key_weight, value_weight], 1)
    qkv_weight = gather_rows(qkv_weight).reshape(feature, -1)

    blocks[-1], cot, anchors = tie(blocks[-1], cot, anchors)
    q, kv, turned = project(blocks, qkv_weight, cosine, sine)
    kv_twin, turned_twin = swap(kv, "yb"), swap(turned, "yb")
    mixed, lses = attend_forward(1, columns - 1, info, q, kv, kv_twin, turned, turned_twin, share)
    q, mixed = tie(q, mixed)
    last = attend_forward(0, 1, info, q, kv, kv_twin, turned, turned_twin, share)
    mixed, lses = last[0] + mixed, last[1] + lses
    attended = [shift(mixed[step], -step) for step in range(columns)]

    result, grad_att, grad_one, *pieces, sent = feed(info, attended, tokens, cot, everywhere, slabs)
    grad_att = lax.all_to_all(grad_att, "col", split_axis=0, concat_axis=0, tiled=True)
    def to_loader(*rows):
        cut = jnp.concatenate([a.astype(bf16).reshape(own, 4, quarter).transpose(1, 0, 2) for a in rows], 2)
        cut = jnp.broadcast_to(cut[None], (dp_count,) + cut.shape).reshape(dp_count * 4, own, -1)
        moved = lax.all_to_all(cut, ("dp",) + ROWS, split_axis=0, concat_axis=0, tiled=True)
        return moved.reshape(-1, len(rows) * quarter)

    spot = jnp.arange(count, dtype=jnp.int32)
    wanted = spot // share * (dp_count * pack) + me * pack + z * share + spot % share
    if dp_count == 2:
        put = (anchors.reshape(-1)[:, None] == wanted[None, :]).astype(bf16)
        settle = lambda wide: contract(wide, put, (0, 0)).astype(bf16)
    else:
        order = jnp.argsort(anchors.reshape(-1))
        spots_in = jnp.searchsorted(anchors.reshape(-1)[order], wanted)
        settle = lambda wide: wide[order[spots_in]].T
    kept = weigh(info, attended, *pieces, lanes, slabs)
    if slabs == 2:
        grad_att, sides = sum_shards(kept, sent, grad_att)
    else:
        flip = lambda a, index, axis: jnp.where(index == 0, a, jnp.flip(a, axis))
        cut = flip(flip(jnp.stack([kept, sent], 1), m, 0), half, 1).reshape(4 * columns, quarter, lanes)
        summed = lax.psum_scatter(cut, SHARDS, scatter_dimension=0, tiled=False)
        summed = lax.psum(summed, "dp").astype(f32)

    dq, near, *far = attend_backward(info, q, kv, kv_twin, turned, turned_twin, grad_att, mixed, lses, share)
    partial, low = unproject(info, dq, near, *(swap(each, "yb") for each in far), qkv_weight, cosine, sine)
    if slabs == 2:
        low, finish = sides(low)
    grad_qkv = project_grad(low, blocks)
    partial = lax.all_to_all(partial, "col", split_axis=0, concat_axis=0, tiled=True)
    grad_tokens = grad_one + jnp.sum(partial.astype(f32), 0)

    def over_dp(values):
        if dp_count == 2:
            return values.astype(f32) + swap(values, "dp").astype(f32)
        return lax.psum(values, "dp").astype(f32)

    def halve(grad, axis, index, place_axis):
        kept, sent = keep(grad, index, place_axis)
        return (kept.astype(f32) + swap(sent, axis).astype(f32)).astype(bf16)

    if slabs == 2:
        summed, grad_qkv = finish(grad_qkv)
    grad_qkv = halve(grad_qkv.reshape(2, 2, quarter, 3 * width), "yb", half, 1)
    grad_qkv = halve(grad_qkv, "ya", m, 0)
    grad_tokens, grad_qkv = tie(grad_tokens, grad_qkv)
    if slabs == 1:
        grad_qkv = over_dp(grad_qkv)
        sum_qkv = [grad_qkv[:, i * width : (i + 1) * width] for i in range(3)]
        sum_inner, sum_outer = summed[:, :hidden_cols], summed[:, hidden_cols : 2 * hidden_cols]
        sum_output = summed[:, 2 * hidden_cols : 2 * hidden_cols + quarter]
        sum_vectors = summed[:, 2 * hidden_cols + quarter : 2 * hidden_cols + quarter + 4].T

    shape = lambda a: a.reshape(quarter, micro, share).transpose(1, 0, 2)
    moved = to_loader(result, grad_tokens)
    if slabs == 2:
        slab = quarter // 2
        mine = jnp.concatenate([summed, grad_qkv[:slab], grad_qkv[slab:]], 1)
        other = swap(mine, "dp")
        moved, summed = tie(moved, summed)
        part = jnp.reshape(me, (1,)).astype(jnp.int32)
        sum_inner, sum_outer, sum_output, sum_vectors, *sum_qkv = open_shards(part, mine, other, hidden_cols, quarter)
    settled = settle(moved)
    final_out, final_grad = shape(settled[:quarter]), shape(settled[quarter:])
    return (
        final_out, final_grad, *sum_qkv,
        sum_output, sum_inner, sum_outer, sum_vectors[0], sum_vectors[1], sum_vectors[2], sum_vectors[3],
    )


def solution(mesh):
    dp, row, col = (mesh.shape[a] for a in ("dp", "row", "col"))
    fine = Mesh(mesh.devices.reshape(dp, 2, row // 2, col), ("dp", "ya", "yb", "col"))
    tokens, matrix = P(None, ROWS, ("dp", "col")), P(ROWS, "col")
    weights = (matrix, matrix, matrix, P("col", ROWS), matrix, matrix, P(ROWS), P(ROWS), P(ROWS), P(ROWS))
    return jax.shard_map(
        body,
        mesh=fine,
        in_specs=(tokens, tokens, P("dp", None), P(None, ("dp", "col"))) + weights,
        out_specs=(tokens, tokens) + weights,
        check_vma=False,
    )
```

```python
import jax
import jax.numpy as jnp
from jax import lax
from jax.experimental import pallas as pl
from jax.experimental.pallas import tpu as pltpu
from jax.sharding import Mesh, PartitionSpec as P

DH = 64
EPSILON = 1e-05
MASKED = -1e30
LOG2E = 1.4426950408889634
SWAP = ((0, 1), (1, 0))
ROWS = ("ya", "yb")
SHARDS = ("ya", "yb", "col")
bf16 = jnp.bfloat16
f32 = jnp.float32


def cost(microseconds):
    return pl.CostEstimate(flops=int(microseconds * 1e9), bytes_accessed=int(microseconds * 3e6), transcendentals=0)


def contract(left, right, dims):
    return lax.dot_general(left, right, ((dims[:1], dims[1:]), ((), ())), preferred_element_type=f32)


def swap(values, axis):
    return lax.ppermute(values, axis, SWAP)


def gather_rows(values):
    first, second = lax.axis_index("ya") == 0, lax.axis_index("yb") == 0
    other = swap(values, "ya")
    pair = jnp.stack([jnp.where(first, values, other), jnp.where(first, other, values)])
    twin = swap(pair, "yb")
    both = jnp.stack([jnp.where(second, pair, twin), jnp.where(second, twin, pair)], 1)
    return both.reshape((4,) + values.shape)


def spread_dp(values):
    if lax.axis_size("dp") == 2:
        other = swap(values, "dp")
        first = lax.axis_index("dp") == 0
        return jnp.stack([jnp.where(first, values, other), jnp.where(first, other, values)])
    return lax.all_gather(values, "dp", axis=0)


def widen(table, lanes):
    return jnp.concatenate([table] * (lanes // table.shape[1]), 1)


def turn(values, cosine, sine):
    lanes = values.shape[1]
    even = lax.broadcasted_iota(jnp.int32, values.shape, 1) % 2 == 0
    swapped = jnp.where(even, pltpu.roll(values, lanes - 1, 1), pltpu.roll(values, 1, 1))
    return values * widen(cosine, lanes) + swapped * widen(sine, lanes)


def project_kernel(blocks, *refs):
    x_refs, (w_ref, cos_ref, sin_ref) = refs[:blocks], refs[blocks : blocks + 3]
    q_ref, kv_ref, turned_ref = refs[-3:]
    width = turned_ref.shape[1]
    for index, x_ref in enumerate(x_refs):
        wide = jnp.dot(x_ref[...], w_ref[...], preferred_element_type=f32)
        turned = turn(wide[:, : 2 * width], cos_ref[index], sin_ref[index])
        parts = turned[:, :width], turned[:, width:], wide[:, 2 * width :]
        for ref, place, part in ((q_ref, index, parts[0]), (kv_ref, index, parts[1]), (kv_ref, blocks + index, parts[2])):
            ref[place] = jnp.concatenate([part, jnp.zeros((part.shape[0], ref.shape[2] - width), f32)], 1).astype(bf16)
        turned_ref[index] = parts[1].T.astype(bf16)
        turned_ref[blocks + index] = parts[2].T.astype(bf16)


def project(blocks, weight, cosine, sine):
    own, width, count = blocks[0].shape[0], weight.shape[1] // 3, len(blocks)
    padded = -(-width // 128) * 128
    return pl.pallas_call(
        lambda *refs: project_kernel(count, *refs),
        out_shape=[
            jax.ShapeDtypeStruct((count, own, padded), bf16),
            jax.ShapeDtypeStruct((2 * count, own, padded), bf16),
            jax.ShapeDtypeStruct((2 * count, width, own), bf16),
        ],
        compiler_params=pltpu.CompilerParams(vmem_limit_bytes=60 << 20),
        cost_estimate=cost(0.001),
        name="project",
    )(*blocks, weight, cosine, sine)


def head_rows(values, head):
    rows = lax.broadcasted_iota(jnp.int32, values.shape, 0)
    return jnp.where((rows >= head * DH) & (rows < (head + 1) * DH), values, jnp.zeros_like(values))


def head_lanes(values, head):
    lanes = lax.broadcasted_iota(jnp.int32, values.shape, 1)
    return jnp.where((lanes >= head * DH) & (lanes < (head + 1) * DH), values, jnp.zeros_like(values))


def block_sides(info_ref, query_block, key_block, columns, share, own):
    boundary, half, column = info_ref[0], info_ref[1], info_ref[2]
    place = lambda block: jnp.where(column >= block, column - block, column - block + columns) * share
    low_q = place(query_block) + half * own
    low_k = place(key_block)
    first_q, second_q = low_q < boundary, low_q + own > boundary
    first_k, second_k = low_k < boundary, low_k + share > boundary
    meets = (first_q & first_k) | (second_q & second_k)
    mixed = (first_q & second_q) | (first_k & second_k)
    side_q = low_q + lax.broadcasted_iota(jnp.int32, (1, own), 1) >= boundary
    rows = lax.broadcasted_iota(jnp.int32, (share, 1), 0)
    shift = jnp.where(rows < own, half * own, (1 - half) * own - own)
    side_k = low_k + rows + shift >= boundary
    return meets, mixed, side_q.astype(f32), side_k.astype(f32)


def visit_blocks(info_ref, query_block, columns, share, own, visit):
    def step(key_block, carry):
        meets, mixed, side_q, side_k = block_sides(info_ref, query_block, key_block, columns, share, own)

        @pl.when(meets & mixed)
        def _():
            visit(key_block, side_q == side_k)

        @pl.when(meets & jnp.logical_not(mixed))
        def _():
            visit(key_block, None)

        return carry

    lax.fori_loop(0, columns, step, 0)


def forward_kernel(first, share, info_ref, q_ref, k0_ref, k1_ref, vt0_ref, vt1_ref, *refs):
    columns, own, _ = k0_ref.shape
    width = vt0_ref.shape[1]
    heads = width // DH
    count = (len(refs) - 4) // 2
    outs, lses, (parts, top, total, sums) = refs[:count], refs[count : 2 * count], refs[2 * count :]
    scaling = DH ** (-0.5) * LOG2E

    def visit(key_block, same):
        keys = jnp.concatenate([k0_ref[key_block], k1_ref[key_block]], 0)
        values = jnp.concatenate([vt0_ref[key_block], vt1_ref[key_block]], 1)
        scores = [contract(keys, parts[head], (1, 1)) * scaling for head in range(heads)]
        if same is not None:
            scores = [jnp.where(same, each, MASKED) for each in scores]
        before = top[...]
        highest = jnp.maximum(before, jnp.concatenate([jnp.max(each, 0, keepdims=True) for each in scores], 0))
        fade = jnp.exp2(before - highest)
        raised = [jnp.exp2(each - highest[head : head + 1]) for head, each in enumerate(scores)]
        if same is not None:
            raised = [jnp.where(same, each, 0.0) for each in raised]
        top[...] = highest
        total[...] = total[...] * fade + jnp.concatenate([jnp.sum(each, 0, keepdims=True) for each in raised], 0)
        products = [
            jnp.dot(values[head * DH : (head + 1) * DH], each.astype(bf16), preferred_element_type=f32)
            for head, each in enumerate(raised)
        ]
        fades = [jnp.broadcast_to(fade[head : head + 1], (DH, fade.shape[1])) for head in range(heads)]
        sums[...] = sums[...] * jnp.concatenate(fades, 0) + jnp.concatenate(products, 0)

    for index in range(count):
        for head in range(heads):
            parts[head] = head_lanes(q_ref[first + index], head)
        top[...] = jnp.full_like(top, MASKED)
        total[...] = jnp.zeros_like(total)
        sums[...] = jnp.zeros_like(sums)
        visit_blocks(info_ref, first + index, columns, share, own, visit)
        for head in range(heads):
            rows = pl.ds(head * DH, DH)
            line = pl.ds(head, 1)
            outs[index][rows, :] = (sums[rows, :] / total[line, :]).astype(bf16)
            lses[index][line, :] = top[line, :] + jnp.log2(total[line, :])


def attend_forward(first, count, info, q, kv, kv_twin, turned, turned_twin, share):
    columns, own, padded = q.shape
    width = turned.shape[1]
    heads = width // DH
    keys = pl.BlockSpec((columns, own, padded), lambda i, s: (0, 0, 0))
    values = pl.BlockSpec((columns, width, own), lambda i, s: (1, 0, 0))
    flat = lambda rows: pl.BlockSpec((rows, own), lambda i, s: (0, 0))
    outs = pl.pallas_call(
        lambda *refs: forward_kernel(first, share, *refs),
        grid_spec=pltpu.PrefetchScalarGridSpec(
            num_scalar_prefetch=1,
            grid=(1,),
            in_specs=[keys, keys, keys, values, values],
            out_specs=[flat(width)] * count + [flat(heads)] * count,
            scratch_shapes=[
                pltpu.VMEM((heads, own, padded), bf16),
                pltpu.VMEM((heads, own), f32),
                pltpu.VMEM((heads, own), f32),
                pltpu.VMEM((width, own), f32),
            ],
        ),
        out_shape=[jax.ShapeDtypeStruct((width, own), bf16)] * count + [jax.ShapeDtypeStruct((heads, own), f32)] * count,
        compiler_params=pltpu.CompilerParams(vmem_limit_bytes=60 << 20),
        cost_estimate=cost(0.001),
        name="attend_forward",
    )(info, q, kv, kv_twin, turned, turned_twin)
    return outs[:count], outs[count:]


def backward_kernel(columns, share, info_ref, q_ref, kv0_ref, kv1_ref, kt0_ref, kt1_ref, *refs):
    grads, outs, lses, refs = refs[0], refs[1 : columns + 1], refs[columns + 1 : 2 * columns + 1], refs[2 * columns + 1 :]
    dq_ref, near_ref, *fars, part_q, part_g, delta, lse, sum_q, sum_k, sum_v = refs
    own, width = q_ref.shape[1], kt0_ref.shape[1]
    heads = width // DH
    scaling = DH ** (-0.5)
    sum_k[...] = jnp.zeros_like(sum_k)
    sum_v[...] = jnp.zeros_like(sum_v)
    for block in range(columns):
        lse[block] = lses[block][...]
        column = info_ref[2] - block
        grad = grads[jnp.where(column < 0, column + columns, column)]
        spare = jnp.zeros((part_g.shape[1] - width, own), bf16)
        product = grad.astype(f32) * outs[block][...].astype(f32)
        for head in range(heads):
            part_q[block, pl.ds(head * own, own), :] = head_lanes(q_ref[block], head)
            part_g[block, :, pl.ds(head * own, own)] = jnp.concatenate([head_rows(grad, head), spare], 0)
            delta[block, pl.ds(head, 1), :] = jnp.sum(product[head * DH : (head + 1) * DH], 0, keepdims=True)

    def query_step(block, carry):
        sum_q[...] = jnp.zeros_like(sum_q)

        def visit(key_block, same):
            keys = jnp.concatenate([kv0_ref[key_block], kv1_ref[key_block]], 0)
            turned = jnp.concatenate([kt0_ref[key_block], kt1_ref[key_block]], 1)
            values = jnp.concatenate([kv0_ref[columns + key_block], kv1_ref[columns + key_block]], 0)
            all_probs, all_grads = [], []
            for head in range(heads):
                span = pl.ds(head * own, own)
                scores = contract(keys, part_q[block, span, :], (1, 1)) * (scaling * LOG2E)
                probs = jnp.exp2(scores - lse[block, pl.ds(head, 1), :])
                if same is not None:
                    probs = jnp.where(same, probs, 0.0)
                slopes = jnp.dot(values, part_g[block, :, span], preferred_element_type=f32)
                grads = (probs * (slopes - delta[block, pl.ds(head, 1), :])).astype(bf16)
                all_probs.append(probs.astype(bf16))
                all_grads.append(grads)
            for head in range(heads):
                rows = pl.ds(head * DH, DH)
                part = turned[head * DH : (head + 1) * DH]
                sum_q[rows, :] += jnp.dot(part, all_grads[head], preferred_element_type=f32)
            sum_v[key_block] += contract(jnp.concatenate(all_probs, 1), part_g[block], (1, 1))
            sum_k[key_block] += jnp.dot(jnp.concatenate(all_grads, 1), part_q[block], preferred_element_type=f32)

        visit_blocks(info_ref, block, columns, share, own, visit)
        dq_ref[block] = sum_q[...].T * scaling
        return carry

    lax.fori_loop(0, columns, query_step, 0)
    for block in range(columns):
        for place, sums, far_ref in ((block, sum_k, fars[0]), (columns + block, sum_v, fars[1])):
            near_ref[place] = sums[block, :own].astype(bf16)
            far_ref[block] = sums[block, own:].astype(bf16)


def attend_backward(info, q, kv, kv_twin, turned, turned_twin, grads, outs, lses, share):
    columns, own, padded = q.shape
    width = turned.shape[1]
    heads = width // DH
    vmem = pl.BlockSpec(memory_space=pltpu.VMEM)
    operands = [q, kv, kv_twin, turned, turned_twin, grads, *outs, *lses]
    return pl.pallas_call(
        lambda *refs: backward_kernel(columns, share, *refs),
        in_specs=[pl.BlockSpec(memory_space=pltpu.SMEM)] + [vmem] * len(operands),
        out_specs=[vmem] * 4,
        out_shape=[jax.ShapeDtypeStruct((columns, own, width), f32)]
        + [jax.ShapeDtypeStruct((many, own, padded), bf16) for many in (2 * columns, columns, columns)],
        scratch_shapes=[
            pltpu.VMEM((columns, heads * own, padded), bf16),
            pltpu.VMEM((columns, padded, heads * own), bf16),
            pltpu.VMEM((columns, heads, own), f32),
            pltpu.VMEM((columns, heads, own), f32),
            pltpu.VMEM((width, own), f32),
            pltpu.VMEM((columns, share, padded), f32),
            pltpu.VMEM((columns, share, padded), f32),
        ],
        compiler_params=pltpu.CompilerParams(vmem_limit_bytes=48 << 20),
        cost_estimate=cost(0.001),
        name="attend_backward",
    )(info, *operands)


def unproject_kernel(info_ref, dq_ref, near_k_ref, far_k_ref, near_v_ref, far_v_ref, w_ref, cos_ref, sin_ref, part_ref, low_ref):
    width = dq_ref.shape[2]
    lanes = 2 * width
    even = lax.broadcasted_iota(jnp.int32, (dq_ref.shape[1], lanes), 1) % 2 == 0
    dk = (near_k_ref[0, :, :width].astype(f32) + far_k_ref[0, :, :width].astype(f32)) * DH ** (-0.5)
    dv = near_v_ref[0, :, :width].astype(f32) + far_v_ref[0, :, :width].astype(f32)
    both = jnp.concatenate([dq_ref[0], dk], 1)
    swapped = jnp.where(even, pltpu.roll(both, lanes - 1, 1), pltpu.roll(both, 1, 1))
    both = both * widen(cos_ref[0], lanes) - swapped * widen(sin_ref[0], lanes)
    low = jnp.concatenate([both, dv], 1).astype(bf16)
    low_ref[0] = low
    part_ref[0] = contract(low, w_ref[...], (1, 1)).astype(bf16)


def unproject(info, dq, near, far_k, far_v, weight, cosine, sine):
    columns, own, width = dq.shape
    feature = weight.shape[0]
    block = lambda a, first: pl.BlockSpec((1,) + a.shape[1:], lambda i, s: (first + i, 0, 0))
    whole = lambda a: pl.BlockSpec(a.shape, lambda i, s: (0, 0))
    place = lambda i, s: (jnp.where(s[2] >= i, s[2] - i, s[2] - i + columns), 0, 0)
    low = jax.ShapeDtypeStruct((columns, own, weight.shape[1]), bf16)
    return pl.pallas_call(
        unproject_kernel,
        grid_spec=pltpu.PrefetchScalarGridSpec(
            num_scalar_prefetch=1,
            grid=(columns,),
            in_specs=[block(dq, 0), block(near, 0), block(far_k, 0), block(near, columns), block(far_v, 0), whole(weight)]
            + [block(cosine, 0), block(sine, 0)],
            out_specs=[pl.BlockSpec((1, own, feature), place), block(low, 0)],
        ),
        out_shape=[jax.ShapeDtypeStruct((columns, own, feature), bf16), low],
        compiler_params=pltpu.CompilerParams(vmem_limit_bytes=40 << 20),
        cost_estimate=cost(0.001),
        name="unproject",
    )(info, dq, near, far_k, near, far_v, weight, cosine, sine)


def project_grad_kernel(low_ref, *refs):
    x_refs, (grad_ref,) = refs[:-1], refs[-1:]
    total = None
    for block, x_ref in enumerate(x_refs):
        piece = contract(x_ref[...], low_ref[block], (0, 0))
        total = piece if total is None else total + piece
    grad_ref[...] = total.astype(bf16)


def project_grad(low, blocks):
    return pl.pallas_call(
        project_grad_kernel,
        out_shape=jax.ShapeDtypeStruct((blocks[0].shape[1], low.shape[2]), bf16),
        compiler_params=pltpu.CompilerParams(vmem_limit_bytes=40 << 20),
        cost_estimate=cost(0.001),
        name="project_grad",
    )(low, *blocks)


def mean_lanes(values):
    return jnp.sum(values, 1, keepdims=True) * (1.0 / values.shape[1])


def norm_forward(values, gain, shift):
    centred = values - mean_lanes(values)
    inverse = lax.rsqrt(mean_lanes(centred * centred) + EPSILON)
    normed = centred * inverse
    return normed * gain + shift, normed, inverse


def norm_backward(grad, normed, inverse, gain):
    scaled = grad * gain
    return inverse * (scaled - mean_lanes(scaled) - normed * mean_lanes(scaled * normed))


def unit(size):
    rows = lax.broadcasted_iota(jnp.int32, (size, size), 0)
    return (rows == lax.broadcasted_iota(jnp.int32, (size, size), 1)).astype(bf16)


def feed_kernel(info_ref, x_ref, cot_ref, w_ref, *refs):
    parts, _, columns, slab, _ = w_ref.shape
    att_refs, refs = refs[:columns], refs[columns:]
    result_ref, grad_att_ref, grad_one_ref, hidden_ref, act_out, gin_out, gtwo_ref, gone_ref, sums_ref, sent_ref, *refs = refs
    w, slopes, outer, act_ref, gin_ref, stage, sems, ends = refs
    rows, columns, quarter, _ = w.shape
    act_copy = pltpu.make_async_copy(act_ref, act_out, ends.at[0])
    gin_copy = pltpu.make_async_copy(gin_ref, gin_out, ends.at[1])

    def turned(step):
        column = info_ref[2] + step
        return jnp.where(column >= columns, column - columns, column)

    hidden_cols = act_ref.shape[2]
    both = 2 * hidden_cols
    spans = ((0, hidden_cols), (hidden_cols, hidden_cols), (both, w.shape[3] - both))

    def copies(kind):
        lanes = pl.ds(*spans[kind])
        for part in range(parts):
            target = w.at[:, :, pl.ds(part * slab, slab), lanes]
            yield pltpu.make_async_copy(w_ref.at[part, :, :, :, lanes], target, sems.at[kind, part])

    def wait(kind):
        for each in copies(kind):
            each.wait()

    for kind in (2, 0, 1):
        for each in copies(kind):
            each.start()

    def block(kind, column):
        lanes = pl.ds(*spans[kind])
        return jnp.concatenate([w[row, column, :, lanes] for row in range(rows)], 0)

    wait(2)
    mix = pl.ds(both, quarter)
    attended = jnp.concatenate([ref[...] for ref in att_refs], 0)
    branch = []
    for row in range(rows):
        weight = jnp.concatenate([w[row, turned(step), :, mix] for step in range(columns)], 0)
        branch.append(contract(attended, weight, (0, 0)))
    branch = jnp.concatenate(branch, 1)
    eye = unit(quarter)
    small = [contract(w[row, 0, :, pl.ds(both + quarter, 12)], eye, (0, 0)) for row in range(rows)]
    small = jnp.concatenate(small, 1)
    vectors = small[0:4] + (small[4:8] + small[8:12])
    gain_one, shift_one, gain_two, shift_two = (vectors[i : i + 1] for i in range(4))

    hidden, normed_one, inverse_one = norm_forward(x_ref[...].astype(f32) + branch, gain_one, shift_one)
    low = hidden.astype(bf16)
    hidden_ref[...] = low.T
    outer[...] = jnp.zeros_like(outer)

    wait(0)

    def forward(column, carry):
        inner = jnp.dot(low, block(0, column), preferred_element_type=f32)
        cumulative = 0.5 * (1.0 + lax.erf(inner * (0.5**0.5)))
        slopes[column] = cumulative + inner * (jnp.exp(-0.5 * inner * inner) * 0.3989422804014327)
        act_ref[column] = (inner * cumulative).astype(bf16)
        return carry

    lax.fori_loop(0, columns, forward, 0)
    act_copy.start()
    wait(1)

    def combine(column, carry):
        outer[...] += contract(act_ref[column], block(1, column), (1, 1))
        return carry

    lax.fori_loop(0, columns, combine, 0)
    result, normed_two, inverse_two = norm_forward(hidden + outer[...], gain_two, shift_two)
    result_ref[...] = result.astype(bf16)
    cot = cot_ref[...].astype(f32)
    grad_two = norm_backward(cot, normed_two, inverse_two, gain_two)
    grad_two_low = grad_two.astype(bf16)
    gtwo_ref[...] = grad_two_low.T
    outer[...] = grad_two

    def backward(column, carry):
        grad = jnp.dot(grad_two_low, block(1, column), preferred_element_type=f32)
        gin_ref[column] = (grad * slopes[column]).astype(bf16)
        outer[...] += contract(gin_ref[column], block(0, column), (1, 1))
        return carry

    lax.fori_loop(0, columns, backward, 0)
    gin_copy.start()
    grad_hidden = outer[...]
    grad_one = norm_backward(grad_hidden, normed_one, inverse_one, gain_one)
    grad_one_ref[...] = grad_one
    grad_one_low = grad_one.astype(bf16)
    for step in range(columns):
        weight = jnp.concatenate([w[row, turned(step), :, mix] for row in range(rows)], 1)
        grad_att_ref[turned(step)] = contract(weight, grad_one_low, (1, 1)).astype(bf16)
    sums = [jnp.sum(a, 0, keepdims=True) for a in (grad_hidden * normed_one, grad_hidden, cot * normed_two, cot)]
    sums = jnp.concatenate(sums, 0)
    for row in range(rows):
        mine = slice(row * quarter, (row + 1) * quarter)
        gone_ref[row] = grad_one_low[:, mine]
        sums_ref[row] = sums[:, mine].astype(bf16)

    def leave(column):
        slot = column % 2
        return pltpu.make_async_copy(stage.at[slot], sent_ref.at[:, :, column], ends.at[2 + slot])

    def send(column, carry):
        @pl.when(column > 1)
        def _():
            leave(column - 2).wait()

        attended = attended_block(info_ref, att_refs, column)
        operands = attended, act_ref[column], gin_ref[column], hidden_ref, gtwo_ref, gone_ref, sums_ref
        weigh_block(1 - info_ref[1], info_ref, *operands, stage.at[column % 2])
        leave(column).start()
        return carry

    lax.fori_loop(0, columns, send, 0)
    for column in (columns - 2, columns - 1):
        leave(column).wait()
    act_copy.wait()
    gin_copy.wait()


def feed(info, attended, tokens, cot, weights, slabs):
    own, feature = tokens.shape
    parts, rows, columns, slab, lanes = weights.shape
    quarter = parts * slab
    hidden_cols = feature
    vmem, smem = pl.BlockSpec(memory_space=pltpu.VMEM), pl.BlockSpec(memory_space=pltpu.SMEM)
    hbm = pl.BlockSpec(memory_space=pltpu.HBM)
    wide = jax.ShapeDtypeStruct((columns, own, hidden_cols), bf16)
    flat = lambda kind: jax.ShapeDtypeStruct((own, feature), kind)
    tall = jax.ShapeDtypeStruct((feature, own), bf16)
    return pl.pallas_call(
        feed_kernel,
        in_specs=[smem, vmem, vmem, pl.BlockSpec(memory_space=pltpu.HBM)] + [vmem] * columns,
        out_specs=[vmem] * 4 + [hbm] * 2 + [vmem] * 3 + [hbm],
        out_shape=[
            flat(bf16), jax.ShapeDtypeStruct((columns, quarter, own), bf16), flat(f32), tall, wide, wide, tall,
            jax.ShapeDtypeStruct((rows, own, quarter), bf16), jax.ShapeDtypeStruct((rows, 4, quarter), bf16),
            jax.ShapeDtypeStruct((2, slabs, columns, quarter // slabs, lanes), bf16),
        ],
        scratch_shapes=[
            pltpu.VMEM((rows, columns, quarter, lanes), bf16),
            pltpu.VMEM((columns, own, hidden_cols), f32),
            pltpu.VMEM((own, feature), f32),
            pltpu.VMEM(wide.shape, bf16),
            pltpu.VMEM(wide.shape, bf16),
            pltpu.VMEM((2, 2, slabs, quarter // slabs, lanes), bf16),
            pltpu.SemaphoreType.DMA((3, parts)),
            pltpu.SemaphoreType.DMA((4,)),
        ],
        compiler_params=pltpu.CompilerParams(vmem_limit_bytes=60 << 20),
        cost_estimate=cost(0.001),
        name="feed",
    )(info, tokens, cot, weights, *attended)


def weigh_block(core, info_ref, attended, act, gin, hidden_ref, gtwo_ref, gone_ref, sums_ref, out):
    _, slabs, slab, lanes = out.shape
    quarter = slabs * slab
    hidden_cols = act.shape[1]
    eye = unit(quarter)
    away = lambda index, mine: jnp.where(index == mine, 0, 1)
    rows = [2 * pair + core for pair in range(2)]
    spans = [pl.ds(pl.multiple_of(row * quarter, quarter), quarter) for row in rows]
    both = lambda ref: jnp.concatenate([ref[span, :] for span in spans], 0)
    inner = jnp.dot(both(hidden_ref), gin, preferred_element_type=f32).astype(bf16)
    outer = jnp.dot(both(gtwo_ref), act, preferred_element_type=f32).astype(bf16)
    for pair, row in enumerate(rows):
        mixed = jnp.dot(attended, gone_ref[row], preferred_element_type=f32).astype(bf16)
        vector = contract(eye, sums_ref[row], (1, 1)).astype(bf16)
        rest = jnp.zeros((quarter, lanes - 2 * hidden_cols - quarter - 4), bf16)
        tail = jnp.concatenate([mixed, vector, rest], 1)
        far = away(pair, info_ref[3])
        for part in range(slabs):
            place = away(part, info_ref[4]) if slabs > 1 else 0
            low = pair * quarter + part * slab
            out[far, place, :, 0:hidden_cols] = inner[low : low + slab]
            out[far, place, :, hidden_cols : 2 * hidden_cols] = outer[low : low + slab]
            out[far, place, :, 2 * hidden_cols :] = tail[part * slab : (part + 1) * slab]


def attended_block(info_ref, att_refs, column):
    step = column - info_ref[2]
    step = jnp.where(step < 0, step + len(att_refs), step)
    attended = att_refs[0][...]
    for index in range(1, len(att_refs)):
        attended = jnp.where(step == index, att_refs[index][...], attended)
    return attended


def weigh_kernel(info_ref, hidden_ref, act_ref, gin_ref, gtwo_ref, gone_ref, sums_ref, *refs):
    att_refs, out_ref = refs[:-1], refs[-1]
    attended = attended_block(info_ref, att_refs, pl.program_id(0))
    operands = attended, act_ref[0], gin_ref[0], hidden_ref, gtwo_ref, gone_ref, sums_ref
    weigh_block(info_ref[1], info_ref, *operands, out_ref.at[:, :, 0])


def weigh(info, attended, hidden, act, gin, gtwo, gone, sums, lanes, slabs):
    columns = act.shape[0]
    quarter = attended[0].shape[0]
    whole = lambda a: pl.BlockSpec(a.shape, lambda i, s: (0,) * a.ndim)
    piece = pl.BlockSpec((1,) + act.shape[1:], lambda i, s: (i, 0, 0))
    slab = quarter // slabs
    return pl.pallas_call(
        weigh_kernel,
        grid_spec=pltpu.PrefetchScalarGridSpec(
            num_scalar_prefetch=1,
            grid=(columns,),
            in_specs=[whole(hidden), piece, piece, whole(gtwo), whole(gone), whole(sums)] + [whole(a) for a in attended],
            out_specs=pl.BlockSpec((2, slabs, 1, slab, lanes), lambda i, s: (0, 0, i, 0, 0)),
        ),
        out_shape=jax.ShapeDtypeStruct((2, slabs, columns, slab, lanes), bf16),
        compiler_params=pltpu.CompilerParams(vmem_limit_bytes=60 << 20),
        cost_estimate=cost(0.001),
        name="weigh",
    )(info, hidden, act, gin, gtwo, gone, sums, *attended)


def parcel_kernel(info_ref, inner_ref, outer_ref, output_ref, *refs):
    small_refs, out_ref = refs[:-1], refs[-1]
    columns = inner_ref.shape[1]
    quarter = output_ref.shape[1]
    slab = out_ref.shape[0]
    offset = info_ref[0] * slab if slab < quarter else 0
    rows = pl.ds(pl.multiple_of(offset, slab), slab)
    values = jnp.concatenate([ref[...] for ref in small_refs], 0)
    high = values.astype(bf16)
    rest = values - high.astype(f32)
    middle = rest.astype(bf16)
    last = (rest - middle.astype(f32)).astype(bf16)
    pick = lax.broadcasted_iota(jnp.int32, (slab, quarter), 0) + offset
    pick = (pick == lax.broadcasted_iota(jnp.int32, (slab, quarter), 1)).astype(bf16)
    small = jnp.concatenate([contract(pick, part, (1, 1)) for part in (high, middle, last)], 1).astype(bf16)
    fill = jnp.zeros((slab, out_ref.shape[1] - 2 * columns - quarter - 12), bf16)
    out_ref[:, 0:columns] = inner_ref[rows, :]
    out_ref[:, columns : 2 * columns] = outer_ref[rows, :]
    out_ref[:, 2 * columns :] = jnp.concatenate([output_ref[rows, :], small, fill], 1)


def parcel(part, inner, outer, output, vectors, lanes, slabs):
    vmem, smem = pl.BlockSpec(memory_space=pltpu.VMEM), pl.BlockSpec(memory_space=pltpu.SMEM)
    return pl.pallas_call(
        parcel_kernel,
        in_specs=[smem] + [vmem] * 7,
        out_shape=jax.ShapeDtypeStruct((inner.shape[0] // slabs, lanes), bf16),
        cost_estimate=cost(0.001),
        name="parcel",
    )(part, inner, outer, output, *(v.reshape(1, -1) for v in vectors))


def keep(values, index, axis=0):
    first, second = lax.index_in_dim(values, 0, axis, False), lax.index_in_dim(values, 1, axis, False)
    chosen = index == 0
    return jnp.where(chosen, first, second), jnp.where(chosen, second, first)


def tie(*values):
    return lax.optimization_barrier(values)


def shift(values, step):
    columns = lax.axis_size("col")
    if step % columns == 0:
        return values
    return lax.ppermute(values, "col", [(i, (i + step) % columns) for i in range(columns)])


def add_kernel(count, sums, *refs):
    results, (*sources, buffer, held, sems, ends) = refs[-count - 4 : -4], refs[: -count - 4] + refs[-4:]
    rows, first, number = [], 0, 0
    for index, start, parts in sums:
        row = []
        for which, lead, low, high in parts:
            source = sources[which].at[lead + (pl.ds(low, high - low),)]
            copy = pltpu.make_async_copy(source, buffer.at[pl.ds(first, high - low)], sems.at[number])
            copy.start()
            row.append((first, high - low, copy))
            first, number = first + high - low, number + 1
        rows.append(row)
    copies, first = [], 0
    for place, ((index, start, _), row) in enumerate(zip(sums, rows)):
        size = row[0][1]
        for *_, copy in row:
            copy.wait()
        total = sum(buffer[at : at + size].astype(f32) for at, *_ in row)
        held[first : first + size] = total.astype(bf16)
        target = results[index].at[pl.ds(start, size)]
        copies.append(pltpu.make_async_copy(held.at[pl.ds(first, size)], target, ends.at[place]))
        copies[-1].start()
        first += size
    for copy in copies:
        copy.wait()


def add_blocks(arrays, lengths, sums):
    hbm = pl.BlockSpec(memory_space=pltpu.HBM)
    tail = arrays[0].shape[-2:]
    parts = [part for *_, each in sums for part in each]
    return pl.pallas_call(
        lambda *refs: add_kernel(len(lengths), sums, *refs),
        in_specs=[hbm] * len(arrays),
        out_specs=[hbm] * len(lengths),
        out_shape=[jax.ShapeDtypeStruct((length,) + tail, bf16) for length in lengths],
        scratch_shapes=[
            pltpu.VMEM((sum(high - low for *_, low, high in parts),) + tail, bf16),
            pltpu.VMEM((sum(lengths),) + tail, bf16),
            pltpu.SemaphoreType.DMA((len(parts),)),
            pltpu.SemaphoreType.DMA((len(sums),)),
        ],
        compiler_params=pltpu.CompilerParams(vmem_limit_bytes=60 << 20),
        cost_estimate=cost(0.001),
        name="add_blocks",
    )(*arrays)


def open_kernel(hidden_cols, part_ref, mine_ref, other_ref, *outs):
    *outs, sums_ref, query_ref, key_ref, value_ref = outs
    slab, quarter = mine_ref.shape[0], outs[2].shape[1]
    spans = (0, hidden_cols), (hidden_cols, hidden_cols), (2 * hidden_cols, quarter)
    lanes = mine_ref.shape[1] - 6 * quarter

    def write(first, second):
        for (start, size), out in zip(spans, outs):
            out[0:slab, :] = first[:, start : start + size].astype(f32)
            out[slab : 2 * slab, :] = second[:, start : start + size].astype(f32)
        start = 2 * hidden_cols + quarter
        last = jnp.concatenate([first[:, start:lanes], second[:, start:lanes]], 0)
        sums_ref[...] = contract(last[:, 0:4], unit(2 * slab), (0, 0))

    @pl.when(part_ref[0] == 0)
    def _():
        write(mine_ref[...], other_ref[...])

    @pl.when(part_ref[0] != 0)
    def _():
        write(other_ref[...], mine_ref[...])

    total = mine_ref[:, lanes:].astype(f32) + other_ref[:, lanes:].astype(f32)
    for index, ref in enumerate((query_ref, key_ref, value_ref)):
        for half in range(2):
            start = (3 * half + index) * quarter
            ref[half * slab : (half + 1) * slab, :] = total[:, start : start + quarter]


def open_shards(part, mine, other, hidden_cols, quarter):
    vmem, smem = pl.BlockSpec(memory_space=pltpu.VMEM), pl.BlockSpec(memory_space=pltpu.SMEM)
    rows = hidden_cols, hidden_cols, quarter
    shape = lambda *dims: jax.ShapeDtypeStruct(dims, f32)
    return pl.pallas_call(
        lambda *refs: open_kernel(hidden_cols, *refs),
        in_specs=[smem, vmem, vmem],
        out_shape=[shape(quarter, a) for a in rows] + [shape(4, quarter)] + [shape(quarter, quarter)] * 3,
        compiler_params=pltpu.CompilerParams(vmem_limit_bytes=16 << 20),
        cost_estimate=cost(0.001),
        name="open_shards",
    )(part, mine, other)


def sum_shards(kept, sent, mark):
    columns = kept.shape[2]
    middle = columns // 2
    pair = kept, swap(sent, "yb")
    both = lambda lead, low, high: [(0, lead, low, high), (1, lead, low, high)]
    to_dp = [(0, 0, both((1, 1), 0, middle)), (0, middle, both((0, 1), 0, middle))]
    to_ya = [(1, 0, both((1, 1), middle, columns)), (1, middle, both((1, 0), middle, columns))]
    to_dp, to_ya = add_blocks(pair, (columns, columns), to_dp + to_ya)
    mark, to_dp, to_ya = tie(mark, to_dp, to_ya)
    by_dp, by_ya = swap(to_dp, "dp"), swap(to_ya, "ya")

    def sides(mark):
        dp, ya, mark = tie(by_dp, by_ya, mark)
        rest_ya = (0, 0, both((1, 0), 0, middle) + [(2, (), 0, middle)])
        rest_dp = (1, 0, both((0, 1), middle, columns) + [(3, (), 0, middle)])
        rest_ya, rest_dp = add_blocks(pair + (dp, ya), (middle, columns - middle), [rest_ya, rest_dp])
        mark, rest_ya, rest_dp = tie(mark, rest_ya, rest_dp)
        rest_ya, rest_dp = swap(rest_ya, "ya"), swap(rest_dp, "dp")

        def finish(mark):
            low_ya, high_dp, mark = tie(rest_ya, rest_dp, mark)
            low = both((0, 0), 0, middle) + [(2, (), middle, columns), (4, (), 0, middle)]
            high = both((0, 0), middle, columns) + [(3, (), middle, columns), (5, (), 0, columns - middle)]
            (own,) = add_blocks(pair + (dp, ya, low_ya, high_dp), (columns,), [(0, 0, low), (0, middle, high)])
            own, mark = tie(own, mark)
            mine = lax.psum_scatter(own, "col", scatter_dimension=0, tiled=False)
            return mine, mark

        return mark, finish

    return mark, sides


def body(
    inputs, cotangent, lengths, source, query_weight, key_weight, value_weight, output_weight, inner_weight, outer_weight,
    first_gain, first_shift, second_gain, second_shift,
):
    micro, quarter, share = inputs.shape
    dp_count, columns = lax.axis_size("dp"), lax.axis_size("col")
    pack, own = share * columns, share // 2
    feature, count = 4 * quarter, share * micro
    width, hidden_cols = query_weight.shape[1], inner_weight.shape[1]
    lanes = -(-(2 * hidden_cols + quarter + 12) // 128) * 128
    me, m, half, z = (lax.axis_index(a) for a in ("dp", "ya", "yb", "col"))

    boundary = jnp.where(m == 0, lengths[0, 0], lengths[0, 1])
    info = jnp.stack([boundary, half, z, m, me]).astype(jnp.int32)
    slabs = 2 if dp_count == 2 else 1

    vectors = (first_gain, first_shift, second_gain, second_shift)
    anchors = spread_dp(source)
    packed = parcel(jnp.reshape(me, (1,)).astype(jnp.int32), inner_weight, outer_weight, output_weight, vectors, lanes, slabs)
    axes = ("dp",) + SHARDS if slabs == 2 else SHARDS
    everywhere = lax.all_gather(packed, axes, axis=0).reshape(slabs, 4, columns, quarter // slabs, lanes)
    anchor = source.reshape(count)
    place = anchor // (dp_count * pack) * share + anchor % share
    holder = anchor % (dp_count * pack) // pack
    wide_in = spread_dp(inputs)

    steps = jnp.arange(columns, dtype=jnp.int32)
    spots = ((z - steps) % columns * share + half * own)[:, None] + jnp.arange(own, dtype=jnp.int32)[None, :]
    frequency = 10000.0 ** (-2.0 * jnp.arange(DH // 2, dtype=f32) / DH)
    angles = (spots - jnp.where(spots >= boundary, boundary, 0)).astype(f32)[..., None] * jnp.tile(jnp.repeat(frequency, 2), 2)
    signs = jnp.where(jnp.arange(2 * DH) % 2 == 0, -1.0, 1.0)
    cosine, sine = jnp.cos(angles), jnp.sin(angles) * signs
    wide_in, cosine, sine = tie(wide_in, cosine, sine)

    if dp_count == 2:
        pick = (holder * count + place)[:, None] == jnp.arange(dp_count * count, dtype=jnp.int32)[None, :]
        pick = pick.astype(bf16).reshape(count, dp_count, micro, share)
        deal = lambda wide: jnp.einsum("tsmj,smfj->tf", pick, wide, preferred_element_type=f32).astype(bf16)
    else:
        deal = lambda wide: wide.transpose(0, 1, 3, 2).reshape(-1, quarter)[holder * count + place]

    def to_tokens(dealt):
        return lax.all_to_all(dealt.reshape(4, own, quarter), ROWS, split_axis=0, concat_axis=0, tiled=True)

    dealt = deal(wide_in)
    cotangent, dealt = tie(cotangent, dealt)
    tokens = to_tokens(dealt).transpose(1, 0, 2).reshape(own, feature)
    wide_cot, tokens = tie(spread_dp(cotangent), tokens)
    blocks = [shift(tokens, step) for step in range(columns)]
    cot = to_tokens(deal(wide_cot)).transpose(1, 0, 2).reshape(own, feature)
    qkv_weight = jnp.concatenate([query_weight, key_weight, value_weight], 1)
    qkv_weight = gather_rows(qkv_weight).reshape(feature, -1)

    blocks[-1], cot, anchors = tie(blocks[-1], cot, anchors)
    q, kv, turned = project(blocks, qkv_weight, cosine, sine)
    kv_twin, turned_twin = swap(kv, "yb"), swap(turned, "yb")
    mixed, lses = attend_forward(1, columns - 1, info, q, kv, kv_twin, turned, turned_twin, share)
    q, mixed = tie(q, mixed)
    last = attend_forward(0, 1, info, q, kv, kv_twin, turned, turned_twin, share)
    mixed, lses = last[0] + mixed, last[1] + lses
    attended = [shift(mixed[step], -step) for step in range(columns)]

    result, grad_att, grad_one, *pieces, sent = feed(info, attended, tokens, cot, everywhere, slabs)
    grad_att = lax.all_to_all(grad_att, "col", split_axis=0, concat_axis=0, tiled=True)
    def to_loader(*rows):
        cut = jnp.concatenate([a.astype(bf16).reshape(own, 4, quarter).transpose(1, 0, 2) for a in rows], 2)
        cut = jnp.broadcast_to(cut[None], (dp_count,) + cut.shape).reshape(dp_count * 4, own, -1)
        moved = lax.all_to_all(cut, ("dp",) + ROWS, split_axis=0, concat_axis=0, tiled=True)
        return moved.reshape(-1, len(rows) * quarter)

    spot = jnp.arange(count, dtype=jnp.int32)
    wanted = spot // share * (dp_count * pack) + me * pack + z * share + spot % share
    if dp_count == 2:
        put = (anchors.reshape(-1)[:, None] == wanted[None, :]).astype(bf16)
        settle = lambda wide: contract(wide, put, (0, 0)).astype(bf16)
    else:
        order = jnp.argsort(anchors.reshape(-1))
        spots_in = jnp.searchsorted(anchors.reshape(-1)[order], wanted)
        settle = lambda wide: wide[order[spots_in]].T
    kept = weigh(info, attended, *pieces, lanes, slabs)
    if slabs == 2:
        grad_att, sides = sum_shards(kept, sent, grad_att)
    else:
        flip = lambda a, index, axis: jnp.where(index == 0, a, jnp.flip(a, axis))
        cut = flip(flip(jnp.stack([kept, sent], 1), m, 0), half, 1).reshape(4 * columns, quarter, lanes)
        summed = lax.psum_scatter(cut, SHARDS, scatter_dimension=0, tiled=False)
        summed = lax.psum(summed, "dp").astype(f32)

    dq, near, *far = attend_backward(info, q, kv, kv_twin, turned, turned_twin, grad_att, mixed, lses, share)
    partial, low = unproject(info, dq, near, *(swap(each, "yb") for each in far), qkv_weight, cosine, sine)
    if slabs == 2:
        low, finish = sides(low)
    grad_qkv = project_grad(low, blocks)
    partial = lax.all_to_all(partial, "col", split_axis=0, concat_axis=0, tiled=True)
    grad_tokens = grad_one + jnp.sum(partial.astype(f32), 0)

    def over_dp(values):
        if dp_count == 2:
            return values.astype(f32) + swap(values, "dp").astype(f32)
        return lax.psum(values, "dp").astype(f32)

    def halve(grad, axis, index, place_axis):
        kept, sent = keep(grad, index, place_axis)
        return (kept.astype(f32) + swap(sent, axis).astype(f32)).astype(bf16)

    if slabs == 2:
        summed, grad_qkv = finish(grad_qkv)
    grad_qkv = halve(grad_qkv.reshape(2, 2, quarter, 3 * width), "yb", half, 1)
    grad_qkv = halve(grad_qkv, "ya", m, 0)
    grad_tokens, grad_qkv = tie(grad_tokens, grad_qkv)
    if slabs == 1:
        grad_qkv = over_dp(grad_qkv)
        sum_qkv = [grad_qkv[:, i * width : (i + 1) * width] for i in range(3)]
        sum_inner, sum_outer = summed[:, :hidden_cols], summed[:, hidden_cols : 2 * hidden_cols]
        sum_output = summed[:, 2 * hidden_cols : 2 * hidden_cols + quarter]
        sum_vectors = summed[:, 2 * hidden_cols + quarter : 2 * hidden_cols + quarter + 4].T

    shape = lambda a: a.reshape(quarter, micro, share).transpose(1, 0, 2)
    moved = to_loader(result, grad_tokens)
    if slabs == 2:
        slab = quarter // 2
        mine = jnp.concatenate([summed, grad_qkv[:slab], grad_qkv[slab:]], 1)
        other = swap(mine, "dp")
        moved, summed = tie(moved, summed)
        part = jnp.reshape(me, (1,)).astype(jnp.int32)
        sum_inner, sum_outer, sum_output, sum_vectors, *sum_qkv = open_shards(part, mine, other, hidden_cols, quarter)
    settled = settle(moved)
    final_out, final_grad = shape(settled[:quarter]), shape(settled[quarter:])
    return (
        final_out, final_grad, *sum_qkv,
        sum_output, sum_inner, sum_outer, sum_vectors[0], sum_vectors[1], sum_vectors[2], sum_vectors[3],
    )


def solution(mesh):
    dp, row, col = (mesh.shape[a] for a in ("dp", "row", "col"))
    fine = Mesh(mesh.devices.reshape(dp, 2, row // 2, col), ("dp", "ya", "yb", "col"))
    tokens, matrix = P(None, ROWS, ("dp", "col")), P(ROWS, "col")
    weights = (matrix, matrix, matrix, P("col", ROWS), matrix, matrix, P(ROWS), P(ROWS), P(ROWS), P(ROWS))
    return jax.shard_map(
        body,
        mesh=fine,
        in_specs=(tokens, tokens, P("dp", None), P(None, ("dp", "col"))) + weights,
        out_specs=(tokens, tokens) + weights,
        check_vma=False,
    )
```

```python
import jax
import jax.numpy as jnp
from jax import lax
from jax.experimental import pallas as pl
from jax.experimental.pallas import tpu as pltpu
from jax.sharding import Mesh, PartitionSpec as P

DH = 64
EPSILON = 1e-05
MASKED = -1e30
LOG2E = 1.4426950408889634
SWAP = ((0, 1), (1, 0))
ROWS = ("ya", "yb")
SHARDS = ("ya", "yb", "col")
bf16 = jnp.bfloat16
f32 = jnp.float32


def cost(microseconds):
    return pl.CostEstimate(flops=int(microseconds * 1e9), bytes_accessed=int(microseconds * 3e6), transcendentals=0)


def contract(left, right, dims):
    return lax.dot_general(left, right, ((dims[:1], dims[1:]), ((), ())), preferred_element_type=f32)


def swap(values, axis):
    return lax.ppermute(values, axis, SWAP)


def gather_rows(values):
    first, second = lax.axis_index("ya") == 0, lax.axis_index("yb") == 0
    other = swap(values, "ya")
    pair = jnp.stack([jnp.where(first, values, other), jnp.where(first, other, values)])
    twin = swap(pair, "yb")
    both = jnp.stack([jnp.where(second, pair, twin), jnp.where(second, twin, pair)], 1)
    return both.reshape((4,) + values.shape)


def spread_dp(values):
    if lax.axis_size("dp") == 2:
        other = swap(values, "dp")
        first = lax.axis_index("dp") == 0
        return jnp.stack([jnp.where(first, values, other), jnp.where(first, other, values)])
    return lax.all_gather(values, "dp", axis=0)


def widen(table, lanes):
    return jnp.concatenate([table] * (lanes // table.shape[1]), 1)


def turn(values, cosine, sine):
    lanes = values.shape[1]
    even = lax.broadcasted_iota(jnp.int32, values.shape, 1) % 2 == 0
    swapped = jnp.where(even, pltpu.roll(values, lanes - 1, 1), pltpu.roll(values, 1, 1))
    return values * widen(cosine, lanes) + swapped * widen(sine, lanes)


def project_kernel(blocks, *refs):
    x_refs, (w_ref, cos_ref, sin_ref) = refs[:blocks], refs[blocks : blocks + 3]
    q_ref, kv_ref, turned_ref = refs[-3:]
    width = turned_ref.shape[1]
    for index, x_ref in enumerate(x_refs):
        wide = jnp.dot(x_ref[...], w_ref[...], preferred_element_type=f32)
        turned = turn(wide[:, : 2 * width], cos_ref[index], sin_ref[index])
        parts = turned[:, :width], turned[:, width:], wide[:, 2 * width :]
        for ref, place, part in ((q_ref, index, parts[0]), (kv_ref, index, parts[1]), (kv_ref, blocks + index, parts[2])):
            ref[place] = jnp.concatenate([part, jnp.zeros((part.shape[0], ref.shape[2] - width), f32)], 1).astype(bf16)
        turned_ref[index] = parts[1].T.astype(bf16)
        turned_ref[blocks + index] = parts[2].T.astype(bf16)


def project(blocks, weight, cosine, sine):
    own, width, count = blocks[0].shape[0], weight.shape[1] // 3, len(blocks)
    padded = -(-width // 128) * 128
    return pl.pallas_call(
        lambda *refs: project_kernel(count, *refs),
        out_shape=[
            jax.ShapeDtypeStruct((count, own, padded), bf16),
            jax.ShapeDtypeStruct((2 * count, own, padded), bf16),
            jax.ShapeDtypeStruct((2 * count, width, own), bf16),
        ],
        compiler_params=pltpu.CompilerParams(vmem_limit_bytes=60 << 20),
        cost_estimate=cost(0.001),
        name="project",
    )(*blocks, weight, cosine, sine)


def head_rows(values, head):
    rows = lax.broadcasted_iota(jnp.int32, values.shape, 0)
    return jnp.where((rows >= head * DH) & (rows < (head + 1) * DH), values, jnp.zeros_like(values))


def head_lanes(values, head):
    lanes = lax.broadcasted_iota(jnp.int32, values.shape, 1)
    return jnp.where((lanes >= head * DH) & (lanes < (head + 1) * DH), values, jnp.zeros_like(values))


def block_sides(info_ref, query_block, key_block, columns, share, own):
    boundary, half, column = info_ref[0], info_ref[1], info_ref[2]
    place = lambda block: jnp.where(column >= block, column - block, column - block + columns) * share
    low_q = place(query_block) + half * own
    low_k = place(key_block)
    first_q, second_q = low_q < boundary, low_q + own > boundary
    first_k, second_k = low_k < boundary, low_k + share > boundary
    meets = (first_q & first_k) | (second_q & second_k)
    mixed = (first_q & second_q) | (first_k & second_k)
    side_q = low_q + lax.broadcasted_iota(jnp.int32, (1, own), 1) >= boundary
    rows = lax.broadcasted_iota(jnp.int32, (share, 1), 0)
    shift = jnp.where(rows < own, half * own, (1 - half) * own - own)
    side_k = low_k + rows + shift >= boundary
    return meets, mixed, side_q.astype(f32), side_k.astype(f32)


def visit_blocks(info_ref, query_block, columns, share, own, visit):
    def step(key_block, carry):
        meets, mixed, side_q, side_k = block_sides(info_ref, query_block, key_block, columns, share, own)

        @pl.when(meets & mixed)
        def _():
            visit(key_block, side_q == side_k)

        @pl.when(meets & jnp.logical_not(mixed))
        def _():
            visit(key_block, None)

        return carry

    lax.fori_loop(0, columns, step, 0)


def forward_kernel(first, share, info_ref, q_ref, k0_ref, k1_ref, vt0_ref, vt1_ref, *refs):
    columns, own, _ = k0_ref.shape
    width = vt0_ref.shape[1]
    heads = width // DH
    count = (len(refs) - 4) // 2
    outs, lses, (parts, top, total, sums) = refs[:count], refs[count : 2 * count], refs[2 * count :]
    scaling = DH ** (-0.5) * LOG2E

    def visit(key_block, same):
        keys = jnp.concatenate([k0_ref[key_block], k1_ref[key_block]], 0)
        values = jnp.concatenate([vt0_ref[key_block], vt1_ref[key_block]], 1)
        scores = [contract(keys, parts[head], (1, 1)) * scaling for head in range(heads)]
        if same is not None:
            scores = [jnp.where(same, each, MASKED) for each in scores]
        before = top[...]
        highest = jnp.maximum(before, jnp.concatenate([jnp.max(each, 0, keepdims=True) for each in scores], 0))
        fade = jnp.exp2(before - highest)
        raised = [jnp.exp2(each - highest[head : head + 1]) for head, each in enumerate(scores)]
        if same is not None:
            raised = [jnp.where(same, each, 0.0) for each in raised]
        top[...] = highest
        total[...] = total[...] * fade + jnp.concatenate([jnp.sum(each, 0, keepdims=True) for each in raised], 0)
        products = [
            jnp.dot(values[head * DH : (head + 1) * DH], each.astype(bf16), preferred_element_type=f32)
            for head, each in enumerate(raised)
        ]
        fades = [jnp.broadcast_to(fade[head : head + 1], (DH, fade.shape[1])) for head in range(heads)]
        sums[...] = sums[...] * jnp.concatenate(fades, 0) + jnp.concatenate(products, 0)

    for index in range(count):
        for head in range(heads):
            parts[head] = head_lanes(q_ref[first + index], head)
        top[...] = jnp.full_like(top, MASKED)
        total[...] = jnp.zeros_like(total)
        sums[...] = jnp.zeros_like(sums)
        visit_blocks(info_ref, first + index, columns, share, own, visit)
        for head in range(heads):
            rows = pl.ds(head * DH, DH)
            line = pl.ds(head, 1)
            outs[index][rows, :] = (sums[rows, :] / total[line, :]).astype(bf16)
            lses[index][line, :] = top[line, :] + jnp.log2(total[line, :])


def attend_forward(first, count, info, q, kv, kv_twin, turned, turned_twin, share):
    columns, own, padded = q.shape
    width = turned.shape[1]
    heads = width // DH
    keys = pl.BlockSpec((columns, own, padded), lambda i, s: (0, 0, 0))
    values = pl.BlockSpec((columns, width, own), lambda i, s: (1, 0, 0))
    flat = lambda rows: pl.BlockSpec((rows, own), lambda i, s: (0, 0))
    outs = pl.pallas_call(
        lambda *refs: forward_kernel(first, share, *refs),
        grid_spec=pltpu.PrefetchScalarGridSpec(
            num_scalar_prefetch=1,
            grid=(1,),
            in_specs=[keys, keys, keys, values, values],
            out_specs=[flat(width)] * count + [flat(heads)] * count,
            scratch_shapes=[
                pltpu.VMEM((heads, own, padded), bf16),
                pltpu.VMEM((heads, own), f32),
                pltpu.VMEM((heads, own), f32),
                pltpu.VMEM((width, own), f32),
            ],
        ),
        out_shape=[jax.ShapeDtypeStruct((width, own), bf16)] * count + [jax.ShapeDtypeStruct((heads, own), f32)] * count,
        compiler_params=pltpu.CompilerParams(vmem_limit_bytes=60 << 20),
        cost_estimate=cost(0.001),
        name="attend_forward",
    )(info, q, kv, kv_twin, turned, turned_twin)
    return outs[:count], outs[count:]


def backward_kernel(columns, share, info_ref, q_ref, kv0_ref, kv1_ref, kt0_ref, kt1_ref, *refs):
    grads, outs, lses, refs = refs[0], refs[1 : columns + 1], refs[columns + 1 : 2 * columns + 1], refs[2 * columns + 1 :]
    dq_ref, near_ref, *fars, part_q, part_g, delta, lse, sum_q, sum_k, sum_v = refs
    own, width = q_ref.shape[1], kt0_ref.shape[1]
    heads = width // DH
    scaling = DH ** (-0.5)
    sum_k[...] = jnp.zeros_like(sum_k)
    sum_v[...] = jnp.zeros_like(sum_v)
    for block in range(columns):
        lse[block] = lses[block][...]
        column = info_ref[2] - block
        grad = grads[jnp.where(column < 0, column + columns, column)]
        spare = jnp.zeros((part_g.shape[1] - width, own), bf16)
        product = grad.astype(f32) * outs[block][...].astype(f32)
        for head in range(heads):
            part_q[block, pl.ds(head * own, own), :] = head_lanes(q_ref[block], head)
            part_g[block, :, pl.ds(head * own, own)] = jnp.concatenate([head_rows(grad, head), spare], 0)
            delta[block, pl.ds(head, 1), :] = jnp.sum(product[head * DH : (head + 1) * DH], 0, keepdims=True)

    def query_step(block, carry):
        sum_q[...] = jnp.zeros_like(sum_q)

        def visit(key_block, same):
            keys = jnp.concatenate([kv0_ref[key_block], kv1_ref[key_block]], 0)
            turned = jnp.concatenate([kt0_ref[key_block], kt1_ref[key_block]], 1)
            values = jnp.concatenate([kv0_ref[columns + key_block], kv1_ref[columns + key_block]], 0)
            all_probs, all_grads = [], []
            for head in range(heads):
                span = pl.ds(head * own, own)
                scores = contract(keys, part_q[block, span, :], (1, 1)) * (scaling * LOG2E)
                probs = jnp.exp2(scores - lse[block, pl.ds(head, 1), :])
                if same is not None:
                    probs = jnp.where(same, probs, 0.0)
                slopes = jnp.dot(values, part_g[block, :, span], preferred_element_type=f32)
                grads = (probs * (slopes - delta[block, pl.ds(head, 1), :])).astype(bf16)
                all_probs.append(probs.astype(bf16))
                all_grads.append(grads)
            for head in range(heads):
                rows = pl.ds(head * DH, DH)
                part = turned[head * DH : (head + 1) * DH]
                sum_q[rows, :] += jnp.dot(part, all_grads[head], preferred_element_type=f32)
            sum_v[key_block] += contract(jnp.concatenate(all_probs, 1), part_g[block], (1, 1))
            sum_k[key_block] += jnp.dot(jnp.concatenate(all_grads, 1), part_q[block], preferred_element_type=f32)

        visit_blocks(info_ref, block, columns, share, own, visit)
        dq_ref[block] = sum_q[...].T * scaling
        return carry

    lax.fori_loop(0, columns, query_step, 0)
    for block in range(columns):
        for place, sums, far_ref in ((block, sum_k, fars[0]), (columns + block, sum_v, fars[1])):
            near_ref[place] = sums[block, :own].astype(bf16)
            far_ref[block] = sums[block, own:].astype(bf16)


def attend_backward(info, q, kv, kv_twin, turned, turned_twin, grads, outs, lses, share):
    columns, own, padded = q.shape
    width = turned.shape[1]
    heads = width // DH
    vmem = pl.BlockSpec(memory_space=pltpu.VMEM)
    operands = [q, kv, kv_twin, turned, turned_twin, grads, *outs, *lses]
    return pl.pallas_call(
        lambda *refs: backward_kernel(columns, share, *refs),
        in_specs=[pl.BlockSpec(memory_space=pltpu.SMEM)] + [vmem] * len(operands),
        out_specs=[vmem] * 4,
        out_shape=[jax.ShapeDtypeStruct((columns, own, width), f32)]
        + [jax.ShapeDtypeStruct((many, own, padded), bf16) for many in (2 * columns, columns, columns)],
        scratch_shapes=[
            pltpu.VMEM((columns, heads * own, padded), bf16),
            pltpu.VMEM((columns, padded, heads * own), bf16),
            pltpu.VMEM((columns, heads, own), f32),
            pltpu.VMEM((columns, heads, own), f32),
            pltpu.VMEM((width, own), f32),
            pltpu.VMEM((columns, share, padded), f32),
            pltpu.VMEM((columns, share, padded), f32),
        ],
        compiler_params=pltpu.CompilerParams(vmem_limit_bytes=48 << 20),
        cost_estimate=cost(0.001),
        name="attend_backward",
    )(info, *operands)


def unproject_kernel(info_ref, dq_ref, near_k_ref, far_k_ref, near_v_ref, far_v_ref, w_ref, cos_ref, sin_ref, part_ref, low_ref):
    width = dq_ref.shape[2]
    lanes = 2 * width
    even = lax.broadcasted_iota(jnp.int32, (dq_ref.shape[1], lanes), 1) % 2 == 0
    dk = (near_k_ref[0, :, :width].astype(f32) + far_k_ref[0, :, :width].astype(f32)) * DH ** (-0.5)
    dv = near_v_ref[0, :, :width].astype(f32) + far_v_ref[0, :, :width].astype(f32)
    both = jnp.concatenate([dq_ref[0], dk], 1)
    swapped = jnp.where(even, pltpu.roll(both, lanes - 1, 1), pltpu.roll(both, 1, 1))
    both = both * widen(cos_ref[0], lanes) - swapped * widen(sin_ref[0], lanes)
    low = jnp.concatenate([both, dv], 1).astype(bf16)
    low_ref[0] = low
    part_ref[0] = contract(low, w_ref[...], (1, 1)).astype(bf16)


def unproject(info, dq, near, far_k, far_v, weight, cosine, sine):
    columns, own, width = dq.shape
    feature = weight.shape[0]
    block = lambda a, first: pl.BlockSpec((1,) + a.shape[1:], lambda i, s: (first + i, 0, 0))
    whole = lambda a: pl.BlockSpec(a.shape, lambda i, s: (0, 0))
    place = lambda i, s: (jnp.where(s[2] >= i, s[2] - i, s[2] - i + columns), 0, 0)
    low = jax.ShapeDtypeStruct((columns, own, weight.shape[1]), bf16)
    return pl.pallas_call(
        unproject_kernel,
        grid_spec=pltpu.PrefetchScalarGridSpec(
            num_scalar_prefetch=1,
            grid=(columns,),
            in_specs=[block(dq, 0), block(near, 0), block(far_k, 0), block(near, columns), block(far_v, 0), whole(weight)]
            + [block(cosine, 0), block(sine, 0)],
            out_specs=[pl.BlockSpec((1, own, feature), place), block(low, 0)],
        ),
        out_shape=[jax.ShapeDtypeStruct((columns, own, feature), bf16), low],
        compiler_params=pltpu.CompilerParams(vmem_limit_bytes=40 << 20),
        cost_estimate=cost(0.001),
        name="unproject",
    )(info, dq, near, far_k, near, far_v, weight, cosine, sine)


def project_grad_kernel(low_ref, *refs):
    x_refs, (grad_ref,) = refs[:-1], refs[-1:]
    total = None
    for block, x_ref in enumerate(x_refs):
        piece = contract(x_ref[...], low_ref[block], (0, 0))
        total = piece if total is None else total + piece
    grad_ref[...] = total.astype(bf16)


def project_grad(low, blocks):
    return pl.pallas_call(
        project_grad_kernel,
        out_shape=jax.ShapeDtypeStruct((blocks[0].shape[1], low.shape[2]), bf16),
        compiler_params=pltpu.CompilerParams(vmem_limit_bytes=40 << 20),
        cost_estimate=cost(0.001),
        name="project_grad",
    )(low, *blocks)


def mean_lanes(values):
    return jnp.sum(values, 1, keepdims=True) * (1.0 / values.shape[1])


def norm_forward(values, gain, shift):
    centred = values - mean_lanes(values)
    inverse = lax.rsqrt(mean_lanes(centred * centred) + EPSILON)
    normed = centred * inverse
    return normed * gain + shift, normed, inverse


def norm_backward(grad, normed, inverse, gain):
    scaled = grad * gain
    return inverse * (scaled - mean_lanes(scaled) - normed * mean_lanes(scaled * normed))


def unit(size):
    rows = lax.broadcasted_iota(jnp.int32, (size, size), 0)
    return (rows == lax.broadcasted_iota(jnp.int32, (size, size), 1)).astype(bf16)


def feed_kernel(info_ref, x_ref, cot_ref, w_ref, *refs):
    parts, _, columns, slab, _ = w_ref.shape
    att_refs, refs = refs[:columns], refs[columns:]
    result_ref, grad_att_ref, grad_one_ref, hidden_ref, act_out, gin_out, gtwo_ref, gone_ref, sums_ref, sent_ref, *refs = refs
    w, slopes, outer, act_ref, gin_ref, stage, sems, ends = refs
    rows, columns, quarter, _ = w.shape
    act_copy = pltpu.make_async_copy(act_ref, act_out, ends.at[0])
    gin_copy = pltpu.make_async_copy(gin_ref, gin_out, ends.at[1])

    def turned(step):
        column = info_ref[2] + step
        return jnp.where(column >= columns, column - columns, column)

    hidden_cols = act_ref.shape[2]
    both = 2 * hidden_cols
    spans = ((0, hidden_cols), (hidden_cols, hidden_cols), (both, w.shape[3] - both))

    def copies(kind):
        lanes = pl.ds(*spans[kind])
        for part in range(parts):
            target = w.at[:, :, pl.ds(part * slab, slab), lanes]
            yield pltpu.make_async_copy(w_ref.at[part, :, :, :, lanes], target, sems.at[kind, part])

    def wait(kind):
        for each in copies(kind):
            each.wait()

    for kind in (2, 0, 1):
        for each in copies(kind):
            each.start()

    def block(kind, column):
        lanes = pl.ds(*spans[kind])
        return jnp.concatenate([w[row, column, :, lanes] for row in range(rows)], 0)

    wait(2)
    mix = pl.ds(both, quarter)
    attended = jnp.concatenate([ref[...] for ref in att_refs], 0)
    branch = []
    for row in range(rows):
        weight = jnp.concatenate([w[row, turned(step), :, mix] for step in range(columns)], 0)
        branch.append(contract(attended, weight, (0, 0)))
    branch = jnp.concatenate(branch, 1)
    eye = unit(quarter)
    small = [contract(w[row, 0, :, pl.ds(both + quarter, 12)], eye, (0, 0)) for row in range(rows)]
    small = jnp.concatenate(small, 1)
    vectors = small[0:4] + (small[4:8] + small[8:12])
    gain_one, shift_one, gain_two, shift_two = (vectors[i : i + 1] for i in range(4))

    hidden, normed_one, inverse_one = norm_forward(x_ref[...].astype(f32) + branch, gain_one, shift_one)
    low = hidden.astype(bf16)
    hidden_ref[...] = low.T
    outer[...] = jnp.zeros_like(outer)

    wait(0)

    def forward(column, carry):
        inner = jnp.dot(low, block(0, column), preferred_element_type=f32)
        cumulative = 0.5 * (1.0 + lax.erf(inner * (0.5**0.5)))
        slopes[column] = cumulative + inner * (jnp.exp(-0.5 * inner * inner) * 0.3989422804014327)
        act_ref[column] = (inner * cumulative).astype(bf16)
        return carry

    lax.fori_loop(0, columns, forward, 0)
    act_copy.start()
    wait(1)

    def combine(column, carry):
        outer[...] += contract(act_ref[column], block(1, column), (1, 1))
        return carry

    lax.fori_loop(0, columns, combine, 0)
    result, normed_two, inverse_two = norm_forward(hidden + outer[...], gain_two, shift_two)
    result_ref[...] = result.astype(bf16)
    cot = cot_ref[...].astype(f32)
    grad_two = norm_backward(cot, normed_two, inverse_two, gain_two)
    grad_two_low = grad_two.astype(bf16)
    gtwo_ref[...] = grad_two_low.T
    outer[...] = grad_two

    def backward(column, carry):
        grad = jnp.dot(grad_two_low, block(1, column), preferred_element_type=f32)
        gin_ref[column] = (grad * slopes[column]).astype(bf16)
        outer[...] += contract(gin_ref[column], block(0, column), (1, 1))
        return carry

    lax.fori_loop(0, columns, backward, 0)
    gin_copy.start()
    grad_hidden = outer[...]
    grad_one = norm_backward(grad_hidden, normed_one, inverse_one, gain_one)
    grad_one_ref[...] = grad_one
    grad_one_low = grad_one.astype(bf16)
    for step in range(columns):
        weight = jnp.concatenate([w[row, turned(step), :, mix] for row in range(rows)], 1)
        grad_att_ref[turned(step)] = contract(weight, grad_one_low, (1, 1)).astype(bf16)
    sums = [jnp.sum(a, 0, keepdims=True) for a in (grad_hidden * normed_one, grad_hidden, cot * normed_two, cot)]
    sums = jnp.concatenate(sums, 0)
    for row in range(rows):
        mine = slice(row * quarter, (row + 1) * quarter)
        gone_ref[row] = grad_one_low[:, mine]
        sums_ref[row] = sums[:, mine].astype(bf16)

    def leave(column):
        slot = column % 2
        return pltpu.make_async_copy(stage.at[slot], sent_ref.at[:, :, column], ends.at[2 + slot])

    def send(column, carry):
        @pl.when(column > 1)
        def _():
            leave(column - 2).wait()

        attended = attended_block(info_ref, att_refs, column)
        operands = attended, act_ref[column], gin_ref[column], hidden_ref, gtwo_ref, gone_ref, sums_ref
        weigh_block(1 - info_ref[1], info_ref, *operands, stage.at[column % 2])
        leave(column).start()
        return carry

    lax.fori_loop(0, columns, send, 0)
    for column in (columns - 2, columns - 1):
        leave(column).wait()
    act_copy.wait()
    gin_copy.wait()


def feed(info, attended, tokens, cot, weights, slabs):
    own, feature = tokens.shape
    parts, rows, columns, slab, lanes = weights.shape
    quarter = parts * slab
    hidden_cols = feature
    vmem, smem = pl.BlockSpec(memory_space=pltpu.VMEM), pl.BlockSpec(memory_space=pltpu.SMEM)
    hbm = pl.BlockSpec(memory_space=pltpu.HBM)
    wide = jax.ShapeDtypeStruct((columns, own, hidden_cols), bf16)
    flat = lambda kind: jax.ShapeDtypeStruct((own, feature), kind)
    tall = jax.ShapeDtypeStruct((feature, own), bf16)
    return pl.pallas_call(
        feed_kernel,
        in_specs=[smem, vmem, vmem, pl.BlockSpec(memory_space=pltpu.HBM)] + [vmem] * columns,
        out_specs=[vmem] * 4 + [hbm] * 2 + [vmem] * 3 + [hbm],
        out_shape=[
            flat(bf16), jax.ShapeDtypeStruct((columns, quarter, own), bf16), flat(f32), tall, wide, wide, tall,
            jax.ShapeDtypeStruct((rows, own, quarter), bf16), jax.ShapeDtypeStruct((rows, 4, quarter), bf16),
            jax.ShapeDtypeStruct((2, slabs, columns, quarter // slabs, lanes), bf16),
        ],
        scratch_shapes=[
            pltpu.VMEM((rows, columns, quarter, lanes), bf16),
            pltpu.VMEM((columns, own, hidden_cols), f32),
            pltpu.VMEM((own, feature), f32),
            pltpu.VMEM(wide.shape, bf16),
            pltpu.VMEM(wide.shape, bf16),
            pltpu.VMEM((2, 2, slabs, quarter // slabs, lanes), bf16),
            pltpu.SemaphoreType.DMA((3, parts)),
            pltpu.SemaphoreType.DMA((4,)),
        ],
        compiler_params=pltpu.CompilerParams(vmem_limit_bytes=52 << 20),
        cost_estimate=cost(0.001),
        name="feed",
    )(info, tokens, cot, weights, *attended)


def weigh_block(core, info_ref, attended, act, gin, hidden_ref, gtwo_ref, gone_ref, sums_ref, out):
    _, slabs, slab, lanes = out.shape
    quarter = slabs * slab
    hidden_cols = act.shape[1]
    eye = unit(quarter)
    away = lambda index, mine: jnp.where(index == mine, 0, 1)
    rows = [2 * pair + core for pair in range(2)]
    spans = [pl.ds(pl.multiple_of(row * quarter, quarter), quarter) for row in rows]
    both = lambda ref: jnp.concatenate([ref[span, :] for span in spans], 0)
    inner = jnp.dot(both(hidden_ref), gin, preferred_element_type=f32).astype(bf16)
    outer = jnp.dot(both(gtwo_ref), act, preferred_element_type=f32).astype(bf16)
    for pair, row in enumerate(rows):
        mixed = jnp.dot(attended, gone_ref[row], preferred_element_type=f32).astype(bf16)
        vector = contract(eye, sums_ref[row], (1, 1)).astype(bf16)
        rest = jnp.zeros((quarter, lanes - 2 * hidden_cols - quarter - 4), bf16)
        tail = jnp.concatenate([mixed, vector, rest], 1)
        far = away(pair, info_ref[3])
        for part in range(slabs):
            place = away(part, info_ref[4]) if slabs > 1 else 0
            low = pair * quarter + part * slab
            out[far, place, :, 0:hidden_cols] = inner[low : low + slab]
            out[far, place, :, hidden_cols : 2 * hidden_cols] = outer[low : low + slab]
            out[far, place, :, 2 * hidden_cols :] = tail[part * slab : (part + 1) * slab]


def attended_block(info_ref, att_refs, column):
    step = column - info_ref[2]
    step = jnp.where(step < 0, step + len(att_refs), step)
    attended = att_refs[0][...]
    for index in range(1, len(att_refs)):
        attended = jnp.where(step == index, att_refs[index][...], attended)
    return attended


def weigh_kernel(info_ref, hidden_ref, act_ref, gin_ref, gtwo_ref, gone_ref, sums_ref, *refs):
    att_refs, out_ref = refs[:-1], refs[-1]
    attended = attended_block(info_ref, att_refs, pl.program_id(0))
    operands = attended, act_ref[0], gin_ref[0], hidden_ref, gtwo_ref, gone_ref, sums_ref
    weigh_block(info_ref[1], info_ref, *operands, out_ref.at[:, :, 0])


def weigh(info, attended, hidden, act, gin, gtwo, gone, sums, lanes, slabs):
    columns = act.shape[0]
    quarter = attended[0].shape[0]
    whole = lambda a: pl.BlockSpec(a.shape, lambda i, s: (0,) * a.ndim)
    piece = pl.BlockSpec((1,) + act.shape[1:], lambda i, s: (i, 0, 0))
    slab = quarter // slabs
    return pl.pallas_call(
        weigh_kernel,
        grid_spec=pltpu.PrefetchScalarGridSpec(
            num_scalar_prefetch=1,
            grid=(columns,),
            in_specs=[whole(hidden), piece, piece, whole(gtwo), whole(gone), whole(sums)] + [whole(a) for a in attended],
            out_specs=pl.BlockSpec((2, slabs, 1, slab, lanes), lambda i, s: (0, 0, i, 0, 0)),
        ),
        out_shape=jax.ShapeDtypeStruct((2, slabs, columns, slab, lanes), bf16),
        compiler_params=pltpu.CompilerParams(vmem_limit_bytes=52 << 20),
        cost_estimate=cost(0.001),
        name="weigh",
    )(info, hidden, act, gin, gtwo, gone, sums, *attended)


def parcel_kernel(info_ref, inner_ref, outer_ref, output_ref, *refs):
    small_refs, out_ref = refs[:-1], refs[-1]
    columns = inner_ref.shape[1]
    quarter = output_ref.shape[1]
    slab = out_ref.shape[0]
    offset = info_ref[0] * slab if slab < quarter else 0
    rows = pl.ds(pl.multiple_of(offset, slab), slab)
    values = jnp.concatenate([ref[...] for ref in small_refs], 0)
    high = values.astype(bf16)
    rest = values - high.astype(f32)
    middle = rest.astype(bf16)
    last = (rest - middle.astype(f32)).astype(bf16)
    pick = lax.broadcasted_iota(jnp.int32, (slab, quarter), 0) + offset
    pick = (pick == lax.broadcasted_iota(jnp.int32, (slab, quarter), 1)).astype(bf16)
    small = jnp.concatenate([contract(pick, part, (1, 1)) for part in (high, middle, last)], 1).astype(bf16)
    fill = jnp.zeros((slab, out_ref.shape[1] - 2 * columns - quarter - 12), bf16)
    out_ref[:, 0:columns] = inner_ref[rows, :]
    out_ref[:, columns : 2 * columns] = outer_ref[rows, :]
    out_ref[:, 2 * columns :] = jnp.concatenate([output_ref[rows, :], small, fill], 1)


def parcel(part, inner, outer, output, vectors, lanes, slabs):
    vmem, smem = pl.BlockSpec(memory_space=pltpu.VMEM), pl.BlockSpec(memory_space=pltpu.SMEM)
    return pl.pallas_call(
        parcel_kernel,
        in_specs=[smem] + [vmem] * 7,
        out_shape=jax.ShapeDtypeStruct((inner.shape[0] // slabs, lanes), bf16),
        cost_estimate=cost(0.001),
        name="parcel",
    )(part, inner, outer, output, *(v.reshape(1, -1) for v in vectors))


def keep(values, index, axis=0):
    first, second = lax.index_in_dim(values, 0, axis, False), lax.index_in_dim(values, 1, axis, False)
    chosen = index == 0
    return jnp.where(chosen, first, second), jnp.where(chosen, second, first)


def tie(*values):
    return lax.optimization_barrier(values)


def shift(values, step):
    columns = lax.axis_size("col")
    if step % columns == 0:
        return values
    return lax.ppermute(values, "col", [(i, (i + step) % columns) for i in range(columns)])


def add_kernel(count, sums, *refs):
    results, (*sources, buffer, held, sems, ends) = refs[-count - 4 : -4], refs[: -count - 4] + refs[-4:]
    rows, first, number = [], 0, 0
    for index, start, parts in sums:
        row = []
        for which, lead, low, high in parts:
            source = sources[which].at[lead + (pl.ds(low, high - low),)]
            copy = pltpu.make_async_copy(source, buffer.at[pl.ds(first, high - low)], sems.at[number])
            copy.start()
            row.append((first, high - low, copy))
            first, number = first + high - low, number + 1
        rows.append(row)
    copies, first = [], 0
    for place, ((index, start, _), row) in enumerate(zip(sums, rows)):
        size = row[0][1]
        for *_, copy in row:
            copy.wait()
        total = sum(buffer[at : at + size].astype(f32) for at, *_ in row)
        held[first : first + size] = total.astype(bf16)
        target = results[index].at[pl.ds(start, size)]
        copies.append(pltpu.make_async_copy(held.at[pl.ds(first, size)], target, ends.at[place]))
        copies[-1].start()
        first += size
    for copy in copies:
        copy.wait()


def add_blocks(arrays, lengths, sums):
    hbm = pl.BlockSpec(memory_space=pltpu.HBM)
    tail = arrays[0].shape[-2:]
    parts = [part for *_, each in sums for part in each]
    return pl.pallas_call(
        lambda *refs: add_kernel(len(lengths), sums, *refs),
        in_specs=[hbm] * len(arrays),
        out_specs=[hbm] * len(lengths),
        out_shape=[jax.ShapeDtypeStruct((length,) + tail, bf16) for length in lengths],
        scratch_shapes=[
            pltpu.VMEM((sum(high - low for *_, low, high in parts),) + tail, bf16),
            pltpu.VMEM((sum(lengths),) + tail, bf16),
            pltpu.SemaphoreType.DMA((len(parts),)),
            pltpu.SemaphoreType.DMA((len(sums),)),
        ],
        compiler_params=pltpu.CompilerParams(vmem_limit_bytes=60 << 20),
        cost_estimate=cost(0.001),
        name="add_blocks",
    )(*arrays)


def open_kernel(hidden_cols, part_ref, mine_ref, other_ref, *outs):
    *outs, sums_ref, query_ref, key_ref, value_ref = outs
    slab, quarter = mine_ref.shape[0], outs[2].shape[1]
    spans = (0, hidden_cols), (hidden_cols, hidden_cols), (2 * hidden_cols, quarter)
    lanes = mine_ref.shape[1] - 6 * quarter

    def write(first, second):
        for (start, size), out in zip(spans, outs):
            out[0:slab, :] = first[:, start : start + size].astype(f32)
            out[slab : 2 * slab, :] = second[:, start : start + size].astype(f32)
        start = 2 * hidden_cols + quarter
        last = jnp.concatenate([first[:, start:lanes], second[:, start:lanes]], 0)
        sums_ref[...] = contract(last[:, 0:4], unit(2 * slab), (0, 0))

    @pl.when(part_ref[0] == 0)
    def _():
        write(mine_ref[...], other_ref[...])

    @pl.when(part_ref[0] != 0)
    def _():
        write(other_ref[...], mine_ref[...])

    total = mine_ref[:, lanes:].astype(f32) + other_ref[:, lanes:].astype(f32)
    for index, ref in enumerate((query_ref, key_ref, value_ref)):
        for half in range(2):
            start = (3 * half + index) * quarter
            ref[half * slab : (half + 1) * slab, :] = total[:, start : start + quarter]


def open_shards(part, mine, other, hidden_cols, quarter):
    vmem, smem = pl.BlockSpec(memory_space=pltpu.VMEM), pl.BlockSpec(memory_space=pltpu.SMEM)
    rows = hidden_cols, hidden_cols, quarter
    shape = lambda *dims: jax.ShapeDtypeStruct(dims, f32)
    return pl.pallas_call(
        lambda *refs: open_kernel(hidden_cols, *refs),
        in_specs=[smem, vmem, vmem],
        out_shape=[shape(quarter, a) for a in rows] + [shape(4, quarter)] + [shape(quarter, quarter)] * 3,
        compiler_params=pltpu.CompilerParams(vmem_limit_bytes=16 << 20),
        cost_estimate=cost(0.001),
        name="open_shards",
    )(part, mine, other)


def sum_shards(kept, sent, mark):
    columns = kept.shape[2]
    middle = columns // 2
    pair = kept, swap(sent, "yb")
    both = lambda lead, low, high: [(0, lead, low, high), (1, lead, low, high)]
    to_dp = [(0, 0, both((1, 1), 0, middle)), (0, middle, both((0, 1), 0, middle))]
    to_ya = [(1, 0, both((1, 1), middle, columns)), (1, middle, both((1, 0), middle, columns))]
    to_dp, to_ya = add_blocks(pair, (columns, columns), to_dp + to_ya)
    mark, to_dp, to_ya = tie(mark, to_dp, to_ya)
    by_dp, by_ya = swap(to_dp, "dp"), swap(to_ya, "ya")

    def sides(mark):
        dp, ya, mark = tie(by_dp, by_ya, mark)
        rest_ya = (0, 0, both((1, 0), 0, middle) + [(2, (), 0, middle)])
        rest_dp = (1, 0, both((0, 1), middle, columns) + [(3, (), 0, middle)])
        rest_ya, rest_dp = add_blocks(pair + (dp, ya), (middle, columns - middle), [rest_ya, rest_dp])
        mark, rest_ya, rest_dp = tie(mark, rest_ya, rest_dp)
        rest_ya, rest_dp = swap(rest_ya, "ya"), swap(rest_dp, "dp")

        def finish(mark):
            low_ya, high_dp, mark = tie(rest_ya, rest_dp, mark)
            low = both((0, 0), 0, middle) + [(2, (), middle, columns), (4, (), 0, middle)]
            high = both((0, 0), middle, columns) + [(3, (), middle, columns), (5, (), 0, columns - middle)]
            (own,) = add_blocks(pair + (dp, ya, low_ya, high_dp), (columns,), [(0, 0, low), (0, middle, high)])
            own, mark = tie(own, mark)
            mine = lax.psum_scatter(own, "col", scatter_dimension=0, tiled=False)
            return mine, mark

        return mark, finish

    return mark, sides


def body(
    inputs, cotangent, lengths, source, query_weight, key_weight, value_weight, output_weight, inner_weight, outer_weight,
    first_gain, first_shift, second_gain, second_shift,
):
    micro, quarter, share = inputs.shape
    dp_count, columns = lax.axis_size("dp"), lax.axis_size("col")
    pack, own = share * columns, share // 2
    feature, count = 4 * quarter, share * micro
    width, hidden_cols = query_weight.shape[1], inner_weight.shape[1]
    lanes = -(-(2 * hidden_cols + quarter + 12) // 128) * 128
    me, m, half, z = (lax.axis_index(a) for a in ("dp", "ya", "yb", "col"))

    boundary = jnp.where(m == 0, lengths[0, 0], lengths[0, 1])
    info = jnp.stack([boundary, half, z, m, me]).astype(jnp.int32)
    slabs = 2 if dp_count == 2 else 1

    vectors = (first_gain, first_shift, second_gain, second_shift)
    anchors = spread_dp(source)
    packed = parcel(jnp.reshape(me, (1,)).astype(jnp.int32), inner_weight, outer_weight, output_weight, vectors, lanes, slabs)
    axes = ("dp",) + SHARDS if slabs == 2 else SHARDS
    everywhere = lax.all_gather(packed, axes, axis=0).reshape(slabs, 4, columns, quarter // slabs, lanes)
    anchor = source.reshape(count)
    place = anchor // (dp_count * pack) * share + anchor % share
    holder = anchor % (dp_count * pack) // pack
    wide_in = spread_dp(inputs)

    steps = jnp.arange(columns, dtype=jnp.int32)
    spots = ((z - steps) % columns * share + half * own)[:, None] + jnp.arange(own, dtype=jnp.int32)[None, :]
    frequency = 10000.0 ** (-2.0 * jnp.arange(DH // 2, dtype=f32) / DH)
    angles = (spots - jnp.where(spots >= boundary, boundary, 0)).astype(f32)[..., None] * jnp.tile(jnp.repeat(frequency, 2), 2)
    signs = jnp.where(jnp.arange(2 * DH) % 2 == 0, -1.0, 1.0)
    cosine, sine = jnp.cos(angles), jnp.sin(angles) * signs
    wide_in, cosine, sine = tie(wide_in, cosine, sine)

    if dp_count == 2:
        pick = (holder * count + place)[:, None] == jnp.arange(dp_count * count, dtype=jnp.int32)[None, :]
        pick = pick.astype(bf16).reshape(count, dp_count, micro, share)
        deal = lambda wide: jnp.einsum("tsmj,smfj->tf", pick, wide, preferred_element_type=f32).astype(bf16)
    else:
        deal = lambda wide: wide.transpose(0, 1, 3, 2).reshape(-1, quarter)[holder * count + place]

    def to_tokens(dealt):
        return lax.all_to_all(dealt.reshape(4, own, quarter), ROWS, split_axis=0, concat_axis=0, tiled=True)

    dealt = deal(wide_in)
    cotangent, dealt = tie(cotangent, dealt)
    tokens = to_tokens(dealt).transpose(1, 0, 2).reshape(own, feature)
    wide_cot, tokens = tie(spread_dp(cotangent), tokens)
    blocks = [shift(tokens, step) for step in range(columns)]
    cot = to_tokens(deal(wide_cot)).transpose(1, 0, 2).reshape(own, feature)
    qkv_weight = jnp.concatenate([query_weight, key_weight, value_weight], 1)
    qkv_weight = gather_rows(qkv_weight).reshape(feature, -1)

    blocks[-1], cot, anchors = tie(blocks[-1], cot, anchors)
    q, kv, turned = project(blocks, qkv_weight, cosine, sine)
    kv_twin, turned_twin = swap(kv, "yb"), swap(turned, "yb")
    mixed, lses = attend_forward(1, columns - 1, info, q, kv, kv_twin, turned, turned_twin, share)
    q, mixed = tie(q, mixed)
    last = attend_forward(0, 1, info, q, kv, kv_twin, turned, turned_twin, share)
    mixed, lses = last[0] + mixed, last[1] + lses
    attended = [shift(mixed[step], -step) for step in range(columns)]

    result, grad_att, grad_one, *pieces, sent = feed(info, attended, tokens, cot, everywhere, slabs)
    grad_att = lax.all_to_all(grad_att, "col", split_axis=0, concat_axis=0, tiled=True)
    def to_loader(*rows):
        cut = jnp.concatenate([a.astype(bf16).reshape(own, 4, quarter).transpose(1, 0, 2) for a in rows], 2)
        cut = jnp.broadcast_to(cut[None], (dp_count,) + cut.shape).reshape(dp_count * 4, own, -1)
        moved = lax.all_to_all(cut, ("dp",) + ROWS, split_axis=0, concat_axis=0, tiled=True)
        return moved.reshape(-1, len(rows) * quarter)

    spot = jnp.arange(count, dtype=jnp.int32)
    wanted = spot // share * (dp_count * pack) + me * pack + z * share + spot % share
    if dp_count == 2:
        put = (anchors.reshape(-1)[:, None] == wanted[None, :]).astype(bf16)
        settle = lambda wide: contract(wide, put, (0, 0)).astype(bf16)
    else:
        order = jnp.argsort(anchors.reshape(-1))
        spots_in = jnp.searchsorted(anchors.reshape(-1)[order], wanted)
        settle = lambda wide: wide[order[spots_in]].T
    kept = weigh(info, attended, *pieces, lanes, slabs)
    if slabs == 2:
        grad_att, sides = sum_shards(kept, sent, grad_att)
    else:
        flip = lambda a, index, axis: jnp.where(index == 0, a, jnp.flip(a, axis))
        cut = flip(flip(jnp.stack([kept, sent], 1), m, 0), half, 1).reshape(4 * columns, quarter, lanes)
        summed = lax.psum_scatter(cut, SHARDS, scatter_dimension=0, tiled=False)
        summed = lax.psum(summed, "dp").astype(f32)

    dq, near, *far = attend_backward(info, q, kv, kv_twin, turned, turned_twin, grad_att, mixed, lses, share)
    partial, low = unproject(info, dq, near, *(swap(each, "yb") for each in far), qkv_weight, cosine, sine)
    if slabs == 2:
        low, finish = sides(low)
    grad_qkv = project_grad(low, blocks)
    partial = lax.all_to_all(partial, "col", split_axis=0, concat_axis=0, tiled=True)
    grad_tokens = grad_one + jnp.sum(partial.astype(f32), 0)

    def over_dp(values):
        if dp_count == 2:
            return values.astype(f32) + swap(values, "dp").astype(f32)
        return lax.psum(values, "dp").astype(f32)

    def halve(grad, axis, index, place_axis):
        kept, sent = keep(grad, index, place_axis)
        return (kept.astype(f32) + swap(sent, axis).astype(f32)).astype(bf16)

    if slabs == 2:
        summed, grad_qkv = finish(grad_qkv)
    grad_qkv = halve(grad_qkv.reshape(2, 2, quarter, 3 * width), "yb", half, 1)
    grad_qkv = halve(grad_qkv, "ya", m, 0)
    grad_tokens, grad_qkv = tie(grad_tokens, grad_qkv)
    if slabs == 1:
        grad_qkv = over_dp(grad_qkv)
        sum_qkv = [grad_qkv[:, i * width : (i + 1) * width] for i in range(3)]
        sum_inner, sum_outer = summed[:, :hidden_cols], summed[:, hidden_cols : 2 * hidden_cols]
        sum_output = summed[:, 2 * hidden_cols : 2 * hidden_cols + quarter]
        sum_vectors = summed[:, 2 * hidden_cols + quarter : 2 * hidden_cols + quarter + 4].T

    shape = lambda a: a.reshape(quarter, micro, share).transpose(1, 0, 2)
    moved = to_loader(result, grad_tokens)
    if slabs == 2:
        slab = quarter // 2
        mine = jnp.concatenate([summed, grad_qkv[:slab], grad_qkv[slab:]], 1)
        other = swap(mine, "dp")
        moved, summed = tie(moved, summed)
        part = jnp.reshape(me, (1,)).astype(jnp.int32)
        sum_inner, sum_outer, sum_output, sum_vectors, *sum_qkv = open_shards(part, mine, other, hidden_cols, quarter)
    settled = settle(moved)
    final_out, final_grad = shape(settled[:quarter]), shape(settled[quarter:])
    return (
        final_out, final_grad, *sum_qkv,
        sum_output, sum_inner, sum_outer, sum_vectors[0], sum_vectors[1], sum_vectors[2], sum_vectors[3],
    )


def solution(mesh):
    dp, row, col = (mesh.shape[a] for a in ("dp", "row", "col"))
    fine = Mesh(mesh.devices.reshape(dp, 2, row // 2, col), ("dp", "ya", "yb", "col"))
    tokens, matrix = P(None, ROWS, ("dp", "col")), P(ROWS, "col")
    weights = (matrix, matrix, matrix, P("col", ROWS), matrix, matrix, P(ROWS), P(ROWS), P(ROWS), P(ROWS))
    return jax.shard_map(
        body,
        mesh=fine,
        in_specs=(tokens, tokens, P("dp", None), P(None, ("dp", "col"))) + weights,
        out_specs=(tokens, tokens) + weights,
        check_vma=False,
    )
```
